128 devices in a mesh: row: 8 (over y, z_hi), col: 16 (over z_lo, x, core).
Axes of the slice: x: 4, y: 4, z: 4 (z_hi: 2, z_lo: 2; z = z_hi * 2 + z_lo), core: 2. Of those that a mesh axis runs over, the one named last changes fastest.
Arguments:
- features: float32 [2, 128, 1024, 128], P(None, 'row', 'col'), may hold values from -6 to 6
- cotangent: float32 [2, 128, 1024, 128], P(None, 'row', 'col'), may hold values from -6 to 6
- conv_kernel: float32 [7, 7, 128], P(None, None, ('row', 'col')), may hold values from -0.875 to 0.875
- conv_bias: float32 [128], P(('row', 'col')), may hold values from -3 to 3
- norm_gain: float32 [128], P(('row', 'col')), may hold values from 0.1 to 1.9
- norm_shift: float32 [128], P(('row', 'col')), may hold values from -2 to 2
- w_in: float32 [128, 512], P(None, ('row', 'col')), may hold values from -0.5 to 0.5
- in_bias: float32 [512], P(('row', 'col')), may hold values from -3 to 3
- w_out: float32 [512, 128], P(('row', 'col')), may hold values from -0.25 to 0.25
- out_bias: float32 [128], P(('row', 'col')), may hold values from -3 to 3
- layer_scale: float32 [128], P(('row', 'col')), may hold values from 0.5 to 1.5
Outputs:
- features_grad: float32 [2, 128, 1024, 128], P(None, 'row', 'col')
- kernel_grad: float32 [7, 7, 128], P(None, None, ('row', 'col'))
- conv_bias_grad: float32 [128], P(('row', 'col'))
- gain_grad: float32 [128], P(('row', 'col'))
- shift_grad: float32 [128], P(('row', 'col'))
- w_in_grad: float32 [128, 512], P(None, ('row', 'col'))
- in_bias_grad: float32 [512], P(('row', 'col'))
- w_out_grad: float32 [512, 128], P(('row', 'col'))
- out_bias_grad: float32 [128], P(('row', 'col'))
- scale_grad: float32 [128], P(('row', 'col'))
The draws below stay inside these ranges and needn't reach their ends.
All inputs are finite; a program needn't handle non-finite values.
Results may differ from the reference program's by a relative error of at most 0.0003.
Values sent between devices are 32-bit elements; how exact they have to be, the bound alone decides.
A program may use at most 64 MiB of HBM per device.

```python
import math
import jax
import jax.numpy as jnp
from jax import lax

C = 128
HID = 512
K = 7
BATCH = 2
IMG_H = 128
IMG_W = 1024


def block_levels(rng, dims, shards, least, largest):
    factor_of, own = 1.0, jax.random.fold_in(rng, 6)
    for dim, shards_of in shards:
        steps = jnp.exp(jax.random.uniform(jax.random.fold_in(own, dim), (shards_of,), jnp.float32, least / len(shards), largest / len(shards)))
        factor_of = factor_of * jnp.repeat(steps, dims[dim] // shards_of).reshape([-1 if axis == dim else 1 for axis in range(len(dims))])
    return factor_of


def normal_values(own_key, shape, scale, reach, split=(), dtype=jnp.bfloat16):
    level = block_levels(own_key, shape, split, -0.22, 0.18) if split else 1.0
    array = jax.random.normal(own_key, shape, jnp.float32) * scale * level
    return jnp.minimum(jnp.maximum(array, -reach), reach).astype(dtype)


def setup_inputs(seed: int = 0) -> dict:
    keys = jax.random.split(jax.random.key(seed), 12)
    features = normal_values(keys[0], (BATCH, IMG_H, IMG_W, C), 1.0, 6.0, ((1, 8), (2, 16)), jnp.float32)
    cotangent = normal_values(keys[1], (BATCH, IMG_H, IMG_W, C), 1.0, 6.0, ((1, 8), (2, 16)), jnp.float32)
    conv_kernel = normal_values(keys[2], (K, K, C), (K * K) ** -0.5, 0.875, ((2, 128),), jnp.float32)
    conv_bias = normal_values(keys[3], (C,), 0.5, 3.0, ((0, 128),), jnp.float32)
    norm_gain = jnp.clip(1.0 + 0.18 * jax.random.normal(keys[4], (C,), jnp.float32), 0.1, 1.9)
    norm_shift = normal_values(keys[5], (C,), 0.3, 2.0, ((0, 128),), jnp.float32)
    w_in = normal_values(keys[6], (C, HID), C ** -0.5, 0.5, ((1, 128),), jnp.float32)
    in_bias = normal_values(keys[7], (HID,), 0.5, 3.0, ((0, 128),), jnp.float32)
    w_out = normal_values(keys[8], (HID, C), HID ** -0.5, 0.25, ((0, 128),), jnp.float32)
    out_bias = normal_values(keys[9], (C,), 0.5, 3.0, ((0, 128),), jnp.float32)
    layer_scale = jnp.clip(0.5 + 1.0 * jax.random.uniform(keys[10], (C,), jnp.float32) ** block_levels(keys[10], (C,), ((0, 128),), -0.2, 0.2), 0.5, 1.5)
    return {"features": features, "cotangent": cotangent, "conv_kernel": conv_kernel, "conv_bias": conv_bias, "norm_gain": norm_gain, "norm_shift": norm_shift, "w_in": w_in, "in_bias": in_bias, "w_out": w_out, "out_bias": out_bias, "layer_scale": layer_scale}


norm_eps = 1e-06

def depthwise(field, kernel):
    return lax.conv_general_dilated(field, kernel[:, :, None, :], (1, 1), 'VALID', dimension_numbers=('NHWC', 'HWIO', 'NHWC'), feature_group_count=field.shape[-1], precision=lax.Precision.HIGHEST)

def mixing(conv_out, norm_gain, norm_shift, w_in, in_bias, w_out, out_bias, layer_scale):
    mean = lax.optimization_barrier(jnp.mean(conv_out, -1, keepdims=True))
    centred = conv_out - mean
    variance = lax.optimization_barrier(jnp.mean(centred * centred, -1, keepdims=True))
    normed = centred * lax.rsqrt(variance + norm_eps)
    lin = normed * norm_gain + norm_shift
    act = jnp.einsum('bhwc,ck->bhwk', lin, w_in, precision=lax.Precision.HIGHEST) + in_bias
    hidden = jax.nn.gelu(act, approximate=False)
    branch = jnp.einsum('bhwk,kc->bhwc', hidden, w_out, precision=lax.Precision.HIGHEST) + out_bias
    return branch * layer_scale

def reference(features, cotangent, conv_kernel, conv_bias, norm_gain, norm_shift, w_in, in_bias, w_out, out_bias, layer_scale):
    margin = K // 2
    padded = jnp.pad(features, ((0, 0), (margin, margin), (margin, margin), (0, 0)))
    conv_out = depthwise(padded, conv_kernel) + conv_bias
    params = (norm_gain, norm_shift, w_in, in_bias, w_out, out_bias, layer_scale)
    block = math.gcd(IMG_H, 16)
    count = IMG_H // block
    conv_blocks = jnp.moveaxis(conv_out.reshape(BATCH, count, block, IMG_W, C), 1, 0)
    cot_blocks = jnp.moveaxis(cotangent.reshape(BATCH, count, block, IMG_W, C), 1, 0)

    def step(carry, pair):
        conv_piece, cot_piece = pair
        outcome, pullback = jax.vjp(mixing, conv_piece, *params)
        grads = pullback(cot_piece)
        carry = tuple((total + part for total, part in zip(carry, grads[1:])))
        return (carry, grads[0])
    start = tuple((jnp.zeros_like(p) for p in params))
    totals, dconv_blocks = lax.scan(step, start, (conv_blocks, cot_blocks))
    d_conv = jnp.moveaxis(dconv_blocks, 0, 1).reshape(BATCH, IMG_H, IMG_W, C)
    conv_value, conv_pull = jax.vjp(depthwise, padded, conv_kernel)
    d_padded, kernel_grad = conv_pull(d_conv)
    features_grad = cotangent + d_padded[:, margin:-margin, margin:-margin]
    factor = 1.0 / math.sqrt(BATCH * IMG_H * IMG_W)
    bias_grad = lax.optimization_barrier(jnp.sum(d_conv, axis=(0, 1, 2)))
    gain_g, shift_g, win_g, inb_g, wout_g, outb_g, scale_g = totals
    return (features_grad, kernel_grad * factor, bias_grad * factor, gain_g * factor, shift_g * factor, win_g * factor, inb_g * factor, wout_g * factor, outb_g * factor, scale_g * factor)
```

```python
import functools
import math

import jax
import jax.numpy as jnp
from jax import lax
from jax.experimental import pallas as pl
from jax.experimental.pallas import tpu as pltpu
from jax.sharding import PartitionSpec as P

norm_eps = 1e-06
inverse_root_two = 0.7071067811865476
inverse_root_twopi = 0.3989422804014327
MESH = pl.DeviceIdType.MESH
f32, bf16 = jnp.float32, jnp.bfloat16

K, R = 7, 3
C, HID = 128, 512
B, H, W = 2, 16, 64
LEFT = 8
WE = W + 2 * LEFT
HE = H + 2 * R
ROWS, COLS = 8, 16
CHUNK = 4
M = CHUNK * W
TAPS, CB, GAIN, SHIFT, OB, SCALE, IB = 0, 49, 50, 51, 52, 53, 54


def split(x):
    hi = x.astype(bf16)
    return hi, (x - hi.astype(f32)).astype(bf16)


def dot(a, b):
    return jnp.dot(a, b, preferred_element_type=f32)


def lanes(x, n, axis):
    return lax.broadcasted_iota(jnp.int32, (x, n), axis)


class Place:
    def __init__(self):
        self.row, self.col = lax.axis_index("row"), lax.axis_index("col")
        self.y = self.row // 2
        self.z = lax.rem(self.row, 2) * 2 + self.col // 8
        self.g = lax.rem(self.col, 8)
        self.x, self.core = self.g // 2, lax.rem(self.g, 2)
        self.index = self.row * COLS + self.col

    def in_group(self, off):
        other = lax.rem(self.g + off, 8)
        return other, (self.row, self.col // 8 * 8 + other)

    def along_z(self, off):
        other = lax.rem(self.z + off, 4)
        return other, (self.y * 2 + other // 2, lax.rem(other, 2) * 8 + self.g)

    def along_y(self, off):
        other = lax.rem(self.y + off, 4)
        return other, (other * 2 + lax.rem(self.row, 2), self.col)

    def sibling(self):
        return (self.row, self.col + 1 - 2 * self.core)

    def neighbour(self, dr, dc):
        return (lax.rem(self.row + dr + ROWS, ROWS), lax.rem(self.col + dc + COLS, COLS))


STEPS = [(-1, 0), (1, 0), (0, -1), (0, 1), (-1, -1), (-1, 1), (1, -1), (1, 1)]


def rows_of(step, base, sent):
    if step == 0:
        return pl.ds(base, H)
    if sent:
        return pl.ds(base, R) if step < 0 else pl.ds(base + H - R, R)
    return pl.ds(R + H, R) if step < 0 else pl.ds(0, R)


def cols_of(step, base, sent):
    if step == 0:
        return pl.ds(base, W)
    if sent:
        return pl.ds(base, LEFT) if step < 0 else pl.ds(base + W - LEFT, LEFT)
    return pl.ds(LEFT + W, LEFT) if step < 0 else pl.ds(0, LEFT)


def edge_copies(place, src, row0, col0, ext, send, recv):
    copies = []
    for n, (dr, dc) in enumerate(STEPS):
        copies.append(
            pltpu.make_async_remote_copy(
                src_ref=src.at[:, rows_of(dr, row0, True), cols_of(dc, col0, True), :],
                dst_ref=ext.at[:, rows_of(dr, R, False), cols_of(dc, LEFT, False), :],
                send_sem=send.at[n],
                recv_sem=recv.at[n],
                device_id=place.neighbour(dr, dc),
                device_id_type=MESH,
            )
        )
    return copies


def clear_outside(place, ext):
    @pl.when(place.row == 0)
    def _():
        ext[:, 0:R] = jnp.zeros((B, R, WE, C), f32)

    @pl.when(place.row == ROWS - 1)
    def _():
        ext[:, R + H :] = jnp.zeros((B, R, WE, C), f32)

    @pl.when(place.col == 0)
    def _():
        ext[:, :, 0:LEFT] = jnp.zeros((B, HE, LEFT, C), f32)

    @pl.when(place.col == COLS - 1)
    def _():
        ext[:, :, LEFT + W :] = jnp.zeros((B, HE, LEFT, C), f32)


def conv_tile(ext, taps, b, wb, flip):
    acc = [None] * H
    for j in range(K):
        tap = [taps[(K - 1 - i) * K + K - 1 - j] if flip else taps[i * K + j] for i in range(K)]
        for e in range(HE):
            x = ext[b, e, LEFT - R + 8 * wb + j : LEFT - R + 8 * wb + j + 8, :]
            for i in range(K):
                p = e - i
                if 0 <= p < H:
                    term = tap[i] * x
                    acc[p] = term if acc[p] is None else acc[p] + term
    return acc


def kernel_grad_tile(ext, dcv, kacc, b, wb):
    grads = [dcv[b, R + p, LEFT + 8 * wb : LEFT + 8 * wb + 8, :] for p in range(H)]
    for j in range(K):
        acc = [kacc[i * K + j] for i in range(K)]
        for e in range(HE):
            x = ext[b, e, LEFT - R + 8 * wb + j : LEFT - R + 8 * wb + j + 8, :]
            for i in range(K):
                p = e - i
                if 0 <= p < H:
                    acc[i] = acc[i] + grads[p] * x
        for i in range(K):
            kacc[i * K + j] = acc[i]


def kernel(
    feat, cot_hbm, small_in, weight_in,
    fg_out, small_out, weight_out,
    src, cot, dcv, mid, fg, sg, wg, taps,
    win2, winlo, wintop, wintlo, wot2, wotlo, bias_eff,
    nacc, macc, inbacc, kacc, cotacc, dbacc,
    wp, wcore, wa, wry, wb_, wrz, wc, wrx, sp, sry, sb, srz, sc, srx,
    local, out_sem, fsend, frecv, dsend, drecv, agsend, agrecv, rssend, rsrecv,
):
    place = Place()
    me = place.index

    own = [
        pltpu.make_async_copy(feat, src.at[:, pl.ds(R, H), pl.ds(LEFT, W), :], local.at[0]),
        pltpu.make_async_copy(cot_hbm, cot, local.at[1]),
        pltpu.make_async_copy(small_in, sg.at[pl.ds(me, 1)], local.at[2]),
        pltpu.make_async_copy(weight_in, wg.at[:, pl.ds(me, 1)], local.at[3]),
    ]
    for copy in own:
        copy.start()

    barrier = pltpu.get_barrier_semaphore()
    partners = [place.neighbour(dr, dc) for dr, dc in STEPS]
    partners += [place.in_group(off)[1] for off in range(1, 8)]
    partners += [place.along_z(off)[1] for off in range(1, 4)]
    partners += [place.along_y(off)[1] for off in range(1, 4)]
    for partner in partners:
        pl.semaphore_signal(barrier, inc=1, device_id=partner, device_id_type=MESH)
    pl.semaphore_wait(barrier, len(partners))

    def remote(s, d, sem, partner, send, recv):
        return pltpu.make_async_remote_copy(
            src_ref=s, dst_ref=d, send_sem=send.at[sem], recv_sem=recv.at[sem],
            device_id=partner, device_id_type=MESH,
        )

    s1 = [remote(small_in, sg.at[pl.ds(me, 1)], off - 1, place.in_group(off)[1], agsend, agrecv) for off in range(1, 8)]
    w1 = [remote(weight_in, wg.at[:, pl.ds(me, 1)], 13 + off - 1, place.in_group(off)[1], agsend, agrecv) for off in range(1, 8)]
    zs, ys = pl.ds(me // 8 * 8, 8), pl.ds(me // 32 * 32, 32)
    s2 = [remote(sg.at[zs], sg.at[zs], 7 + off - 1, place.along_z(off)[1], agsend, agrecv) for off in range(1, 4)]
    w2 = [remote(wg.at[:, zs], wg.at[:, zs], 20 + off - 1, place.along_z(off)[1], agsend, agrecv) for off in range(1, 4)]
    s3 = [remote(sg.at[ys], sg.at[ys], 10 + off - 1, place.along_y(off)[1], agsend, agrecv) for off in range(1, 4)]
    w3 = [remote(wg.at[:, ys], wg.at[:, ys], 23 + off - 1, place.along_y(off)[1], agsend, agrecv) for off in range(1, 4)]
    edges = edge_copies(place, feat, 0, 0, src, fsend, frecv)

    def start(copies):
        for copy in copies:
            copy.start()

    def arrive(copies):
        for copy in copies:
            copy.wait_recv()

    start(s1)
    start(w1)
    start(edges)
    own[2].wait()
    own[3].wait()
    arrive(s1)
    start(s2)
    arrive(w1)
    start(w2)

    kacc[...] = jnp.zeros_like(kacc)
    nacc[...] = jnp.zeros_like(nacc)
    macc[...] = jnp.zeros_like(macc)
    inbacc[...] = jnp.zeros_like(inbacc)
    cotacc[...] = jnp.zeros_like(cotacc)
    dbacc[...] = jnp.zeros_like(dbacc)

    arrive(s2)
    start(s3)
    arrive(w2)
    start(w3)
    arrive(s3)

    small = sg[...].reshape(128, C)
    small_t = small.T
    for n in range(K * K):
        taps[n] = jnp.broadcast_to(small_t[TAPS + n : TAPS + n + 1, :], (8, C))
    conv_bias = jnp.broadcast_to(small_t[CB : CB + 1, :], (8, C))
    gain_col, shift_col = small[:, GAIN : GAIN + 1], small[:, SHIFT : SHIFT + 1]
    scale_col, ob_col = small[:, SCALE : SCALE + 1], small[:, OB : OB + 1]

    own[0].wait()
    own[1].wait()
    arrive(edges)
    clear_outside(place, src)

    def conv_step(b, carry):
        for wb in range(W // 8):
            acc = conv_tile(src, taps, b, wb, False)
            for p in range(H):
                mid[b, p, 8 * wb : 8 * wb + 8, :] = acc[p] + conv_bias
        return carry

    lax.fori_loop(0, B, conv_step, 0)

    arrive(w3)
    win_t = wg[0].reshape(HID, C)
    wo_t = wg[1].reshape(HID, C).T
    win = win_t.T
    hi, lo = split(win * gain_col)
    win2[0:C, :] = hi
    win2[C:, :] = hi
    winlo[...] = lo
    gain_row = small_t[GAIN : GAIN + 1, :]
    hi, lo = split(win_t * gain_row)
    wintop[:, 0:C] = hi
    wintop[:, C:] = lo
    hi, lo = split(wo_t * scale_col)
    wot2[0:C, :] = hi
    wot2[C:, :] = hi
    wotlo[...] = lo
    unit, chan = lanes(C, HID, 1), lanes(C, HID, 0)
    bias_terms = win * shift_col
    for k in range(4):
        bias_terms = bias_terms + jnp.where(unit == 4 * chan + k, small[:, IB + k : IB + k + 1], 0.0)
    bias_eff[...] = jnp.sum(bias_terms, axis=0, keepdims=True)

    def mix(b, p0):
        x = mid[b, pl.ds(p0, CHUNK)].reshape(M, C)
        ct = cot[b, pl.ds(p0, CHUNK)].reshape(M, C)
        mean = jnp.mean(x, axis=-1, keepdims=True)
        cen = x - mean
        inv = lax.rsqrt(jnp.mean(cen * cen, axis=-1, keepdims=True) + norm_eps)
        normed = cen * inv
        n_hi, n_lo = split(normed)
        n2 = jnp.concatenate([n_hi, n_lo], axis=1)
        c_hi, c_lo = split(ct)
        c2 = jnp.concatenate([c_hi, c_lo], axis=1)
        nt2 = jnp.concatenate(split(normed.T), axis=0)
        ct2 = jnp.concatenate(split(ct.T), axis=0)
        cotacc[...] += jnp.sum(ct.reshape(M // 8, 8, C), axis=0)
        dn = jnp.zeros((M, C), f32)
        step = 256
        for h in range(0, HID, step):
            cut = slice(h, h + step)
            act = dot(n2, win2[:, cut]) + dot(n_hi, winlo[:, cut]) + bias_eff[:, cut]
            dh = dot(c2, wot2[:, cut]) + dot(c_hi, wotlo[:, cut])
            phi = 0.5 * (1.0 + lax.erf(act * inverse_root_two))
            slope = phi + act * jnp.exp(-0.5 * act * act) * inverse_root_twopi
            hid_hi, hid_lo = split(act * phi)
            da = dh * slope
            inbacc[:, cut] += jnp.sum(da.reshape(M // 8, 8, step), axis=0)
            da_hi, da_lo = split(da)
            both = dot(da_hi, wintop[cut, :])
            dn = dn + both[:, 0:C] + both[:, C:] + dot(da_lo, wintop[cut, 0:C])
            both = dot(nt2, da_hi)
            nacc[:, cut] += both[0:C] + both[C:] + dot(nt2[0:C], da_lo)
            both = dot(ct2, hid_hi)
            macc[:, cut] += both[0:C] + both[C:] + dot(ct2[0:C], hid_lo)
        dc = inv * (
            dn
            - jnp.mean(dn, axis=-1, keepdims=True)
            - normed * jnp.mean(dn * normed, axis=-1, keepdims=True)
        )
        dbacc[...] += jnp.sum(dc.reshape(M // 8, 8, C), axis=0)
        dcv[b, pl.ds(R + p0, CHUNK), pl.ds(LEFT, W), :] = dc.reshape(CHUNK, W, C)

    def edge_step(n, carry):
        mix(n // 2, lax.rem(n, 2) * (H - CHUNK))
        return carry

    def inner_step(n, carry):
        mix(n // 2, CHUNK + lax.rem(n, 2) * CHUNK)
        return carry

    lax.fori_loop(0, 4, edge_step, 0)
    back = edge_copies(place, dcv, R, LEFT, dcv, dsend, drecv)
    start(back[0:2] + back[4:])
    lax.fori_loop(0, 4, inner_step, 0)
    start(back[2:4])

    factor = 1.0 / math.sqrt(B * H * W * ROWS * COLS)
    nsum, msum = nacc[...], macc[...]
    inb = jnp.sum(inbacc[...], axis=0, keepdims=True)
    wp[0] = ((nsum * gain_col + shift_col * inb) * factor).T
    wp[1] = (msum * (scale_col * factor)).T
    other = 1 - place.core
    r0 = remote(wp.at[other], wcore, 0, place.sibling(), rssend, rsrecv)
    r0.start()

    gain_g = jnp.sum(win * nsum, axis=1, keepdims=True)
    shift_g = jnp.sum(win * inb, axis=1, keepdims=True)
    scale_g = jnp.sum(wo_t * msum, axis=1, keepdims=True)
    inb_g = [jnp.sum(jnp.where(unit == 4 * chan + k, inb, 0.0), axis=1, keepdims=True) for k in range(4)]

    def kgrad_step(b, carry):
        for wb in range(W // 8):
            kernel_grad_tile(src, dcv, kacc, b, wb)
        return carry

    lax.fori_loop(0, 1, kgrad_step, 0)
    r0.wait_recv()
    wa[...] = wp[place.core] + wcore[...]
    r1 = []
    for off in range(1, 4):
        y, partner = place.along_y(off)
        r1.append(remote(wa.at[pl.ds(y * 128, 128)], wry.at[off - 1], off, partner, rssend, rsrecv))
    start(r1)
    lax.fori_loop(1, 2, kgrad_step, 0)

    for n in range(K * K):
        sc[n : n + 1, :] = jnp.sum(kacc[n], axis=0, keepdims=True)
    sc[K * K : K * K + 1, :] = jnp.sum(dbacc[...], axis=0, keepdims=True)
    sc[K * K + 1 :, :] = jnp.zeros((128 - K * K - 1, C), f32)
    grads = sc[...].T
    lane = lanes(C, 128, 1)
    cot_col = jnp.sum(cotacc[...], axis=0, keepdims=True)
    cot_col = jnp.broadcast_to(cot_col, (128, C)).T[:, 0:1]
    columns = [(GAIN, gain_g), (SHIFT, shift_g), (OB, scale_col * cot_col), (SCALE, scale_g + ob_col * cot_col)]
    columns += [(IB + k, inb_g[k]) for k in range(4)]
    for at, column in columns:
        grads = jnp.where(lane == at, column, grads)
    sp[...] = grads * factor
    q1 = []
    for off in range(1, 4):
        y, partner = place.along_y(off)
        q1.append(remote(sp.at[pl.ds(y * 32, 32)], sry.at[off - 1], 14 + off - 1, partner, rssend, rsrecv))
    start(q1)

    arrive(r1)
    wb_[...] = wa[pl.ds(place.y * 128, 128)] + wry[0] + wry[1] + wry[2]
    r2 = []
    for off in range(1, 4):
        z, partner = place.along_z(off)
        r2.append(remote(wb_.at[pl.ds(z * 32, 32)], wrz.at[off - 1], 4 + off - 1, partner, rssend, rsrecv))
    start(r2)
    arrive(q1)
    sb[...] = sp[pl.ds(place.y * 32, 32)] + sry[0] + sry[1] + sry[2]
    q2 = []
    for off in range(1, 4):
        z, partner = place.along_z(off)
        q2.append(remote(sb.at[pl.ds(z * 8, 8)], srz.at[off - 1], 17 + off - 1, partner, rssend, rsrecv))
    start(q2)

    arrive(back)
    clear_outside(place, dcv)

    def out_step(b, carry):
        for wb in range(W // 8):
            acc = conv_tile(dcv, taps, b, wb, True)
            for p in range(H):
                at = slice(8 * wb, 8 * wb + 8)
                fg[b, p, at, :] = acc[p] + cot[b, p, at, :]
        return carry

    lax.fori_loop(0, 1, out_step, 0)
    put0 = pltpu.make_async_copy(fg.at[0], fg_out.at[0], out_sem.at[0])
    put0.start()

    arrive(r2)
    wc[...] = wb_[pl.ds(place.z * 32, 32)] + wrz[0] + wrz[1] + wrz[2]
    r3 = []
    for off in range(1, 8):
        g, partner = place.in_group(off)
        r3.append(
            remote(wc.at[pl.ds(g // 2 * 8, 8)], wrx.at[place.core, place.x], 7 + off - 1, partner, rssend, rsrecv)
        )
    start(r3)
    wrx[place.core, place.x] = wc[pl.ds(place.x * 8, 8)]
    arrive(q2)
    srx[0] = sb[pl.ds(place.z * 8, 8)] + srz[0] + srz[1] + srz[2]
    q3 = []
    for off in range(1, 8):
        q3.append(remote(srx.at[0], srx.at[off], 20 + off - 1, place.in_group(off)[1], rssend, rsrecv))
    start(q3)

    lax.fori_loop(1, 2, out_step, 0)
    put1 = pltpu.make_async_copy(fg.at[1], fg_out.at[1], out_sem.at[1])
    put1.start()

    arrive(r3)
    for kind in range(2):
        total = wrx[kind, 0] + wrx[kind, 1] + wrx[kind, 2] + wrx[kind, 3]
        weight_out[kind] = jnp.where(place.core == 0, total[0:4], total[4:8])
    arrive(q3)
    total = srx[0]
    for off in range(1, 8):
        total = total + srx[off]
    mine = lanes(8, C, 0) == place.g
    small_out[...] = jnp.sum(jnp.where(mine, total, 0.0), axis=0, keepdims=True)

    put0.wait()
    put1.wait()
    for copy in s1 + w1 + s2 + w2 + s3 + w3 + edges + back + [r0] + r1 + r2 + r3 + q1 + q2 + q3:
        copy.wait_send()


def call(features, cotangent, small, weights):
    vmem = lambda *shape: pltpu.VMEM(shape, f32)
    half = lambda *shape: pltpu.VMEM(shape, bf16)
    dma = lambda n: pltpu.SemaphoreType.DMA((n,))
    anywhere = pl.BlockSpec(memory_space=pl.ANY)
    inside = pl.BlockSpec(memory_space=pltpu.VMEM)
    return pl.pallas_call(
        kernel,
        out_shape=(
            jax.ShapeDtypeStruct((B, H, W, C), f32),
            jax.ShapeDtypeStruct((1, C), f32),
            jax.ShapeDtypeStruct((2, 4, C), f32),
        ),
        in_specs=[anywhere, anywhere, inside, inside],
        out_specs=(anywhere, inside, inside),
        scratch_shapes=[
            vmem(B, HE, WE, C), vmem(B, H, W, C), vmem(B, HE, WE, C), vmem(B, H, W, C), vmem(B, H, W, C),
            vmem(128, 1, C), vmem(2, 128, 4, C), vmem(K * K, 8, C),
            half(2 * C, HID), half(C, HID), half(HID, 2 * C), half(8, C), half(2 * C, HID), half(C, HID), vmem(1, HID),
            vmem(C, HID), vmem(C, HID), vmem(8, HID), vmem(K * K, 8, C), vmem(8, C), vmem(8, C),
            vmem(2, HID, C), vmem(HID, C), vmem(HID, C), vmem(3, 128, C), vmem(128, C), vmem(3, 32, C), vmem(32, C),
            vmem(2, 4, 8, C), vmem(128, C), vmem(3, 32, C), vmem(32, C), vmem(3, 8, C), vmem(128, C), vmem(8, 8, C),
            dma(4), dma(2), dma(8), dma(8), dma(8), dma(8), dma(26), dma(26), dma(27), dma(27),
        ],
        compiler_params=pltpu.CompilerParams(
            collective_id=0, has_side_effects=True, vmem_limit_bytes=56 * 2**20
        ),
    )(features, cotangent, small, weights)


def per_device(
    features, cotangent, conv_kernel, conv_bias, norm_gain, norm_shift,
    w_in, in_bias, w_out, out_bias, layer_scale,
):
    small = jnp.concatenate(
        [
            conv_kernel.reshape(K * K), conv_bias, norm_gain, norm_shift, out_bias, layer_scale,
            in_bias, jnp.zeros((128 - IB - 4,), f32),
        ]
    ).reshape(1, 1, C)
    weights = jnp.stack([w_in.T, w_out]).reshape(2, 1, 4, C)
    fg, small_g, weight_g = call(features, cotangent, small, weights)
    row = small_g[0]
    return (
        fg,
        row[0 : K * K].reshape(K, K, 1),
        row[CB : CB + 1],
        row[GAIN : GAIN + 1],
        row[SHIFT : SHIFT + 1],
        weight_g[0].T,
        row[IB : IB + 4],
        weight_g[1],
        row[OB : OB + 1],
        row[SCALE : SCALE + 1],
    )


def solution(mesh):
    both = ("row", "col")
    tile = P(None, "row", "col", None)
    taps, vector = P(None, None, both), P(both)
    return jax.shard_map(
        per_device,
        mesh=mesh,
        in_specs=(tile, tile, taps, vector, vector, vector, P(None, both), vector, P(both, None), vector, vector),
        out_specs=(tile, taps, vector, vector, vector, P(None, both), vector, P(both, None), vector, vector),
        check_vma=False,
    )
```

```python
import functools
import math

import jax
import jax.numpy as jnp
from jax import lax
from jax.experimental import pallas as pl
from jax.experimental.pallas import tpu as pltpu
from jax.sharding import PartitionSpec as P

norm_eps = 1e-06
inverse_root_two = 0.7071067811865476
inverse_root_twopi = 0.3989422804014327
MESH = pl.DeviceIdType.MESH
f32, bf16 = jnp.float32, jnp.bfloat16

K, R = 7, 3
C, HID = 128, 512
B, H, W = 2, 16, 64
LEFT = 8
WE = W + 2 * LEFT
HE = H + 2 * R
ROWS, COLS = 8, 16
QUARTER = H // 4
M = 2 * QUARTER * W
TAPS, CB, GAIN, SHIFT, OB, SCALE, IB = 0, 49, 50, 51, 52, 53, 54


def split(x):
    hi = x.astype(bf16)
    return hi, (x - hi.astype(f32)).astype(bf16)


def dot(a, b):
    return jnp.dot(a, b, preferred_element_type=f32)


def lanes(x, n, axis):
    return lax.broadcasted_iota(jnp.int32, (x, n), axis)


class Place:
    def __init__(self):
        self.row, self.col = lax.axis_index("row"), lax.axis_index("col")
        self.y = self.row // 2
        self.z = lax.rem(self.row, 2) * 2 + self.col // 8
        self.g = lax.rem(self.col, 8)
        self.x, self.core = self.g // 2, lax.rem(self.g, 2)

    def at(self, y, z, x, core):
        return (y * 2 + z // 2, lax.rem(z, 2) * 8 + x * 2 + core)

    def turn(self, y=0, z=0, x=0):
        y, z, x = lax.rem(self.y + y, 4), lax.rem(self.z + z, 4), lax.rem(self.x + x, 4)
        return y, z, x, self.at(y, z, x, self.core)

    def in_plane(self, off):
        other = lax.rem(self.g + off, 8)
        return self.at(self.y, self.z, other // 2, lax.rem(other, 2))

    def in_column(self, off):
        other = lax.rem(self.z * 2 + self.core + off, 8)
        return self.at(self.y, other // 2, self.x, lax.rem(other, 2))

    def sibling(self):
        return self.at(self.y, self.z, self.x, 1 - self.core)

    def neighbour(self, dr, dc):
        return (lax.rem(self.row + dr + ROWS, ROWS), lax.rem(self.col + dc + COLS, COLS))


STEPS = [(0, -1), (0, 1), (-1, 0), (1, 0), (-1, -1), (-1, 1), (1, -1), (1, 1)]


def rows_of(step, base, sent):
    if step == 0:
        return pl.ds(base, H)
    if sent:
        return pl.ds(base, R) if step < 0 else pl.ds(base + H - R, R)
    return pl.ds(R + H, R) if step < 0 else pl.ds(0, R)


def cols_of(step, base, sent):
    if step == 0:
        return pl.ds(base, W)
    if sent:
        return pl.ds(base, LEFT) if step < 0 else pl.ds(base + W - LEFT, LEFT)
    return pl.ds(LEFT + W, LEFT) if step < 0 else pl.ds(0, LEFT)


def edge_copies(place, src, row0, col0, ext, send, recv):
    copies = []
    for n, (dr, dc) in enumerate(STEPS):
        copies.append(
            pltpu.make_async_remote_copy(
                src_ref=src.at[:, rows_of(dr, row0, True), cols_of(dc, col0, True), :],
                dst_ref=ext.at[:, rows_of(dr, R, False), cols_of(dc, LEFT, False), :],
                send_sem=send.at[n],
                recv_sem=recv.at[n],
                device_id=place.neighbour(dr, dc),
                device_id_type=MESH,
            )
        )
    return copies


def clear_columns(place, ext):
    @pl.when(place.col == 0)
    def _():
        ext[:, R : R + H, 0:LEFT] = jnp.zeros((B, H, LEFT, C), f32)

    @pl.when(place.col == COLS - 1)
    def _():
        ext[:, R : R + H, LEFT + W :] = jnp.zeros((B, H, LEFT, C), f32)


def clear_rows(place, ext):
    for edge, at in ((0, slice(0, R)), (ROWS - 1, slice(R + H, HE))):

        @pl.when(place.row == edge)
        def _():
            ext[:, at] = jnp.zeros((B, R, WE, C), f32)

        @pl.when(place.col == 0)
        def _():
            ext[:, at, 0:LEFT] = jnp.zeros((B, R, LEFT, C), f32)

        @pl.when(place.col == COLS - 1)
        def _():
            ext[:, at, LEFT + W :] = jnp.zeros((B, R, LEFT, C), f32)


def conv_tile(ext, taps, b, wb, flip, rows, acc):
    for j in range(K):
        tap = [taps[(K - 1 - i) * K + K - 1 - j] if flip else taps[i * K + j] for i in range(K)]
        for e in rows:
            x = ext[b, e, LEFT - R + 8 * wb + j : LEFT - R + 8 * wb + j + 8, :]
            for i in range(K):
                p = e - i
                if 0 <= p < H:
                    acc[p] = acc[p] + tap[i] * x
    return acc


INNER = range(R, R + H)
OUTER = (*range(R), *range(R + H, HE))
FRINGE = (*range(R), *range(H - R, H))


def kernel_grad_tile(ext, dcv, kacc, b, wb):
    grads = [dcv[b, R + p, LEFT + 8 * wb : LEFT + 8 * wb + 8, :] for p in range(H)]
    for j in range(K):
        acc = [kacc[i * K + j] for i in range(K)]
        for e in range(HE):
            x = ext[b, e, LEFT - R + 8 * wb + j : LEFT - R + 8 * wb + j + 8, :]
            for i in range(K):
                p = e - i
                if 0 <= p < H:
                    acc[i] = acc[i] + grads[p] * x
        for i in range(K):
            kacc[i * K + j] = acc[i]


def widen(column, n):
    one = jnp.broadcast_to(column, (column.shape[0], 128))
    return jnp.concatenate([one] * n, axis=1)


def kernel(
    feat, cot_hbm, taps_in, cb_in, gain_in, shift_in, ob_in, scale_in, ib_in, win_in, wout_in,
    fg_out, small_out, weight_out,
    taps_s, cb_s, gain_s, shift_s, ob_s, scale_s, ib_s, srow,
    src, cot, dcv, mid, fg, sg, wg, taps,
    win2, winlo, wintop, wot2, wotlo, bias_eff,
    nacc, macc, inbacc, kacc, cotacc, dbacc,
    wp, wcore, wa, wr1, wb_, wr2, wc, wr3, wd, wr4, rows, sp, sry, sb, srz, srx,
    local, out_sem, fsend, frecv, dsend, drecv, agsend, agrecv, rssend, rsrecv,
):
    place = Place()
    y, z, x, core = place.y, place.z, place.x, place.core

    scalars = [(taps_in, taps_s), (cb_in, cb_s), (gain_in, gain_s), (shift_in, shift_s), (ob_in, ob_s), (scale_in, scale_s), (ib_in, ib_s)]
    params = [pltpu.make_async_copy(a, b, local.at[4 + n]) for n, (a, b) in enumerate(scalars)]
    own = [
        pltpu.make_async_copy(feat, src.at[:, pl.ds(R, H), pl.ds(LEFT, W), :], local.at[0]),
        pltpu.make_async_copy(cot_hbm, cot, local.at[1]),
        pltpu.make_async_copy(win_in, wg.at[0, y, z, x, core], local.at[2]),
        pltpu.make_async_copy(wout_in, wg.at[1, y, z, x, core], local.at[3]),
    ]
    for copy in params + own:
        copy.start()

    barrier = pltpu.get_barrier_semaphore()
    partners = [place.neighbour(dr, dc) for dr, dc in STEPS]
    partners += [place.in_plane(off) for off in range(1, 8)]
    partners += [place.in_column(off) for off in range(1, 8)]
    partners += [place.turn(y=off)[3] for off in range(1, 4)]
    for partner in partners:
        pl.semaphore_signal(barrier, inc=1, device_id=partner, device_id_type=MESH)

    for copy in params:
        copy.wait()
    lane = lanes(1, 128, 1)
    row = jnp.zeros((1, 128), f32)
    for i in range(K):
        for j in range(K):
            row = jnp.where(lane == TAPS + i * K + j, taps_s[i, 0, j], row)
    for at, ref in ((CB, cb_s), (GAIN, gain_s), (SHIFT, shift_s), (OB, ob_s), (SCALE, scale_s)):
        row = jnp.where(lane == at, ref[0], row)
    for k in range(4):
        row = jnp.where(lane == IB + k, ib_s[k], row)
    srow[...] = row
    sg[y, z, x, core] = row
    kacc[...] = jnp.zeros_like(kacc)
    nacc[...] = jnp.zeros_like(nacc)
    macc[...] = jnp.zeros_like(macc)
    inbacc[...] = jnp.zeros_like(inbacc)
    cotacc[...] = jnp.zeros_like(cotacc)
    dbacc[...] = jnp.zeros_like(dbacc)

    pl.semaphore_wait(barrier, len(partners))

    def remote(s, d, sem, partner, send, recv):
        return pltpu.make_async_remote_copy(
            src_ref=s, dst_ref=d, send_sem=send.at[sem], recv_sem=recv.at[sem],
            device_id=partner, device_id_type=MESH,
        )

    def same(ref, sem, partner):
        return remote(ref, ref, sem, partner, agsend, agrecv)

    cell = (y, z, x, core)
    group = [place.in_column(off) for off in range(1, 8)]
    xs = [place.turn(x=off)[3] for off in range(1, 4)]
    ys = [place.turn(y=off)[3] for off in range(1, 4)]
    s1 = [remote(srow, sg.at[cell], n, p, agsend, agrecv) for n, p in enumerate(group)]
    w1 = [remote(win_in, wg.at[(0, *cell)], 7 + n, p, agsend, agrecv) for n, p in enumerate(group)]
    v1 = [remote(wout_in, wg.at[(1, *cell)], 14 + n, p, agsend, agrecv) for n, p in enumerate(group)]
    s2 = [same(sg.at[y, :, x], 21 + n, p) for n, p in enumerate(xs)]
    w2 = [same(wg.at[0, y, :, x], 24 + n, p) for n, p in enumerate(xs)]
    v2 = [same(wg.at[1, y, :, x], 27 + n, p) for n, p in enumerate(ys)]
    s3 = [same(sg.at[y], 30 + n, p) for n, p in enumerate(ys)]
    w3 = [same(wg.at[0, y], 33 + n, p) for n, p in enumerate(ys)]
    v3 = [same(wg.at[1, :, :, x], 36 + n, p) for n, p in enumerate(xs)]
    edges = edge_copies(place, feat, 0, 0, src, fsend, frecv)

    def start(copies):
        for copy in copies:
            copy.start()

    def arrive(copies):
        for copy in copies:
            copy.wait_recv()

    start(s1)
    start(w1)
    start(v1)
    start(edges)
    own[2].wait()
    own[3].wait()
    arrive(s1)
    start(s2)
    arrive(w1)
    start(w2)
    arrive(v1)
    start(v2)
    arrive(s2)
    start(s3)
    arrive(w2)
    start(w3)
    arrive(v2)
    start(v3)
    own[0].wait()
    own[1].wait()
    arrive(edges[0:2])
    clear_columns(place, src)
    arrive(s3)

    small = sg.reshape(128, C)[...]
    small_t = small.T
    for n in range(K * K):
        taps[n] = jnp.broadcast_to(small_t[TAPS + n : TAPS + n + 1, :], (8, C))
    conv_bias = jnp.broadcast_to(small_t[CB : CB + 1, :], (8, C))

    def conv_step(b, carry):
        for wb in range(W // 8):
            acc = conv_tile(src, taps, b, wb, False, INNER, {p: conv_bias for p in range(H)})
            for p in range(H):
                mid[b, p, 8 * wb : 8 * wb + 8, :] = acc[p]
        return carry

    lax.fori_loop(0, B, conv_step, 0)
    arrive(edges[2:])
    clear_rows(place, src)

    def conv_rest(b, carry):
        for wb in range(W // 8):
            at = slice(8 * wb, 8 * wb + 8)
            acc = conv_tile(src, taps, b, wb, False, OUTER, {p: mid[b, p, at, :] for p in FRINGE})
            for p in FRINGE:
                mid[b, p, at, :] = acc[p]
        return carry

    lax.fori_loop(0, B, conv_rest, 0)

    arrive(w3)
    arrive(v3)
    gain_wide, shift_wide = widen(small[:, GAIN : GAIN + 1], 4), widen(small[:, SHIFT : SHIFT + 1], 4)
    scale_wide, ob_wide = widen(small[:, SCALE : SCALE + 1], 4), widen(small[:, OB : OB + 1], 1)
    win_t = wg.at[0].reshape(HID, C)[...]
    win = win_t.T
    wo_t = wg.at[1].reshape(HID, C)[...].T
    hi, lo = split(win * gain_wide)
    win2[0:C, :] = hi
    win2[C:, :] = hi
    winlo[...] = lo
    hi, lo = split(win_t * small_t[GAIN : GAIN + 1, :])
    wintop[:, 0:C] = hi
    wintop[:, C:] = lo
    hi, lo = split(wo_t * scale_wide)
    wot2[0:C, :] = hi
    wot2[C:, :] = hi
    wotlo[...] = lo
    pick = [lanes(32, 128, 1) == 4 * lanes(32, 128, 0) + k for k in range(4)]
    shifted = win * shift_wide
    for t in range(4):
        cut, band = slice(128 * t, 128 * t + 128), slice(32 * t, 32 * t + 32)
        terms = [jnp.where(pick[k], small[band, IB + k : IB + k + 1], 0.0) for k in range(4)]
        bias_eff[:, cut] = jnp.sum(shifted[:, cut], axis=0, keepdims=True) + jnp.sum(sum(terms), axis=0, keepdims=True)

    def mix(b, starts):
        spans = [slice(p, p + QUARTER) for p in starts]
        x = jnp.concatenate([mid[b, s].reshape(M // 2, C) for s in spans], axis=0)
        ct = jnp.concatenate([cot[b, s].reshape(M // 2, C) for s in spans], axis=0)
        mean = jnp.mean(x, axis=-1, keepdims=True)
        cen = x - mean
        inv = lax.rsqrt(jnp.mean(cen * cen, axis=-1, keepdims=True) + norm_eps)
        normed = cen * inv
        n_hi, n_lo = split(normed)
        n2 = jnp.concatenate([n_hi, n_lo], axis=1)
        c_hi, c_lo = split(ct)
        c2 = jnp.concatenate([c_hi, c_lo], axis=1)
        nt2 = jnp.concatenate(split(normed.T), axis=0)
        ct2 = jnp.concatenate(split(ct.T), axis=0)
        cotacc[...] += jnp.sum(ct.reshape(M // 8, 8, C), axis=0)
        dn = jnp.zeros((M, C), f32)
        step = 256
        for h in range(0, HID, step):
            cut = slice(h, h + step)
            act = dot(n2, win2[:, cut]) + dot(n_hi, winlo[:, cut]) + bias_eff[:, cut]
            dh = dot(c2, wot2[:, cut]) + dot(c_hi, wotlo[:, cut])
            phi = 0.5 * (1.0 + lax.erf(act * inverse_root_two))
            slope = phi + act * jnp.exp(-0.5 * act * act) * inverse_root_twopi
            hid_hi, hid_lo = split(act * phi)
            da = dh * slope
            inbacc[:, cut] += jnp.sum(da.reshape(M // 8, 8, step), axis=0)
            da_hi, da_lo = split(da)
            both = dot(da_hi, wintop[cut, :])
            dn = dn + both[:, 0:C] + both[:, C:] + dot(da_lo, wintop[cut, 0:C])
            both = dot(nt2, da_hi)
            nacc[:, cut] += both[0:C] + both[C:] + dot(nt2[0:C], da_lo)
            both = dot(ct2, hid_hi)
            macc[:, cut] += both[0:C] + both[C:] + dot(ct2[0:C], hid_lo)
        dc = inv * (
            dn
            - jnp.mean(dn, axis=-1, keepdims=True)
            - normed * jnp.mean(dn * normed, axis=-1, keepdims=True)
        )
        dbacc[...] += jnp.sum(dc.reshape(M // 8, 8, C), axis=0)
        for n, p in enumerate(starts):
            part = dc[n * (M // 2) : (n + 1) * (M // 2)]
            dcv[b, R + p : R + p + QUARTER, LEFT : LEFT + W, :] = part.reshape(QUARTER, W, C)

    def edge_step(b, carry):
        mix(b, (0, H - QUARTER))
        return carry

    def inner_step(b, carry):
        mix(b, (QUARTER, 2 * QUARTER))
        return carry

    lax.fori_loop(0, B, edge_step, 0)
    back = edge_copies(place, dcv, R, LEFT, dcv, dsend, drecv)
    start(back[2:])
    lax.fori_loop(0, B, inner_step, 0)
    start(back[0:2])

    factor = 1.0 / math.sqrt(B * H * W * ROWS * COLS)
    nsum, msum = nacc[...], macc[...]
    inb = jnp.sum(inbacc[...], axis=0, keepdims=True)
    wp[0] = ((nsum * gain_wide + shift_wide * inb) * factor).T.reshape(4, 4, 4, 8, C)
    wp[1] = (msum * (scale_wide * factor)).T.reshape(4, 4, 4, 8, C)
    r0 = [remote(wp.at[1 - core], wcore, 0, place.sibling(), rssend, rsrecv)]
    start(r0)

    def kgrad_step(b, carry):
        for wb in range(W // 8):
            kernel_grad_tile(src, dcv, kacc, b, wb)
        return carry

    lax.fori_loop(0, 1, kgrad_step, 0)
    arrive(r0)
    for a in range(4):
        for b in range(4):
            yy, xx = a * (1 - core) + b * core, b * (1 - core) + a * core
            wa[a, :, b] = wp[core, yy, :, xx] + wcore[yy, :, xx]
    first, second = y * (1 - core) + x * core, x * (1 - core) + y * core
    r1, r2, r3 = [], [], []
    for off in range(1, 4):
        to = place.turn(y=off * (1 - core), x=off * core)[3]
        r1.append(remote(wa.at[lax.rem(first + off, 4)], wr1.at[off - 1], off, to, rssend, rsrecv))
        to = place.turn(y=off * core, x=off * (1 - core))[3]
        r2.append(remote(wb_.at[lax.rem(second + off, 4)], wr2.at[off - 1], 3 + off, to, rssend, rsrecv))
        zz, to = place.turn(z=off)[1::2]
        r3.append(remote(wc.at[zz], wr3.at[off - 1], 6 + off, to, rssend, rsrecv))
    r4 = [remote(wd, wr4, 10, place.sibling(), rssend, rsrecv)]
    start(r1)
    lax.fori_loop(1, 2, kgrad_step, 0)

    gain_g = jnp.sum(win * nsum, axis=1, keepdims=True)
    shift_g = jnp.sum(win * inb, axis=1, keepdims=True)
    scale_g = jnp.sum(wo_t * msum, axis=1, keepdims=True)
    for n in range(K * K):
        rows[n : n + 1, :] = jnp.sum(kacc[n], axis=0, keepdims=True)
    rows[K * K : K * K + 1, :] = jnp.sum(dbacc[...], axis=0, keepdims=True)
    rows[K * K + 1 : K * K + 2, :] = jnp.sum(cotacc[...], axis=0, keepdims=True)
    rows[K * K + 2 :, :] = jnp.zeros((128 - K * K - 2, C), f32)
    grads = rows[...].T
    lane = lanes(C, 128, 1)
    cot_wide = widen(grads[:, K * K + 1 : K * K + 2], 1)
    columns = [(GAIN, gain_g), (SHIFT, shift_g), (OB, scale_wide[:, 0:C] * cot_wide), (SCALE, scale_g + ob_wide * cot_wide)]
    for k in range(4):
        terms = [jnp.where(pick[k], inb[:, 128 * t : 128 * t + 128], 0.0) for t in range(4)]
        columns.append((IB + k, jnp.sum(jnp.concatenate(terms, axis=0), axis=1, keepdims=True)))
    for at, column in columns:
        grads = jnp.where(lane == at, column, grads)
    sp[...] = grads * factor
    q1, q2, q3 = [], [], []
    for off in range(1, 4):
        yy, _, _, to = place.turn(y=off)
        q1.append(remote(sp.at[pl.ds(yy * 32, 32)], sry.at[off - 1], 10 + off, to, rssend, rsrecv))
        zz, to = place.turn(z=off)[1::2]
        q2.append(remote(sb.at[pl.ds(zz * 8, 8)], srz.at[off - 1], 13 + off, to, rssend, rsrecv))
    for off in range(1, 8):
        q3.append(remote(srx.at[0], srx.at[off], 16 + off, place.in_plane(off), rssend, rsrecv))
    start(q1)

    arrive(back[0:2])
    clear_columns(place, dcv)

    def out_step(b, carry):
        for wb in range(W // 8):
            at = slice(8 * wb, 8 * wb + 8)
            acc = conv_tile(dcv, taps, b, wb, True, INNER, {p: cot[b, p, at, :] for p in range(H)})
            for p in range(H):
                fg[b, p, at, :] = acc[p]
        return carry

    def out_rest(b, carry):
        for wb in range(W // 8):
            at = slice(8 * wb, 8 * wb + 8)
            acc = conv_tile(dcv, taps, b, wb, True, OUTER, {p: fg[b, p, at, :] for p in FRINGE})
            for p in FRINGE:
                fg[b, p, at, :] = acc[p]
        return carry

    lax.fori_loop(0, 1, out_step, 0)
    arrive(r1)
    for n in range(4):
        wb_[n] = wa[first, :, n] + wr1[0, :, n] + wr1[1, :, n] + wr1[2, :, n]
    start(r2)
    arrive(q1)
    sb[...] = sp[pl.ds(y * 32, 32)] + sry[0] + sry[1] + sry[2]
    start(q2)
    lax.fori_loop(1, 2, out_step, 0)
    arrive(r2)
    wc[...] = wb_[second] + wr2[0] + wr2[1] + wr2[2]
    start(r3)
    arrive(q2)
    srx[0] = sb[pl.ds(z * 8, 8)] + srz[0] + srz[1] + srz[2]
    start(q3)
    arrive(back[2:])
    clear_rows(place, dcv)
    lax.fori_loop(0, B, out_rest, 0)
    put = pltpu.make_async_copy(fg, fg_out, out_sem.at[0])
    put.start()

    arrive(r3)
    wd[...] = wc[z] + wr3[0] + wr3[1] + wr3[2]
    start(r4)
    arrive(q3)
    total = srx[0]
    for off in range(1, 8):
        total = total + srx[off]
    mine = lanes(8, C, 0) == place.g
    small_out[...] = jnp.sum(jnp.where(mine, total, 0.0), axis=0, keepdims=True)
    arrive(r4)
    kept, got = wd[...], wr4[...]
    weight_out[core] = jnp.where(core == 0, kept[0:4], kept[4:8])
    weight_out[1 - core] = jnp.where(core == 0, got[0:4], got[4:8])

    put.wait()
    for copy in s1 + w1 + v1 + s2 + w2 + v2 + s3 + w3 + v3 + edges + back + r0 + r1 + r2 + r3 + r4 + q1 + q2 + q3:
        copy.wait_send()


def deliver(
    fg_in, small_in, weight_in,
    fg_out, taps_out, cb_out, gain_out, shift_out, win_out, ib_out, wout_out, ob_out, scale_out,
    buf, row, sem,
):
    pieces = [(b, pl.ds(h, H // 2)) for b in range(B) for h in range(0, H, H // 2)]
    small = pltpu.make_async_copy(small_in, row, sem.at[8])
    weights = [pltpu.make_async_copy(weight_in.at[k], ref, sem.at[9 + k]) for k, ref in enumerate((win_out, wout_out))]
    small.start()
    gets = [pltpu.make_async_copy(fg_in.at[at], buf.at[at], sem.at[n]) for n, at in enumerate(pieces)]
    puts = [pltpu.make_async_copy(buf.at[at], fg_out.at[at], sem.at[4 + n]) for n, at in enumerate(pieces)]
    for copy in gets + weights:
        copy.start()
    small.wait()
    for i in range(K):
        for j in range(K):
            taps_out[i, 0, j] = row[0, TAPS + i * K + j]
    for at, ref in ((CB, cb_out), (GAIN, gain_out), (SHIFT, shift_out), (OB, ob_out), (SCALE, scale_out)):
        ref[0] = row[0, at]
    for k in range(4):
        ib_out[k] = row[0, IB + k]
    for get, put in zip(gets, puts):
        get.wait()
        put.start()
    for copy in weights + puts:
        copy.wait()


def per_device(
    features, cotangent, conv_kernel, conv_bias, norm_gain, norm_shift,
    w_in, in_bias, w_out, out_bias, layer_scale,
):
    vmem = lambda *shape: pltpu.VMEM(shape, f32)
    smem = lambda *shape: pltpu.SMEM(shape, f32)
    half = lambda *shape: pltpu.VMEM(shape, bf16)
    dma = lambda n: pltpu.SemaphoreType.DMA((n,))
    out = lambda *shape: jax.ShapeDtypeStruct(shape, f32)
    anywhere = pl.BlockSpec(memory_space=pl.ANY)
    inside = pl.BlockSpec(memory_space=pltpu.VMEM)
    scalar = pl.BlockSpec(memory_space=pltpu.SMEM)
    tile = (B, H, W, C)
    fg, small, weights = pl.pallas_call(
        kernel,
        out_shape=(out(*tile), out(1, C), out(2, 4, C)),
        in_specs=[anywhere] * 11,
        out_specs=(anywhere, inside, inside),
        scratch_shapes=[
            smem(K, 1, K), smem(1), smem(1), smem(1), smem(1), smem(1), smem(4), vmem(1, C),
            vmem(B, HE, WE, C), vmem(*tile), vmem(B, HE, WE, C), vmem(*tile), vmem(*tile),
            vmem(4, 4, 4, 2, 1, C), vmem(2, 4, 4, 4, 2, 4, C), vmem(K * K, 8, C),
            half(2 * C, HID), half(C, HID), half(HID, 2 * C), half(2 * C, HID), half(C, HID), vmem(1, HID),
            vmem(C, HID), vmem(C, HID), vmem(8, HID), vmem(K * K, 8, C), vmem(8, C), vmem(8, C),
            vmem(2, 4, 4, 4, 8, C), vmem(4, 4, 4, 8, C), vmem(4, 4, 4, 8, C), vmem(3, 4, 4, 8, C),
            vmem(4, 4, 8, C), vmem(3, 4, 8, C), vmem(4, 8, C), vmem(3, 8, C), vmem(8, C), vmem(8, C),
            vmem(128, C), vmem(128, C), vmem(3, 32, C), vmem(32, C), vmem(3, 8, C), vmem(8, 8, C),
            dma(11), dma(1), dma(8), dma(8), dma(8), dma(8), dma(39), dma(39), dma(24), dma(24),
        ],
        compiler_params=pltpu.CompilerParams(
            collective_id=0, has_side_effects=True, vmem_limit_bytes=56 * 2**20
        ),
    )(
        features, cotangent, conv_kernel.transpose(0, 2, 1), conv_bias, norm_gain, norm_shift,
        out_bias, layer_scale, in_bias, w_in.T, w_out,
    )
    fg, taps_g, cb_g, gain_g, shift_g, win_g, ib_g, wout_g, ob_g, scale_g = pl.pallas_call(
        deliver,
        out_shape=(
            out(*tile), out(K, 1, K), out(1), out(1), out(1), out(4, C), out(4), out(4, C), out(1), out(1),
        ),
        in_specs=[anywhere] * 3,
        out_specs=(anywhere, scalar, scalar, scalar, scalar, inside, scalar, inside, scalar, scalar),
        scratch_shapes=[vmem(*tile), smem(1, C), dma(11)],
    )(fg, small, weights)
    return fg, taps_g.transpose(0, 2, 1), cb_g, gain_g, shift_g, win_g.T, ib_g, wout_g, ob_g, scale_g


def solution(mesh):
    both = ("row", "col")
    tile = P(None, "row", "col", None)
    taps, vector = P(None, None, both), P(both)
    return jax.shard_map(
        per_device,
        mesh=mesh,
        in_specs=(tile, tile, taps, vector, vector, vector, P(None, both), vector, P(both, None), vector, vector),
        out_specs=(tile, taps, vector, vector, vector, P(None, both), vector, P(both, None), vector, vector),
        check_vma=False,
    )
```

```python
import functools
import math

import jax
import jax.numpy as jnp
from jax import lax
from jax.experimental import pallas as pl
from jax.experimental.pallas import tpu as pltpu
from jax.sharding import PartitionSpec as P

norm_eps = 1e-06
inverse_root_two = 0.7071067811865476
inverse_root_twopi = 0.3989422804014327
MESH = pl.DeviceIdType.MESH
f32, bf16 = jnp.float32, jnp.bfloat16

K, R = 7, 3
C, HID = 128, 512
B, H, W = 2, 16, 64
LEFT = 8
WE = W + 2 * LEFT
HE = H + 2 * R
ROWS, COLS = 8, 16
QUARTER = H // 4
BLOCKS = B * W // 8
M = 2 * QUARTER * W
TAPS, CB, GAIN, SHIFT, OB, SCALE, IB = 0, 49, 50, 51, 52, 53, 54


def split(x):
    hi = x.astype(bf16)
    return hi, (x - hi.astype(f32)).astype(bf16)


def dot(a, b):
    return jnp.dot(a, b, preferred_element_type=f32)


def lanes(x, n, axis):
    return lax.broadcasted_iota(jnp.int32, (x, n), axis)


class Place:
    def __init__(self):
        self.row, self.col = lax.axis_index("row"), lax.axis_index("col")
        self.y = self.row // 2
        self.z = lax.rem(self.row, 2) * 2 + self.col // 8
        self.g = lax.rem(self.col, 8)
        self.x, self.core = self.g // 2, lax.rem(self.g, 2)

    def at(self, y, z, x, core):
        return (y * 2 + z // 2, lax.rem(z, 2) * 8 + x * 2 + core)

    def turn(self, y=0, z=0, x=0):
        y, z, x = lax.rem(self.y + y, 4), lax.rem(self.z + z, 4), lax.rem(self.x + x, 4)
        return y, z, x, self.at(y, z, x, self.core)

    def in_plane(self, off):
        other = lax.rem(self.g + off, 8)
        return other, self.at(self.y, self.z, other // 2, lax.rem(other, 2))

    def in_column(self, off):
        other = lax.rem(self.z * 2 + self.core + off, 8)
        return self.at(self.y, other // 2, self.x, lax.rem(other, 2))

    def sibling(self):
        return self.at(self.y, self.z, self.x, 1 - self.core)

    def neighbour(self, dr, dc):
        return (lax.rem(self.row + dr + ROWS, ROWS), lax.rem(self.col + dc + COLS, COLS))


STEPS = [(0, -1), (0, 1), (-1, 0), (1, 0), (-1, -1), (-1, 1), (1, -1), (1, 1)]


def rows_of(step, base, sent):
    if step == 0:
        return pl.ds(base, H)
    if sent:
        return pl.ds(base, R) if step < 0 else pl.ds(base + H - R, R)
    return pl.ds(R + H, R) if step < 0 else pl.ds(0, R)


def cols_of(step, base, sent):
    if step == 0:
        return pl.ds(base, W)
    if sent:
        return pl.ds(base, LEFT) if step < 0 else pl.ds(base + W - LEFT, LEFT)
    return pl.ds(LEFT + W, LEFT) if step < 0 else pl.ds(0, LEFT)


def edge_copies(place, src, row0, col0, ext, send, recv):
    copies = []
    for n, (dr, dc) in enumerate(STEPS):
        copies.append(
            pltpu.make_async_remote_copy(
                src_ref=src.at[:, rows_of(dr, row0, True), cols_of(dc, col0, True), :],
                dst_ref=ext.at[:, rows_of(dr, R, False), cols_of(dc, LEFT, False), :],
                send_sem=send.at[n],
                recv_sem=recv.at[n],
                device_id=place.neighbour(dr, dc),
                device_id_type=MESH,
            )
        )
    return copies


def clear_columns(place, ext):
    @pl.when(place.col == 0)
    def _():
        ext[:, R : R + H, 0:LEFT] = jnp.zeros((B, H, LEFT, C), f32)

    @pl.when(place.col == COLS - 1)
    def _():
        ext[:, R : R + H, LEFT + W :] = jnp.zeros((B, H, LEFT, C), f32)


def clear_rows(place, ext):
    for edge, at in ((0, slice(0, R)), (ROWS - 1, slice(R + H, HE))):

        @pl.when(place.row == edge)
        def _():
            ext[:, at] = jnp.zeros((B, R, WE, C), f32)

        @pl.when(place.col == 0)
        def _():
            ext[:, at, 0:LEFT] = jnp.zeros((B, R, LEFT, C), f32)

        @pl.when(place.col == COLS - 1)
        def _():
            ext[:, at, LEFT + W :] = jnp.zeros((B, R, LEFT, C), f32)


def conv_tile(ext, taps, b, wb, flip, rows, acc):
    for j in range(K):
        tap = [taps[(K - 1 - i) * K + K - 1 - j] if flip else taps[i * K + j] for i in range(K)]
        for e in rows:
            x = ext[b, e, pl.ds(8 * wb + LEFT - R + j, 8), :]
            for i in range(K):
                p = e - i
                if 0 <= p < H:
                    acc[p] = acc[p] + tap[i] * x
    return acc


INNER = range(R, R + H)
OUTER = (*range(R), *range(R + H, HE))
FRINGE = (*range(R), *range(H - R, H))


def kernel_grad_tile(ext, dcv, kacc, b, wb):
    grads = [dcv[b, R + p, pl.ds(pl.multiple_of(8 * wb + LEFT, 8), 8), :] for p in range(H)]
    for j in range(K):
        acc = [kacc[i * K + j] for i in range(K)]
        for e in range(HE):
            x = ext[b, e, pl.ds(8 * wb + LEFT - R + j, 8), :]
            for i in range(K):
                p = e - i
                if 0 <= p < H:
                    acc[i] = acc[i] + grads[p] * x
        for i in range(K):
            kacc[i * K + j] = acc[i]


def widen(column, n):
    one = jnp.broadcast_to(column, (column.shape[0], 128))
    return jnp.concatenate([one] * n, axis=1)


def kernel(
    feat, cot_hbm, taps_in, cb_in, gain_in, shift_in, ob_in, scale_in, ib_in, win_in, wout_in,
    fg_out, small_out, weight_out,
    taps_s, cb_s, gain_s, shift_s, ob_s, scale_s, ib_s, srow,
    src, cot, dcv, mid, fg, sg, wg, taps,
    win2, winlo, wintop, wot2, wotlo, bias_eff,
    nacc, macc, inbacc, kacc, cotacc, dbacc,
    wp, wcore, wa, wr1, wb_, wr2, wc, wr3, wd, wr4, rows, sp, srx, sb, sry, sc, srz,
    local, out_sem, fsend, frecv, dsend, drecv, agsend, agrecv, rssend, rsrecv,
):
    place = Place()
    y, z, x, core = place.y, place.z, place.x, place.core

    scalars = [(taps_in, taps_s), (cb_in, cb_s), (gain_in, gain_s), (shift_in, shift_s), (ob_in, ob_s), (scale_in, scale_s), (ib_in, ib_s)]
    params = [pltpu.make_async_copy(a, b, local.at[4 + n]) for n, (a, b) in enumerate(scalars)]
    own = [
        pltpu.make_async_copy(feat, src.at[:, pl.ds(R, H), pl.ds(LEFT, W), :], local.at[0]),
        pltpu.make_async_copy(cot_hbm, cot, local.at[1]),
        pltpu.make_async_copy(win_in, wg.at[0, y, z, x, core], local.at[2]),
        pltpu.make_async_copy(wout_in, wg.at[1, y, z, x, core], local.at[3]),
    ]
    for copy in params + own:
        copy.start()

    barrier = pltpu.get_barrier_semaphore()
    partners = [place.neighbour(dr, dc) for dr, dc in STEPS]
    partners += [place.in_plane(off)[1] for off in range(1, 8)]
    partners += [place.in_column(off) for off in range(1, 8)]
    partners += [place.turn(y=off)[3] for off in range(1, 4)]
    for partner in partners:
        pl.semaphore_signal(barrier, inc=1, device_id=partner, device_id_type=MESH)

    for copy in params:
        copy.wait()
    lane = lanes(1, 128, 1)
    row = jnp.zeros((1, 128), f32)
    for i in range(K):
        for j in range(K):
            row = jnp.where(lane == TAPS + i * K + j, taps_s[i, 0, j], row)
    for at, ref in ((CB, cb_s), (GAIN, gain_s), (SHIFT, shift_s), (OB, ob_s), (SCALE, scale_s)):
        row = jnp.where(lane == at, ref[0], row)
    for k in range(4):
        row = jnp.where(lane == IB + k, ib_s[k], row)
    srow[...] = row
    sg[y, z, x, core] = row
    kacc[...] = jnp.zeros_like(kacc)
    nacc[...] = jnp.zeros_like(nacc)
    macc[...] = jnp.zeros_like(macc)
    inbacc[...] = jnp.zeros_like(inbacc)
    cotacc[...] = jnp.zeros_like(cotacc)
    dbacc[...] = jnp.zeros_like(dbacc)

    pl.semaphore_wait(barrier, len(partners))

    def remote(s, d, sem, partner, send, recv):
        return pltpu.make_async_remote_copy(
            src_ref=s, dst_ref=d, send_sem=send.at[sem], recv_sem=recv.at[sem],
            device_id=partner, device_id_type=MESH,
        )

    def same(ref, sem, partner):
        return remote(ref, ref, sem, partner, agsend, agrecv)

    cell = (y, z, x, core)
    group = [place.in_column(off) for off in range(1, 8)]
    xs = [place.turn(x=off)[3] for off in range(1, 4)]
    ys = [place.turn(y=off)[3] for off in range(1, 4)]
    s1 = [remote(srow, sg.at[cell], n, p, agsend, agrecv) for n, p in enumerate(group)]
    w1 = [remote(win_in, wg.at[(0, *cell)], 7 + n, p, agsend, agrecv) for n, p in enumerate(group)]
    v1 = [remote(wout_in, wg.at[(1, *cell)], 14 + n, p, agsend, agrecv) for n, p in enumerate(group)]
    s2 = [same(sg.at[y, :, x], 21 + n, p) for n, p in enumerate(ys)]
    w2 = [same(wg.at[0, y, :, x], 24 + n, p) for n, p in enumerate(xs)]
    v2 = [same(wg.at[1, y, :, x], 27 + n, p) for n, p in enumerate(ys)]
    s3 = [same(sg.at[:, :, x], 30 + n, p) for n, p in enumerate(xs)]
    w3 = [same(wg.at[0, y], 33 + n, p) for n, p in enumerate(ys)]
    v3 = [same(wg.at[1, :, :, x], 36 + n, p) for n, p in enumerate(xs)]
    edges = edge_copies(place, feat, 0, 0, src, fsend, frecv)

    def start(copies):
        for copy in copies:
            copy.start()

    def arrive(copies):
        for copy in copies:
            copy.wait_recv()

    def leave(copies):
        for copy in copies:
            copy.wait_send()

    start(s1)
    start(w1)
    start(v1)
    start(edges[0:2])
    own[2].wait()
    own[3].wait()
    arrive(s1)
    start(s2)
    arrive(w1)
    start(w2)
    arrive(v1)
    start(v2)
    start(edges[2:])
    arrive(s2)
    start(s3)
    arrive(w2)
    start(w3)
    arrive(v2)
    start(v3)
    own[0].wait()
    own[1].wait()
    arrive(edges[0:2])
    clear_columns(place, src)
    arrive(s3)

    small = sg.reshape(128, C)[...]
    small_t = small.T
    for n in range(K * K):
        taps[n] = jnp.broadcast_to(small_t[TAPS + n : TAPS + n + 1, :], (8, C))
    conv_bias = jnp.broadcast_to(small_t[CB : CB + 1, :], (8, C))

    def column_block(n):
        return n // 8, lax.rem(n, 8), pl.ds(pl.multiple_of(lax.rem(n, 8) * 8, 8), 8)

    def conv_step(n, carry):
        b, wb, at = column_block(n)
        acc = conv_tile(src, taps, b, wb, False, INNER, {p: conv_bias for p in range(H)})
        for p in range(H):
            mid[b, p, at, :] = acc[p]
        return carry

    lax.fori_loop(0, BLOCKS, conv_step, 0)

    def conv_rest(n, carry):
        b, wb, at = column_block(n)
        acc = conv_tile(src, taps, b, wb, False, OUTER, {p: mid[b, p, at, :] for p in FRINGE})
        for p in FRINGE:
            mid[b, p, at, :] = acc[p]
        return carry

    arrive(w3)
    arrive(v3)
    gain_wide, shift_wide = widen(small[:, GAIN : GAIN + 1], 4), widen(small[:, SHIFT : SHIFT + 1], 4)
    scale_wide, ob_wide = widen(small[:, SCALE : SCALE + 1], 4), widen(small[:, OB : OB + 1], 1)
    win_t = wg.at[0].reshape(HID, C)[...]
    win = win_t.T
    wo_t = wg.at[1].reshape(HID, C)[...].T
    hi, lo = split(win * gain_wide)
    win2[0:C, :] = hi
    win2[C:, :] = hi
    winlo[...] = lo
    hi, lo = split(win_t * small_t[GAIN : GAIN + 1, :])
    wintop[:, 0:C] = hi
    wintop[:, C:] = lo
    hi, lo = split(wo_t * scale_wide)
    wot2[0:C, :] = hi
    wot2[C:, :] = hi
    wotlo[...] = lo
    pick = [lanes(32, 128, 1) == 4 * lanes(32, 128, 0) + k for k in range(4)]
    shifted = win * shift_wide
    for t in range(4):
        cut, band = slice(128 * t, 128 * t + 128), slice(32 * t, 32 * t + 32)
        terms = [jnp.where(pick[k], small[band, IB + k : IB + k + 1], 0.0) for k in range(4)]
        bias_eff[:, cut] = jnp.sum(shifted[:, cut], axis=0, keepdims=True) + jnp.sum(sum(terms), axis=0, keepdims=True)

    def mix(b, starts):
        spans = [pl.ds(p, QUARTER) for p in starts]
        x = jnp.concatenate([mid[b, s].reshape(M // 2, C) for s in spans], axis=0)
        ct = jnp.concatenate([cot[b, s].reshape(M // 2, C) for s in spans], axis=0)
        mean = jnp.mean(x, axis=-1, keepdims=True)
        cen = x - mean
        inv = lax.rsqrt(jnp.mean(cen * cen, axis=-1, keepdims=True) + norm_eps)
        normed = cen * inv
        n_hi, n_lo = split(normed)
        n2 = jnp.concatenate([n_hi, n_lo], axis=1)
        c_hi, c_lo = split(ct)
        c2 = jnp.concatenate([c_hi, c_lo], axis=1)
        nt2 = jnp.concatenate(split(normed.T), axis=0)
        ct2 = jnp.concatenate(split(ct.T), axis=0)
        cotacc[...] += jnp.sum(ct.reshape(M // 8, 8, C), axis=0)
        dn = jnp.zeros((M, C), f32)
        step = 256
        for h in range(0, HID, step):
            cut = slice(h, h + step)
            act = dot(n2, win2[:, cut]) + dot(n_hi, winlo[:, cut]) + bias_eff[:, cut]
            dh = dot(c2, wot2[:, cut]) + dot(c_hi, wotlo[:, cut])
            phi = 0.5 * (1.0 + lax.erf(act * inverse_root_two))
            slope = phi + act * jnp.exp(-0.5 * act * act) * inverse_root_twopi
            hid_hi, hid_lo = split(act * phi)
            da = dh * slope
            inbacc[:, cut] += jnp.sum(da.reshape(M // 8, 8, step), axis=0)
            da_hi, da_lo = split(da)
            both = dot(da_hi, wintop[cut, :])
            dn = dn + both[:, 0:C] + both[:, C:] + dot(da_lo, wintop[cut, 0:C])
            both = dot(nt2, da_hi)
            nacc[:, cut] += both[0:C] + both[C:] + dot(nt2[0:C], da_lo)
            both = dot(ct2, hid_hi)
            macc[:, cut] += both[0:C] + both[C:] + dot(ct2[0:C], hid_lo)
        dc = inv * (
            dn
            - jnp.mean(dn, axis=-1, keepdims=True)
            - normed * jnp.mean(dn * normed, axis=-1, keepdims=True)
        )
        dbacc[...] += jnp.sum(dc.reshape(M // 8, 8, C), axis=0)
        for n, p in enumerate(starts):
            part = dc[n * (M // 2) : (n + 1) * (M // 2)]
            dcv[b, pl.ds(R + p, QUARTER), LEFT : LEFT + W, :] = part.reshape(QUARTER, W, C)

    back = edge_copies(place, dcv, R, LEFT, dcv, dsend, drecv)

    def mix_step(n, carry):
        outer = lax.rem((n + 1) // 2, 2)

        @pl.when(n == 1)
        def _():
            arrive(edges[2:])
            clear_rows(place, src)
            lax.fori_loop(0, BLOCKS, conv_rest, 0)

        @pl.when(n == 3)
        def _():
            start(back[2:])

        mix(n // 2, (QUARTER * (1 - outer), QUARTER * (2 + outer)))
        return carry

    lax.fori_loop(0, 4, mix_step, 0)
    start(back[0:2])

    factor = 1.0 / math.sqrt(B * H * W * ROWS * COLS)
    nsum, msum = nacc[...], macc[...]
    inb = jnp.sum(inbacc[...], axis=0, keepdims=True)
    wp[0] = ((nsum * gain_wide + shift_wide * inb) * factor).T.reshape(4, 4, 4, 8, C)
    wp[1] = (msum * (scale_wide * factor)).T.reshape(4, 4, 4, 8, C)
    r0 = [remote(wp.at[1 - core], wcore, 0, place.sibling(), rssend, rsrecv)]
    start(r0)

    def kgrad_step(n, carry):
        kernel_grad_tile(src, dcv, kacc, n // 8, lax.rem(n, 8))
        return carry

    lax.fori_loop(0, BLOCKS // 2, kgrad_step, 0)
    arrive(r0)
    for a in range(4):
        for b in range(4):
            yy, xx = a * (1 - core) + b * core, b * (1 - core) + a * core
            wa[a, :, b] = wp[core, yy, :, xx] + wcore[yy, :, xx]
    first, second = y * (1 - core) + x * core, x * (1 - core) + y * core
    r1, r2, r3 = [], [], []
    for off in range(1, 4):
        to = place.turn(y=off * (1 - core), x=off * core)[3]
        r1.append(remote(wa.at[lax.rem(first + off, 4)], wr1.at[off - 1], off, to, rssend, rsrecv))
        to = place.turn(y=off * core, x=off * (1 - core))[3]
        r2.append(remote(wb_.at[lax.rem(second + off, 4)], wr2.at[off - 1], 3 + off, to, rssend, rsrecv))
        zz, to = place.turn(z=off)[1::2]
        r3.append(remote(wc.at[zz], wr3.at[off - 1], 6 + off, to, rssend, rsrecv))
    r4 = [remote(wd, wr4, 10, place.sibling(), rssend, rsrecv)]
    start(r1)
    lax.fori_loop(BLOCKS // 2, BLOCKS, kgrad_step, 0)

    gain_g = jnp.sum(win * nsum, axis=1, keepdims=True)
    shift_g = jnp.sum(win * inb, axis=1, keepdims=True)
    scale_g = jnp.sum(wo_t * msum, axis=1, keepdims=True)
    for n in range(K * K):
        rows[n : n + 1, :] = jnp.sum(kacc[n], axis=0, keepdims=True)
    rows[K * K : K * K + 1, :] = jnp.sum(dbacc[...], axis=0, keepdims=True)
    rows[K * K + 1 : K * K + 2, :] = jnp.sum(cotacc[...], axis=0, keepdims=True)
    rows[K * K + 2 :, :] = jnp.zeros((128 - K * K - 2, C), f32)
    grads = rows[...].T
    lane = lanes(C, 128, 1)
    cot_wide = widen(grads[:, K * K + 1 : K * K + 2], 1)
    columns = [(GAIN, gain_g), (SHIFT, shift_g), (OB, scale_wide[:, 0:C] * cot_wide), (SCALE, scale_g + ob_wide * cot_wide)]
    for k in range(4):
        terms = [jnp.where(pick[k], inb[:, 128 * t : 128 * t + 128], 0.0) for t in range(4)]
        columns.append((IB + k, jnp.sum(jnp.concatenate(terms, axis=0), axis=1, keepdims=True)))
    for at, column in columns:
        grads = jnp.where(lane == at, column, grads)
    sp.reshape(128, C)[...] = grads * factor
    q1, q2, q3 = [], [], []
    for off in range(1, 8):
        g, to = place.in_plane(off)
        q1.append(remote(sp.at[:, :, g // 2, lax.rem(g, 2)], srx.at[off - 1], 10 + off, to, rssend, rsrecv))
    for off in range(1, 4):
        yy, _, _, to = place.turn(y=off)
        q2.append(remote(sb.at[yy], sry.at[off - 1], 17 + off, to, rssend, rsrecv))
        zz, to = place.turn(z=off)[1::2]
        q3.append(remote(sc.at[zz], srz.at[off - 1], 20 + off, to, rssend, rsrecv))
    start(q1)

    arrive(back[0:2])
    clear_columns(place, dcv)

    def out_step(n, carry):
        b, wb, at = column_block(n)
        acc = conv_tile(dcv, taps, b, wb, True, INNER, {p: cot[b, p, at, :] for p in range(H)})
        for p in range(H):
            fg[b, p, at, :] = acc[p]
        return carry

    def out_rest(n, carry):
        b, wb, at = column_block(n)
        acc = conv_tile(dcv, taps, b, wb, True, OUTER, {p: fg[b, p, at, :] for p in FRINGE})
        for p in FRINGE:
            fg[b, p, at, :] = acc[p]
        return carry

    lax.fori_loop(0, 6, out_step, 0)
    arrive(r1)
    for n in range(4):
        wb_[n] = wa[first, :, n] + wr1[0, :, n] + wr1[1, :, n] + wr1[2, :, n]
    start(r2)
    lax.fori_loop(6, 9, out_step, 0)
    arrive(q1)
    total = sp[:, :, x, core]
    for n in range(7):
        total = total + srx[n]
    sb[...] = total
    start(q2)
    lax.fori_loop(9, 13, out_step, 0)
    arrive(r2)
    wc[...] = wb_[second] + wr2[0] + wr2[1] + wr2[2]
    start(r3)
    arrive(q2)
    sc[...] = sb[y] + sry[0] + sry[1] + sry[2]
    start(q3)
    lax.fori_loop(13, BLOCKS, out_step, 0)
    arrive(back[2:])
    clear_rows(place, dcv)
    lax.fori_loop(0, BLOCKS, out_rest, 0)
    put = pltpu.make_async_copy(fg, fg_out, out_sem.at[0])
    put.start()

    leave(s1 + w1 + v1 + s2 + w2 + v2 + s3 + w3 + v3 + edges + back + r0 + r1 + r2 + q1 + q2)
    arrive(r3)
    wd[...] = wc[z] + wr3[0] + wr3[1] + wr3[2]
    start(r4)
    arrive(q3)
    small_out[...] = sc[z] + srz[0] + srz[1] + srz[2]
    arrive(r4)
    kept, got = wd[...], wr4[...]
    weight_out[core] = jnp.where(core == 0, kept[0:4], kept[4:8])
    weight_out[1 - core] = jnp.where(core == 0, got[0:4], got[4:8])

    put.wait()
    leave(r3 + r4 + q3)


def deliver(
    fg_in, small_in, weight_in,
    fg_out, taps_out, cb_out, gain_out, shift_out, win_out, ib_out, wout_out, ob_out, scale_out,
    buf, row, sem,
):
    pieces = [(b, pl.ds(h, H // 2)) for b in range(B) for h in range(0, H, H // 2)]
    small = pltpu.make_async_copy(small_in, row, sem.at[8])
    weights = [pltpu.make_async_copy(weight_in.at[k], ref, sem.at[9 + k]) for k, ref in enumerate((win_out, wout_out))]
    small.start()
    gets = [pltpu.make_async_copy(fg_in.at[at], buf.at[at], sem.at[n]) for n, at in enumerate(pieces)]
    puts = [pltpu.make_async_copy(buf.at[at], fg_out.at[at], sem.at[4 + n]) for n, at in enumerate(pieces)]
    for copy in gets + weights:
        copy.start()
    small.wait()
    for i in range(K):
        for j in range(K):
            taps_out[i, 0, j] = row[0, TAPS + i * K + j]
    for at, ref in ((CB, cb_out), (GAIN, gain_out), (SHIFT, shift_out), (OB, ob_out), (SCALE, scale_out)):
        ref[0] = row[0, at]
    for k in range(4):
        ib_out[k] = row[0, IB + k]
    for get, put in zip(gets, puts):
        get.wait()
        put.start()
    for copy in weights + puts:
        copy.wait()


def per_device(
    features, cotangent, conv_kernel, conv_bias, norm_gain, norm_shift,
    w_in, in_bias, w_out, out_bias, layer_scale,
):
    vmem = lambda *shape: pltpu.VMEM(shape, f32)
    smem = lambda *shape: pltpu.SMEM(shape, f32)
    half = lambda *shape: pltpu.VMEM(shape, bf16)
    dma = lambda n: pltpu.SemaphoreType.DMA((n,))
    out = lambda *shape: jax.ShapeDtypeStruct(shape, f32)
    anywhere = pl.BlockSpec(memory_space=pl.ANY)
    inside = pl.BlockSpec(memory_space=pltpu.VMEM)
    scalar = pl.BlockSpec(memory_space=pltpu.SMEM)
    tile = (B, H, W, C)
    fg, small, weights = pl.pallas_call(
        kernel,
        out_shape=(out(*tile), out(1, C), out(2, 4, C)),
        in_specs=[anywhere] * 11,
        out_specs=(anywhere, inside, inside),
        scratch_shapes=[
            smem(K, 1, K), smem(1), smem(1), smem(1), smem(1), smem(1), smem(4), vmem(1, C),
            vmem(B, HE, WE, C), vmem(*tile), vmem(B, HE, WE, C), vmem(*tile), vmem(*tile),
            vmem(4, 4, 4, 2, 1, C), vmem(2, 4, 4, 4, 2, 4, C), vmem(K * K, 8, C),
            half(2 * C, HID), half(C, HID), half(HID, 2 * C), half(2 * C, HID), half(C, HID), vmem(1, HID),
            vmem(C, HID), vmem(C, HID), vmem(8, HID), vmem(K * K, 8, C), vmem(8, C), vmem(8, C),
            vmem(2, 4, 4, 4, 8, C), vmem(4, 4, 4, 8, C), vmem(4, 4, 4, 8, C), vmem(3, 4, 4, 8, C),
            vmem(4, 4, 8, C), vmem(3, 4, 8, C), vmem(4, 8, C), vmem(3, 8, C), vmem(8, C), vmem(8, C),
            vmem(128, C), vmem(4, 4, 4, 2, 1, C), vmem(7, 4, 4, 1, C), vmem(4, 4, 1, C), vmem(3, 4, 1, C), vmem(4, 1, C), vmem(3, 1, C),
            dma(11), dma(1), dma(8), dma(8), dma(8), dma(8), dma(39), dma(39), dma(24), dma(24),
        ],
        compiler_params=pltpu.CompilerParams(
            collective_id=0, has_side_effects=True, vmem_limit_bytes=56 * 2**20
        ),
    )(
        features, cotangent, conv_kernel.transpose(0, 2, 1), conv_bias, norm_gain, norm_shift,
        out_bias, layer_scale, in_bias, w_in.T, w_out,
    )
    fg, taps_g, cb_g, gain_g, shift_g, win_g, ib_g, wout_g, ob_g, scale_g = pl.pallas_call(
        deliver,
        out_shape=(
            out(*tile), out(K, 1, K), out(1), out(1), out(1), out(4, C), out(4), out(4, C), out(1), out(1),
        ),
        in_specs=[anywhere] * 3,
        out_specs=(anywhere, scalar, scalar, scalar, scalar, inside, scalar, inside, scalar, scalar),
        scratch_shapes=[vmem(*tile), smem(1, C), dma(11)],
    )(fg, small, weights)
    return fg, taps_g.transpose(0, 2, 1), cb_g, gain_g, shift_g, win_g.T, ib_g, wout_g, ob_g, scale_g


def solution(mesh):
    both = ("row", "col")
    tile = P(None, "row", "col", None)
    taps, vector = P(None, None, both), P(both)
    return jax.shard_map(
        per_device,
        mesh=mesh,
        in_specs=(tile, tile, taps, vector, vector, vector, P(None, both), vector, P(both, None), vector, vector),
        out_specs=(tile, taps, vector, vector, vector, P(None, both), vector, P(both, None), vector, vector),
        check_vma=False,
    )
```

```python
import functools
import math

import jax
import jax.numpy as jnp
from jax import lax
from jax.experimental import pallas as pl
from jax.experimental.pallas import tpu as pltpu
from jax.sharding import PartitionSpec as P

norm_eps = 1e-06
inverse_root_two = 0.7071067811865476
inverse_root_twopi = 0.3989422804014327
MESH = pl.DeviceIdType.MESH
f32, bf16 = jnp.float32, jnp.bfloat16

K, R = 7, 3
C, HID = 128, 512
B, H, W = 2, 16, 64
LEFT = 8
WE = W + 2 * LEFT
HE = H + 2 * R
ROWS, COLS = 8, 16
QUARTER = H // 4
BLOCKS = B * W // 8
CUT = BLOCKS // 2 + 1
M = 2 * QUARTER * W
TAPS, CB, GAIN, SHIFT, OB, SCALE, IB = 0, 49, 50, 51, 52, 53, 54


def split(x):
    hi = x.astype(bf16)
    return hi, (x - hi.astype(f32)).astype(bf16)


def dot(a, b):
    return jnp.dot(a, b, preferred_element_type=f32)


def lanes(x, n, axis):
    return lax.broadcasted_iota(jnp.int32, (x, n), axis)


class Place:
    def __init__(self):
        self.row, self.col = lax.axis_index("row"), lax.axis_index("col")
        self.y = self.row // 2
        self.z = lax.rem(self.row, 2) * 2 + self.col // 8
        self.g = lax.rem(self.col, 8)
        self.x, self.core = self.g // 2, lax.rem(self.g, 2)

    def at(self, y, z, x, core):
        return (y * 2 + z // 2, lax.rem(z, 2) * 8 + x * 2 + core)

    def turn(self, y=0, z=0, x=0):
        y, z, x = lax.rem(self.y + y, 4), lax.rem(self.z + z, 4), lax.rem(self.x + x, 4)
        return y, z, x, self.at(y, z, x, self.core)

    def in_plane(self, off):
        other = lax.rem(self.g + off, 8)
        return other, self.at(self.y, self.z, other // 2, lax.rem(other, 2))

    def in_column(self, off):
        other = lax.rem(self.z * 2 + self.core + off, 8)
        return other // 2, self.at(self.y, other // 2, self.x, lax.rem(other, 2))

    def in_wall(self, off):
        y, z = lax.rem(self.y + off // 4, 4), lax.rem(self.z + off % 4, 4)
        return y, z, self.at(y, z, self.x, self.core)

    def sibling(self):
        return self.at(self.y, self.z, self.x, 1 - self.core)

    def neighbour(self, dr, dc):
        return (lax.rem(self.row + dr + ROWS, ROWS), lax.rem(self.col + dc + COLS, COLS))


STEPS = [(0, -1), (0, 1), (-1, 0), (1, 0), (-1, -1), (-1, 1), (1, -1), (1, 1)]


def rows_of(step, base, sent):
    if step == 0:
        return pl.ds(base, H)
    if sent:
        return pl.ds(base, R) if step < 0 else pl.ds(base + H - R, R)
    return pl.ds(R + H, R) if step < 0 else pl.ds(0, R)


def cols_of(step, base, sent):
    if step == 0:
        return pl.ds(base, W)
    if sent:
        return pl.ds(base, LEFT) if step < 0 else pl.ds(base + W - LEFT, LEFT)
    return pl.ds(LEFT + W, LEFT) if step < 0 else pl.ds(0, LEFT)


def edge_ends(place, src, row0, col0, ext):
    return [
        (
            src.at[:, rows_of(dr, row0, True), cols_of(dc, col0, True), :],
            ext.at[:, rows_of(dr, R, False), cols_of(dc, LEFT, False), :],
            place.neighbour(dr, dc),
        )
        for dr, dc in STEPS
    ]


def clear_columns(place, ext):
    @pl.when(place.col == 0)
    def _():
        ext[:, R : R + H, 0:LEFT] = jnp.zeros((B, H, LEFT, C), f32)

    @pl.when(place.col == COLS - 1)
    def _():
        ext[:, R : R + H, LEFT + W :] = jnp.zeros((B, H, LEFT, C), f32)


def clear_rows(place, ext):
    for edge, at in ((0, slice(0, R)), (ROWS - 1, slice(R + H, HE))):

        @pl.when(place.row == edge)
        def _():
            ext[:, at] = jnp.zeros((B, R, WE, C), f32)

        @pl.when(place.col == 0)
        def _():
            ext[:, at, 0:LEFT] = jnp.zeros((B, R, LEFT, C), f32)

        @pl.when(place.col == COLS - 1)
        def _():
            ext[:, at, LEFT + W :] = jnp.zeros((B, R, LEFT, C), f32)


def conv_tile(ext, taps, b, wb, flip, rows, acc):
    for j in range(K):
        tap = [taps[(K - 1 - i) * K + K - 1 - j] if flip else taps[i * K + j] for i in range(K)]
        for e in rows:
            x = ext[b, e, pl.ds(8 * wb + LEFT - R + j, 8), :]
            for i in range(K):
                p = e - i
                if 0 <= p < H:
                    acc[p] = acc[p] + tap[i] * x
    return acc


INNER = range(R, R + H)
OUTER = (*range(R), *range(R + H, HE))
FRINGE = (*range(R), *range(H - R, H))


def kernel_grad_tile(ext, dcv, kacc, b, wb):
    grads = [dcv[b, R + p, pl.ds(pl.multiple_of(8 * wb + LEFT, 8), 8), :] for p in range(H)]
    for j in range(K):
        acc = [kacc[i * K + j] for i in range(K)]
        for e in range(HE):
            x = ext[b, e, pl.ds(8 * wb + LEFT - R + j, 8), :]
            for i in range(K):
                p = e - i
                if 0 <= p < H:
                    acc[i] = acc[i] + grads[p] * x
        for i in range(K):
            kacc[i * K + j] = acc[i]


def widen(column, n):
    one = jnp.broadcast_to(column, (column.shape[0], 128))
    return jnp.concatenate([one] * n, axis=1)


def kernel(
    feat, cot_hbm, taps_in, cb_in, gain_in, shift_in, ob_in, scale_in, ib_in, win_in, wout_in,
    fg_out, small_out, weight_out,
    taps_s, cb_s, gain_s, shift_s, ob_s, scale_s, ib_s, srow,
    src, cot, dcv, mid, fg, sg, wg, taps,
    win2, winlo, wintop, wot2, wotlo, bias_eff,
    nacc, macc, inbacc, kacc, cotacc, dbacc,
    wp, wcore, wa, wr1, wb_, wr2, wc, wr3, rows, sp, srx, sb, sry,
    local, out_sem, sent, arrived,
):
    place = Place()
    y, z, x, core = place.y, place.z, place.x, place.core

    scalars = [(taps_in, taps_s), (cb_in, cb_s), (gain_in, gain_s), (shift_in, shift_s), (ob_in, ob_s), (scale_in, scale_s), (ib_in, ib_s)]
    params = [pltpu.make_async_copy(a, b, local.at[4 + n]) for n, (a, b) in enumerate(scalars)]
    own = [
        pltpu.make_async_copy(feat, src.at[:, pl.ds(R, H), pl.ds(LEFT, W), :], local.at[0]),
        pltpu.make_async_copy(cot_hbm, cot, local.at[1]),
        pltpu.make_async_copy(win_in, wg.at[0, y, z, x, core], local.at[2]),
        pltpu.make_async_copy(wout_in, wg.at[1, y, z, x, core], local.at[3]),
    ]
    for copy in params + own:
        copy.start()

    barrier = pltpu.get_barrier_semaphore()
    partners = [place.neighbour(dr, dc) for dr, dc in STEPS]
    partners += [place.in_plane(off)[1] for off in range(1, 8)]
    partners += [place.in_column(off)[1] for off in range(1, 8)]
    partners += [place.in_wall(off)[2] for off in range(1, 16)]
    for partner in partners:
        pl.semaphore_signal(barrier, inc=1, device_id=partner, device_id_type=MESH)

    for copy in params:
        copy.wait()
    lane = lanes(1, 128, 1)
    row = jnp.zeros((1, 128), f32)
    for i in range(K):
        for j in range(K):
            row = jnp.where(lane == TAPS + i * K + j, taps_s[i, 0, j], row)
    for at, ref in ((CB, cb_s), (GAIN, gain_s), (SHIFT, shift_s), (OB, ob_s), (SCALE, scale_s)):
        row = jnp.where(lane == at, ref[0], row)
    for k in range(4):
        row = jnp.where(lane == IB + k, ib_s[k], row)
    srow[...] = row
    sg[y, z, x, core] = row
    kacc[...] = jnp.zeros_like(kacc)
    nacc[...] = jnp.zeros_like(nacc)
    macc[...] = jnp.zeros_like(macc)
    inbacc[...] = jnp.zeros_like(inbacc)
    cotacc[...] = jnp.zeros_like(cotacc)
    dbacc[...] = jnp.zeros_like(dbacc)

    pl.semaphore_wait(barrier, len(partners))

    stages = []

    class Stage:
        def __init__(self, amount, copies):
            self.n = len(stages)
            stages.append(self)
            self.amount = amount
            self.copies = [self.copy(*ends) for ends in copies]

        def copy(self, a, b, partner):
            return pltpu.make_async_remote_copy(
                src_ref=a, dst_ref=b, send_sem=sent.at[self.n], recv_sem=arrived.at[self.n],
                device_id=partner, device_id_type=MESH,
            )

        def start(self):
            for copy in self.copies:
                copy.start()

        def arrive(self):
            self.copy(self.amount, self.amount, place.sibling()).wait_recv()

        def leave(self):
            self.copy(self.amount, self.amount, place.sibling()).wait_send()

    cell = (y, z, x, core)
    plane = [place.in_plane(off)[1] for off in range(1, 8)]
    column = [place.in_column(off)[1] for off in range(1, 8)]
    wall = [place.in_wall(off)[2] for off in range(1, 16)]
    xs = [place.turn(x=off)[3] for off in range(1, 4)]
    ys = [place.turn(y=off)[3] for off in range(1, 4)]
    cells = wg.at[0].reshape(128, 4, C)
    s1 = Stage(srx.at[:, 0, 0], [(srow, sg.at[cell], p) for p in plane])
    w1 = Stage(cells.at[pl.ds(0, 7)], [(win_in, wg.at[(0, *cell)], p) for p in column])
    v1 = Stage(cells.at[pl.ds(0, 7)], [(wout_in, wg.at[(1, *cell)], p) for p in column])
    s2 = Stage(sg.reshape(128, 1, C).at[pl.ds(0, 120)], [(sg.at[y, z], sg.at[y, z], p) for p in wall])
    w2 = Stage(cells.at[pl.ds(0, 24)], [(wg.at[0, y, :, x], wg.at[0, y, :, x], p) for p in xs])
    v2 = Stage(cells.at[pl.ds(0, 24)], [(wg.at[1, y, :, x], wg.at[1, y, :, x], p) for p in ys])
    w3 = Stage(cells.at[pl.ds(0, 96)], [(wg.at[0, y], wg.at[0, y], p) for p in ys])
    v3 = Stage(cells.at[pl.ds(0, 96)], [(wg.at[1, :, :, x], wg.at[1, :, :, x], p) for p in xs])
    edges = edge_ends(place, feat, 0, 0, src)
    side = Stage(src.at[:, pl.ds(0, H), pl.ds(0, 2 * LEFT), :], edges[0:2])
    ends = Stage(src.at[:, pl.ds(0, 2 * R), :, :], edges[2:])

    s1.start()
    w1.start()
    v1.start()
    side.start()
    own[2].wait()
    own[3].wait()
    s1.arrive()
    s2.start()
    w1.arrive()
    w2.start()
    v1.arrive()
    v2.start()
    ends.start()
    w2.arrive()
    w3.start()
    v2.arrive()
    v3.start()
    own[0].wait()
    own[1].wait()
    side.arrive()
    clear_columns(place, src)
    s2.arrive()

    small = sg.reshape(128, C)[...]
    small_t = small.T
    for n in range(K * K):
        taps[n] = jnp.broadcast_to(small_t[TAPS + n : TAPS + n + 1, :], (8, C))
    conv_bias = jnp.broadcast_to(small_t[CB : CB + 1, :], (8, C))

    def column_block(n):
        return n // 8, lax.rem(n, 8), pl.ds(pl.multiple_of(lax.rem(n, 8) * 8, 8), 8)

    def conv_step(n, carry):
        b, wb, at = column_block(n)
        acc = conv_tile(src, taps, b, wb, False, INNER, {p: conv_bias for p in range(H)})
        for p in range(H):
            mid[b, p, at, :] = acc[p]
        return carry

    lax.fori_loop(0, BLOCKS, conv_step, 0)

    def conv_rest(n, carry):
        b, wb, at = column_block(n)
        acc = conv_tile(src, taps, b, wb, False, OUTER, {p: mid[b, p, at, :] for p in FRINGE})
        for p in FRINGE:
            mid[b, p, at, :] = acc[p]
        return carry

    w3.arrive()
    v3.arrive()
    gain_wide, shift_wide = widen(small[:, GAIN : GAIN + 1], 4), widen(small[:, SHIFT : SHIFT + 1], 4)
    scale_wide, ob_wide = widen(small[:, SCALE : SCALE + 1], 4), widen(small[:, OB : OB + 1], 1)
    win_t = wg.at[0].reshape(HID, C)[...]
    win = win_t.T
    wo_t = wg.at[1].reshape(HID, C)[...].T
    hi, lo = split(win * gain_wide)
    win2[0:C, :] = hi
    win2[C:, :] = hi
    winlo[...] = lo
    hi, lo = split(win_t * small_t[GAIN : GAIN + 1, :])
    wintop[:, 0:C] = hi
    wintop[:, C:] = lo
    hi, lo = split(wo_t * scale_wide)
    wot2[0:C, :] = hi
    wot2[C:, :] = hi
    wotlo[...] = lo
    pick = [lanes(32, 128, 1) == 4 * lanes(32, 128, 0) + k for k in range(4)]
    shifted = win * shift_wide
    for t in range(4):
        cut, band = slice(128 * t, 128 * t + 128), slice(32 * t, 32 * t + 32)
        terms = [jnp.where(pick[k], small[band, IB + k : IB + k + 1], 0.0) for k in range(4)]
        bias_eff[:, cut] = jnp.sum(shifted[:, cut], axis=0, keepdims=True) + jnp.sum(sum(terms), axis=0, keepdims=True)

    def mix(b, starts):
        spans = [pl.ds(p, QUARTER) for p in starts]
        x = jnp.concatenate([mid[b, s].reshape(M // 2, C) for s in spans], axis=0)
        ct = jnp.concatenate([cot[b, s].reshape(M // 2, C) for s in spans], axis=0)
        mean = jnp.mean(x, axis=-1, keepdims=True)
        cen = x - mean
        inv = lax.rsqrt(jnp.mean(cen * cen, axis=-1, keepdims=True) + norm_eps)
        normed = cen * inv
        n_hi, n_lo = split(normed)
        n2 = jnp.concatenate([n_hi, n_lo], axis=1)
        c_hi, c_lo = split(ct)
        c2 = jnp.concatenate([c_hi, c_lo], axis=1)
        nt2 = jnp.concatenate(split(normed.T), axis=0)
        ct2 = jnp.concatenate(split(ct.T), axis=0)
        cotacc[...] += jnp.sum(ct.reshape(M // 8, 8, C), axis=0)
        dn = jnp.zeros((M, C), f32)
        step = 256
        for h in range(0, HID, step):
            cut = slice(h, h + step)
            act = dot(n2, win2[:, cut]) + dot(n_hi, winlo[:, cut]) + bias_eff[:, cut]
            dh = dot(c2, wot2[:, cut]) + dot(c_hi, wotlo[:, cut])
            phi = 0.5 * (1.0 + lax.erf(act * inverse_root_two))
            slope = phi + act * jnp.exp(-0.5 * act * act) * inverse_root_twopi
            hid_hi, hid_lo = split(act * phi)
            da = dh * slope
            inbacc[:, cut] += jnp.sum(da.reshape(M // 8, 8, step), axis=0)
            da_hi, da_lo = split(da)
            both = dot(da_hi, wintop[cut, :])
            dn = dn + both[:, 0:C] + both[:, C:] + dot(da_lo, wintop[cut, 0:C])
            both = dot(nt2, da_hi)
            nacc[:, cut] += both[0:C] + both[C:] + dot(nt2[0:C], da_lo)
            both = dot(ct2, hid_hi)
            macc[:, cut] += both[0:C] + both[C:] + dot(ct2[0:C], hid_lo)
        dc = inv * (
            dn
            - jnp.mean(dn, axis=-1, keepdims=True)
            - normed * jnp.mean(dn * normed, axis=-1, keepdims=True)
        )
        dbacc[...] += jnp.sum(dc.reshape(M // 8, 8, C), axis=0)
        for n, p in enumerate(starts):
            part = dc[n * (M // 2) : (n + 1) * (M // 2)]
            dcv[b, pl.ds(R + p, QUARTER), LEFT : LEFT + W, :] = part.reshape(QUARTER, W, C)

    back = edge_ends(place, dcv, R, LEFT, dcv)
    back_side = Stage(src.at[:, pl.ds(0, H), pl.ds(0, 2 * LEFT), :], back[0:2])
    back_ends = Stage(src.at[:, pl.ds(0, 2 * R), :, :], back[2:])

    def mix_step(n, carry):
        outer = lax.rem((n + 1) // 2, 2)

        @pl.when(n == 1)
        def _():
            ends.arrive()
            clear_rows(place, src)
            lax.fori_loop(0, BLOCKS, conv_rest, 0)

        @pl.when(n == 3)
        def _():
            back_ends.start()

        mix(n // 2, (QUARTER * (1 - outer), QUARTER * (2 + outer)))
        return carry

    lax.fori_loop(0, 4, mix_step, 0)
    back_side.start()

    factor = 1.0 / math.sqrt(B * H * W * ROWS * COLS)
    nsum, msum = nacc[...], macc[...]
    inb = jnp.sum(inbacc[...], axis=0, keepdims=True)
    wp[0] = ((nsum * gain_wide + shift_wide * inb) * factor).T.reshape(4, 4, 4, 8, C)
    wp[1] = (msum * (scale_wide * factor)).T.reshape(4, 4, 4, 8, C)
    r0 = Stage(wcore, [(wp.at[1 - core], wcore, place.sibling())])
    r0.start()

    def kgrad_step(n, carry):
        kernel_grad_tile(src, dcv, kacc, n // 8, lax.rem(n, 8))
        return carry

    lax.fori_loop(0, CUT, kgrad_step, 0)
    r0.arrive()
    for a in range(4):
        for b in range(4):
            yy, xx = a * (1 - core) + b * core, b * (1 - core) + a * core
            wa[a, :, b] = wp[core, yy, :, xx] + wcore[yy, :, xx]
    first, second = y * (1 - core) + x * core, x * (1 - core) + y * core
    to1 = [place.turn(y=off * (1 - core), x=off * core)[3] for off in range(1, 4)]
    to2 = [place.turn(y=off * core, x=off * (1 - core))[3] for off in range(1, 4)]
    to3 = [place.in_column(off) for off in range(1, 8)]
    r1 = Stage(wr1, [(wa.at[lax.rem(first + 1 + n, 4)], wr1.at[n], p) for n, p in enumerate(to1)])
    r2 = Stage(wr2, [(wb_.at[lax.rem(second + 1 + n, 4)], wr2.at[n], p) for n, p in enumerate(to2)])
    r3 = Stage(wr3.reshape(8, 8, C).at[pl.ds(0, 7)], [(wc.at[zz], wr3.at[core, z], p) for zz, p in to3])
    r1.start()
    lax.fori_loop(CUT, BLOCKS, kgrad_step, 0)

    gain_g = jnp.sum(win * nsum, axis=1, keepdims=True)
    shift_g = jnp.sum(win * inb, axis=1, keepdims=True)
    scale_g = jnp.sum(wo_t * msum, axis=1, keepdims=True)
    for n in range(K * K):
        rows[n : n + 1, :] = jnp.sum(kacc[n], axis=0, keepdims=True)
    rows[K * K : K * K + 1, :] = jnp.sum(dbacc[...], axis=0, keepdims=True)
    rows[K * K + 1 : K * K + 2, :] = jnp.sum(cotacc[...], axis=0, keepdims=True)
    rows[K * K + 2 :, :] = jnp.zeros((128 - K * K - 2, C), f32)
    grads = rows[...].T
    lane = lanes(C, 128, 1)
    cot_wide = widen(grads[:, K * K + 1 : K * K + 2], 1)
    columns = [(GAIN, gain_g), (SHIFT, shift_g), (OB, scale_wide[:, 0:C] * cot_wide), (SCALE, scale_g + ob_wide * cot_wide)]
    for k in range(4):
        terms = [jnp.where(pick[k], inb[:, 128 * t : 128 * t + 128], 0.0) for t in range(4)]
        columns.append((IB + k, jnp.sum(jnp.concatenate(terms, axis=0), axis=1, keepdims=True)))
    for at, column in columns:
        grads = jnp.where(lane == at, column, grads)
    sp.reshape(128, C)[...] = grads * factor
    q1, q2 = [], []
    for off in range(1, 8):
        g, to = place.in_plane(off)
        q1.append((sp.at[:, :, g // 2, lax.rem(g, 2)], srx.at[off - 1], to))
    for off in range(1, 16):
        yy, zz, to = place.in_wall(off)
        q2.append((sb.at[yy, zz], sry.at[off - 1], to))
    q1, q2 = Stage(srx, q1), Stage(sry, q2)
    q1.start()

    back_side.arrive()
    clear_columns(place, dcv)

    def out_step(n, carry):
        b, wb, at = column_block(n)
        acc = conv_tile(dcv, taps, b, wb, True, INNER, {p: cot[b, p, at, :] for p in range(H)})
        for p in range(H):
            fg[b, p, at, :] = acc[p]
        return carry

    def out_rest(n, carry):
        b, wb, at = column_block(n)
        acc = conv_tile(dcv, taps, b, wb, True, OUTER, {p: fg[b, p, at, :] for p in FRINGE})
        for p in FRINGE:
            fg[b, p, at, :] = acc[p]
        return carry

    lax.fori_loop(0, 5, out_step, 0)
    r1.arrive()
    for n in range(4):
        wb_[n] = wa[first, :, n] + wr1[0, :, n] + wr1[1, :, n] + wr1[2, :, n]
    r2.start()
    lax.fori_loop(5, 8, out_step, 0)
    q1.arrive()
    total = sp[:, :, x, core]
    for n in range(7):
        total = total + srx[n]
    sb[...] = total
    q2.start()
    lax.fori_loop(8, 13, out_step, 0)
    r2.arrive()
    wc[...] = wb_[second] + wr2[0] + wr2[1] + wr2[2]
    r3.start()
    wr3[core, z] = wc[z]
    lax.fori_loop(13, BLOCKS, out_step, 0)
    back_ends.arrive()
    clear_rows(place, dcv)
    lax.fori_loop(0, BLOCKS, out_rest, 0)
    put = pltpu.make_async_copy(fg, fg_out, out_sem.at[0])
    put.start()

    for stage in stages:
        if stage not in (r3, q2):
            stage.leave()
    q2.arrive()
    total = sb[y, z]
    for n in range(15):
        total = total + sry[n]
    small_out[...] = total
    r3.arrive()
    for kind in range(2):
        total = wr3[kind, 0] + wr3[kind, 1] + wr3[kind, 2] + wr3[kind, 3]
        weight_out[kind] = jnp.where(core == 0, total[0:4], total[4:8])

    put.wait()
    r3.leave()
    q2.leave()


def deliver(
    fg_in, small_in, weight_in,
    fg_out, taps_out, cb_out, gain_out, shift_out, win_out, ib_out, wout_out, ob_out, scale_out,
    buf, row, weights, taps, cb, gain, shift, ib, ob, scale, sem,
):
    pieces = [(b, pl.ds(h, H // 2)) for b in range(B) for h in range(0, H, H // 2)]
    small = pltpu.make_async_copy(small_in, row, sem.at[8])
    weight = pltpu.make_async_copy(weight_in, weights, sem.at[9])
    gets = [pltpu.make_async_copy(fg_in.at[at], buf.at[at], sem.at[n]) for n, at in enumerate(pieces)]
    puts = [pltpu.make_async_copy(buf.at[at], fg_out.at[at], sem.at[4 + n]) for n, at in enumerate(pieces)]
    for copy in [small, weight] + gets:
        copy.start()
    small.wait()
    for i in range(K):
        for j in range(K):
            taps[i, 0, j] = row[0, TAPS + i * K + j]
    for at, ref in ((CB, cb), (GAIN, gain), (SHIFT, shift), (OB, ob), (SCALE, scale)):
        ref[0] = row[0, at]
    for k in range(4):
        ib[k] = row[0, IB + k]
    ends = [
        (taps, taps_out), (cb, cb_out), (gain, gain_out), (shift, shift_out), (ob, ob_out), (scale, scale_out),
        (ib, ib_out), (weights.at[0], win_out), (weights.at[1], wout_out),
    ]
    weight.wait()
    rest = [pltpu.make_async_copy(a, b, sem.at[10 + n]) for n, (a, b) in enumerate(ends)]
    for copy in rest:
        copy.start()
    for get, put in zip(gets, puts):
        get.wait()
        put.start()
    for copy in rest + puts:
        copy.wait()


def per_device(
    features, cotangent, conv_kernel, conv_bias, norm_gain, norm_shift,
    w_in, in_bias, w_out, out_bias, layer_scale,
):
    vmem = lambda *shape: pltpu.VMEM(shape, f32)
    smem = lambda *shape: pltpu.SMEM(shape, f32)
    half = lambda *shape: pltpu.VMEM(shape, bf16)
    dma = lambda n: pltpu.SemaphoreType.DMA((n,))
    out = lambda *shape: jax.ShapeDtypeStruct(shape, f32)
    anywhere = pl.BlockSpec(memory_space=pl.ANY)
    inside = pl.BlockSpec(memory_space=pltpu.VMEM)
    tile = (B, H, W, C)
    fg, small, weights = pl.pallas_call(
        kernel,
        out_shape=(out(*tile), out(1, C), out(2, 4, C)),
        in_specs=[anywhere] * 11,
        out_specs=(anywhere, inside, inside),
        scratch_shapes=[
            smem(K, 1, K), smem(1), smem(1), smem(1), smem(1), smem(1), smem(4), vmem(1, C),
            vmem(B, HE, WE, C), vmem(*tile), vmem(B, HE, WE, C), vmem(*tile), vmem(*tile),
            vmem(4, 4, 4, 2, 1, C), vmem(2, 4, 4, 4, 2, 4, C), vmem(K * K, 8, C),
            half(2 * C, HID), half(C, HID), half(HID, 2 * C), half(2 * C, HID), half(C, HID), vmem(1, HID),
            vmem(C, HID), vmem(C, HID), vmem(8, HID), vmem(K * K, 8, C), vmem(8, C), vmem(8, C),
            vmem(2, 4, 4, 4, 8, C), vmem(4, 4, 4, 8, C), vmem(4, 4, 4, 8, C), vmem(3, 4, 4, 8, C),
            vmem(4, 4, 8, C), vmem(3, 4, 8, C), vmem(4, 8, C), vmem(2, 4, 8, C),
            vmem(128, C), vmem(4, 4, 4, 2, 1, C), vmem(7, 4, 4, 1, C), vmem(4, 4, 1, C), vmem(15, 1, C),
            dma(11), dma(1), dma(18), dma(18),
        ],
        compiler_params=pltpu.CompilerParams(
            collective_id=0, has_side_effects=True, vmem_limit_bytes=56 * 2**20
        ),
    )(
        features, cotangent, conv_kernel.transpose(0, 2, 1), conv_bias, norm_gain, norm_shift,
        out_bias, layer_scale, in_bias, w_in.T, w_out,
    )
    fg, taps_g, cb_g, gain_g, shift_g, win_g, ib_g, wout_g, ob_g, scale_g = pl.pallas_call(
        deliver,
        out_shape=(
            out(*tile), out(K, 1, K), out(1), out(1), out(1), out(4, C), out(4), out(4, C), out(1), out(1),
        ),
        in_specs=[anywhere] * 3,
        out_specs=(anywhere,) * 10,
        scratch_shapes=[
            vmem(*tile), smem(1, C), vmem(2, 4, C), smem(K, 1, K), smem(1), smem(1), smem(1), smem(4), smem(1), smem(1), dma(19),
        ],
    )(fg, small, weights)
    return fg, taps_g.transpose(0, 2, 1), cb_g, gain_g, shift_g, win_g.T, ib_g, wout_g, ob_g, scale_g


def solution(mesh):
    both = ("row", "col")
    tile = P(None, "row", "col", None)
    taps, vector = P(None, None, both), P(both)
    return jax.shard_map(
        per_device,
        mesh=mesh,
        in_specs=(tile, tile, taps, vector, vector, vector, P(None, both), vector, P(both, None), vector, vector),
        out_specs=(tile, taps, vector, vector, vector, P(None, both), vector, P(both, None), vector, vector),
        check_vma=False,
    )
```

```python
import functools
import math

import jax
import jax.numpy as jnp
from jax import lax
from jax.experimental import pallas as pl
from jax.experimental.pallas import tpu as pltpu
from jax.sharding import PartitionSpec as P

norm_eps = 1e-06
inverse_root_two = 0.7071067811865476
inverse_root_twopi = 0.3989422804014327
MESH = pl.DeviceIdType.MESH
f32, bf16 = jnp.float32, jnp.bfloat16

K, R = 7, 3
C, HID = 128, 512
B, H, W = 2, 16, 64
LEFT = 8
WE = W + 2 * LEFT
HE = H + 2 * R
ROWS, COLS = 8, 16
QUARTER = H // 4
BLOCKS = B * W // 8
CUT = BLOCKS // 2 + 1
M = 2 * QUARTER * W
TAPS, CB, GAIN, SHIFT, OB, SCALE, IB = 0, 49, 50, 51, 52, 53, 54


def split(x):
    hi = x.astype(bf16)
    return hi, (x - hi.astype(f32)).astype(bf16)


def dot(a, b):
    return jnp.dot(a, b, preferred_element_type=f32)


def lanes(x, n, axis):
    return lax.broadcasted_iota(jnp.int32, (x, n), axis)


class Place:
    def __init__(self):
        self.row, self.col = lax.axis_index("row"), lax.axis_index("col")
        self.y = self.row // 2
        self.z = lax.rem(self.row, 2) * 2 + self.col // 8
        self.g = lax.rem(self.col, 8)
        self.x, self.core = self.g // 2, lax.rem(self.g, 2)

    def at(self, y, z, x, core):
        return (y * 2 + z // 2, lax.rem(z, 2) * 8 + x * 2 + core)

    def turn(self, y=0, z=0, x=0):
        y, z, x = lax.rem(self.y + y, 4), lax.rem(self.z + z, 4), lax.rem(self.x + x, 4)
        return y, z, x, self.at(y, z, x, self.core)

    def in_plane(self, off):
        other = lax.rem(self.g + off, 8)
        return other, self.at(self.y, self.z, other // 2, lax.rem(other, 2))

    def in_column(self, off):
        other = lax.rem(self.z * 2 + self.core + off, 8)
        return other // 2, self.at(self.y, other // 2, self.x, lax.rem(other, 2))

    def in_wall(self, off):
        y, z = lax.rem(self.y + off // 4, 4), lax.rem(self.z + off % 4, 4)
        return y, z, self.at(y, z, self.x, self.core)

    def sibling(self):
        return self.at(self.y, self.z, self.x, 1 - self.core)

    def neighbour(self, dr, dc):
        return (lax.rem(self.row + dr + ROWS, ROWS), lax.rem(self.col + dc + COLS, COLS))


STEPS = [(0, -1), (0, 1), (-1, 0), (1, 0), (-1, -1), (-1, 1), (1, -1), (1, 1)]


def rows_of(step, base, sent):
    if step == 0:
        return pl.ds(base, H)
    if sent:
        return pl.ds(base, R) if step < 0 else pl.ds(base + H - R, R)
    return pl.ds(R + H, R) if step < 0 else pl.ds(0, R)


def cols_of(step, base, sent):
    if step == 0:
        return pl.ds(base, W)
    if sent:
        return pl.ds(base, LEFT) if step < 0 else pl.ds(base + W - LEFT, LEFT)
    return pl.ds(LEFT + W, LEFT) if step < 0 else pl.ds(0, LEFT)


def edge_ends(place, src, row0, col0, ext):
    return [
        (
            src.at[rows_of(dr, row0, True), cols_of(dc, col0, True), :],
            ext.at[rows_of(dr, R, False), cols_of(dc, LEFT, False), :],
            place.neighbour(dr, dc),
        )
        for dr, dc in STEPS
    ]


def clear_columns(place, ext):
    @pl.when(place.col == 0)
    def _():
        ext[:, R : R + H, 0:LEFT] = jnp.zeros((B, H, LEFT, C), f32)

    @pl.when(place.col == COLS - 1)
    def _():
        ext[:, R : R + H, LEFT + W :] = jnp.zeros((B, H, LEFT, C), f32)


def clear_rows(place, ext):
    for edge, at in ((0, slice(0, R)), (ROWS - 1, slice(R + H, HE))):

        @pl.when(place.row == edge)
        def _():
            ext[:, at] = jnp.zeros((B, R, WE, C), f32)

        @pl.when(place.col == 0)
        def _():
            ext[:, at, 0:LEFT] = jnp.zeros((B, R, LEFT, C), f32)

        @pl.when(place.col == COLS - 1)
        def _():
            ext[:, at, LEFT + W :] = jnp.zeros((B, R, LEFT, C), f32)


def conv_tile(ext, taps, b, wb, flip, rows, acc):
    for j in range(K):
        tap = [taps[(K - 1 - i) * K + K - 1 - j] if flip else taps[i * K + j] for i in range(K)]
        for e in rows:
            x = ext[b, e, pl.ds(8 * wb + LEFT - R + j, 8), :]
            for i in range(K):
                p = e - i
                if 0 <= p < H:
                    acc[p] = acc[p] + tap[i] * x
    return acc


INNER = range(R, R + H)
OUTER = (*range(R), *range(R + H, HE))
FRINGE = (*range(R), *range(H - R, H))


def kernel_grad_tile(ext, dcv, kacc, b, wb):
    grads = [dcv[b, R + p, pl.ds(pl.multiple_of(8 * wb + LEFT, 8), 8), :] for p in range(H)]
    for j in range(K):
        acc = [kacc[i * K + j] for i in range(K)]
        for e in range(HE):
            x = ext[b, e, pl.ds(8 * wb + LEFT - R + j, 8), :]
            for i in range(K):
                p = e - i
                if 0 <= p < H:
                    acc[i] = acc[i] + grads[p] * x
        for i in range(K):
            kacc[i * K + j] = acc[i]


def widen(column, n):
    one = jnp.broadcast_to(column, (column.shape[0], 128))
    return jnp.concatenate([one] * n, axis=1)


def kernel(
    feat, cot_hbm, taps_in, cb_in, gain_in, shift_in, ob_in, scale_in, ib_in, win_in, wout_in,
    fg_out, small_out, weight_out,
    taps_s, cb_s, gain_s, shift_s, ob_s, scale_s, ib_s, srow,
    src, cot, dcv, mid, fg, sg, wg, taps,
    win2, winlo, wintop, wot2, wotlo, bias_eff,
    nacc, macc, inbacc, kacc, cotacc, dbacc,
    wp, wcore, wa, wr1, wb_, wr2, wc, wr3, rows, sp, srx, sb, sry,
    local, out_sem, sent, arrived,
):
    place = Place()
    y, z, x, core = place.y, place.z, place.x, place.core

    scalars = [(taps_in, taps_s), (cb_in, cb_s), (gain_in, gain_s), (shift_in, shift_s), (ob_in, ob_s), (scale_in, scale_s), (ib_in, ib_s)]
    params = [pltpu.make_async_copy(a, b, local.at[4 + n]) for n, (a, b) in enumerate(scalars)]
    own = [
        pltpu.make_async_copy(feat, src.at[:, pl.ds(R, H), pl.ds(LEFT, W), :], local.at[0]),
        pltpu.make_async_copy(cot_hbm, cot, local.at[1]),
        pltpu.make_async_copy(win_in, wg.at[0, y, z, x, core], local.at[2]),
        pltpu.make_async_copy(wout_in, wg.at[1, y, z, x, core], local.at[3]),
    ]
    for copy in params + own:
        copy.start()

    barrier = pltpu.get_barrier_semaphore()
    partners = [place.neighbour(dr, dc) for dr, dc in STEPS]
    partners += [place.in_plane(off)[1] for off in range(1, 8)]
    partners += [place.in_column(off)[1] for off in range(1, 8)]
    partners += [place.in_wall(off)[2] for off in range(1, 16)]
    for partner in partners:
        pl.semaphore_signal(barrier, inc=1, device_id=partner, device_id_type=MESH)

    for copy in params:
        copy.wait()
    lane = lanes(1, 128, 1)
    row = jnp.zeros((1, 128), f32)
    for i in range(K):
        for j in range(K):
            row = jnp.where(lane == TAPS + i * K + j, taps_s[i, 0, j], row)
    for at, ref in ((CB, cb_s), (GAIN, gain_s), (SHIFT, shift_s), (OB, ob_s), (SCALE, scale_s)):
        row = jnp.where(lane == at, ref[0], row)
    for k in range(4):
        row = jnp.where(lane == IB + k, ib_s[k], row)
    srow[...] = row
    sg[y, z, x, core] = row
    kacc[...] = jnp.zeros_like(kacc)
    nacc[...] = jnp.zeros_like(nacc)
    macc[...] = jnp.zeros_like(macc)
    inbacc[...] = jnp.zeros_like(inbacc)
    cotacc[...] = jnp.zeros_like(cotacc)
    dbacc[...] = jnp.zeros_like(dbacc)

    pl.semaphore_wait(barrier, len(partners))

    stages = []

    class Stage:
        def __init__(self, amount, copies):
            self.n = len(stages)
            stages.append(self)
            self.amount = amount
            self.copies = [self.copy(*ends) for ends in copies]

        def copy(self, a, b, partner):
            return pltpu.make_async_remote_copy(
                src_ref=a, dst_ref=b, send_sem=sent.at[self.n], recv_sem=arrived.at[self.n],
                device_id=partner, device_id_type=MESH,
            )

        def start(self):
            for copy in self.copies:
                copy.start()

        def arrive(self):
            self.copy(self.amount, self.amount, place.sibling()).wait_recv()

        def leave(self):
            self.copy(self.amount, self.amount, place.sibling()).wait_send()

    cell = (y, z, x, core)
    plane = [place.in_plane(off)[1] for off in range(1, 8)]
    zs = [place.turn(z=off)[3] for off in range(1, 4)]
    wall = [place.in_wall(off)[2] for off in range(1, 16)]
    xs = [place.turn(x=off)[3] for off in range(1, 4)]
    ys = [place.turn(y=off)[3] for off in range(1, 4)]
    cells = wg.at[0].reshape(128, 4, C)
    s1 = Stage(srx.at[:, 0, 0], [(srow, sg.at[cell], p) for p in plane])
    w1 = Stage(cells.at[pl.ds(0, 3)], [(win_in, wg.at[(0, *cell)], p) for p in zs])
    v1 = Stage(cells.at[pl.ds(0, 3)], [(wout_in, wg.at[(1, *cell)], p) for p in zs])
    s2 = Stage(sg.reshape(128, 1, C).at[pl.ds(0, 120)], [(sg.at[y, z], sg.at[y, z], p) for p in wall])
    part = wg.at[0, y, :, x, core]
    w2 = Stage(cells.at[pl.ds(0, 12)], [(part, part, p) for p in xs])
    other = wg.at[1, y, :, x, core]
    v2 = Stage(cells.at[pl.ds(0, 12)], [(other, other, p) for p in ys])
    layer = wg.at[0, y, :, :, core]
    w3 = Stage(cells.at[pl.ds(0, 48)], [(layer, layer, p) for p in ys])
    slab = wg.at[1, :, :, x, core]
    v3 = Stage(cells.at[pl.ds(0, 48)], [(slab, slab, p) for p in xs])
    lot = wg.at[:, :, :, :, core]
    w4 = Stage(cells, [(lot, lot, place.sibling())])
    def tile_edges(b, ref, row0, col0, ext):
        edges = edge_ends(place, ref.at[b], row0, col0, ext.at[b])
        sides = Stage(src.at[b, pl.ds(0, H), pl.ds(0, 2 * LEFT), :], edges[0:2])
        return sides, Stage(src.at[b, pl.ds(0, 2 * R), :, :], edges[2:])

    (side0, ends0), (side1, ends1) = (tile_edges(b, feat, 0, 0, src) for b in range(B))

    s1.start()
    w1.start()
    v1.start()
    side0.start()
    side1.start()
    own[2].wait()
    own[3].wait()
    s1.arrive()
    s2.start()
    w1.arrive()
    w2.start()
    v1.arrive()
    v2.start()
    ends0.start()
    ends1.start()
    w2.arrive()
    w3.start()
    v2.arrive()
    v3.start()
    own[0].wait()
    own[1].wait()
    side0.arrive()
    side1.arrive()
    clear_columns(place, src)
    s2.arrive()

    small = sg.reshape(128, C)[...]
    small_t = small.T
    for n in range(K * K):
        taps[n] = jnp.broadcast_to(small_t[TAPS + n : TAPS + n + 1, :], (8, C))
    conv_bias = jnp.broadcast_to(small_t[CB : CB + 1, :], (8, C))

    def column_block(n):
        return n // 8, lax.rem(n, 8), pl.ds(pl.multiple_of(lax.rem(n, 8) * 8, 8), 8)

    def conv_step(n, carry):
        b, wb, at = column_block(n)
        acc = conv_tile(src, taps, b, wb, False, INNER, {p: conv_bias for p in range(H)})
        for p in range(H):
            mid[b, p, at, :] = acc[p]
        return carry

    lax.fori_loop(0, BLOCKS // 2, conv_step, 0)
    w3.arrive()
    v3.arrive()
    w4.start()
    lax.fori_loop(BLOCKS // 2, BLOCKS, conv_step, 0)

    def conv_rest(n, carry):
        b, wb, at = column_block(n)
        acc = conv_tile(src, taps, b, wb, False, OUTER, {p: mid[b, p, at, :] for p in FRINGE})
        for p in FRINGE:
            mid[b, p, at, :] = acc[p]
        return carry

    w4.arrive()
    gain_wide, shift_wide = widen(small[:, GAIN : GAIN + 1], 4), widen(small[:, SHIFT : SHIFT + 1], 4)
    scale_wide, ob_wide = widen(small[:, SCALE : SCALE + 1], 4), widen(small[:, OB : OB + 1], 1)
    win_t = wg.at[0].reshape(HID, C)[...]
    win = win_t.T
    wo_t = wg.at[1].reshape(HID, C)[...].T
    hi, lo = split(win * gain_wide)
    win2[0:C, :] = hi
    win2[C:, :] = hi
    winlo[...] = lo
    hi, lo = split(win_t * small_t[GAIN : GAIN + 1, :])
    wintop[:, 0:C] = hi
    wintop[:, C:] = lo
    hi, lo = split(wo_t * scale_wide)
    wot2[0:C, :] = hi
    wot2[C:, :] = hi
    wotlo[...] = lo
    pick = [lanes(32, 128, 1) == 4 * lanes(32, 128, 0) + k for k in range(4)]
    shifted = win * shift_wide
    for t in range(4):
        cut, band = slice(128 * t, 128 * t + 128), slice(32 * t, 32 * t + 32)
        terms = [jnp.where(pick[k], small[band, IB + k : IB + k + 1], 0.0) for k in range(4)]
        bias_eff[:, cut] = jnp.sum(shifted[:, cut], axis=0, keepdims=True) + jnp.sum(sum(terms), axis=0, keepdims=True)

    def mix(b, starts):
        spans = [pl.ds(p, QUARTER) for p in starts]
        x = jnp.concatenate([mid[b, s].reshape(M // 2, C) for s in spans], axis=0)
        ct = jnp.concatenate([cot[b, s].reshape(M // 2, C) for s in spans], axis=0)
        mean = jnp.mean(x, axis=-1, keepdims=True)
        cen = x - mean
        inv = lax.rsqrt(jnp.mean(cen * cen, axis=-1, keepdims=True) + norm_eps)
        normed = cen * inv
        n_hi, n_lo = split(normed)
        n2 = jnp.concatenate([n_hi, n_lo], axis=1)
        c_hi, c_lo = split(ct)
        c2 = jnp.concatenate([c_hi, c_lo], axis=1)
        nt2 = jnp.concatenate(split(normed.T), axis=0)
        ct2 = jnp.concatenate(split(ct.T), axis=0)
        cotacc[...] += jnp.sum(ct.reshape(M // 8, 8, C), axis=0)
        dn = jnp.zeros((M, C), f32)
        step = 256
        for h in range(0, HID, step):
            cut = slice(h, h + step)
            act = dot(n2, win2[:, cut]) + dot(n_hi, winlo[:, cut]) + bias_eff[:, cut]
            dh = dot(c2, wot2[:, cut]) + dot(c_hi, wotlo[:, cut])
            phi = 0.5 * (1.0 + lax.erf(act * inverse_root_two))
            slope = phi + act * jnp.exp(-0.5 * act * act) * inverse_root_twopi
            hid_hi, hid_lo = split(act * phi)
            da = dh * slope
            inbacc[:, cut] += jnp.sum(da.reshape(M // 8, 8, step), axis=0)
            da_hi, da_lo = split(da)
            both = dot(da_hi, wintop[cut, :])
            dn = dn + both[:, 0:C] + both[:, C:] + dot(da_lo, wintop[cut, 0:C])
            both = dot(nt2, da_hi)
            nacc[:, cut] += both[0:C] + both[C:] + dot(nt2[0:C], da_lo)
            both = dot(ct2, hid_hi)
            macc[:, cut] += both[0:C] + both[C:] + dot(ct2[0:C], hid_lo)
        dc = inv * (
            dn
            - jnp.mean(dn, axis=-1, keepdims=True)
            - normed * jnp.mean(dn * normed, axis=-1, keepdims=True)
        )
        dbacc[...] += jnp.sum(dc.reshape(M // 8, 8, C), axis=0)
        for n, p in enumerate(starts):
            part = dc[n * (M // 2) : (n + 1) * (M // 2)]
            dcv[b, pl.ds(R + p, QUARTER), LEFT : LEFT + W, :] = part.reshape(QUARTER, W, C)

    (back_side0, back_ends0), (back_side1, back_ends1) = (tile_edges(b, dcv, R, LEFT, dcv) for b in range(B))

    def mix_step(n, carry):
        outer = lax.rem((n + 1) // 2, 2)

        @pl.when(n == 1)
        def _():
            ends0.arrive()
            ends1.arrive()
            clear_rows(place, src)
            lax.fori_loop(0, BLOCKS, conv_rest, 0)

        @pl.when(n == 2)
        def _():
            back_ends0.start()
            back_side0.start()

        @pl.when(n == 3)
        def _():
            back_ends1.start()

        mix(n // 2, (QUARTER * (1 - outer), QUARTER * (2 + outer)))
        return carry

    lax.fori_loop(0, 4, mix_step, 0)
    back_side1.start()

    factor = 1.0 / math.sqrt(B * H * W * ROWS * COLS)
    nsum, msum = nacc[...], macc[...]
    inb = jnp.sum(inbacc[...], axis=0, keepdims=True)
    wp[0] = ((nsum * gain_wide + shift_wide * inb) * factor).T.reshape(4, 4, 4, 8, C)
    wp[1] = (msum * (scale_wide * factor)).T.reshape(4, 4, 4, 8, C)
    r0 = Stage(wcore, [(wp.at[1 - core], wcore, place.sibling())])
    r0.start()

    def kgrad_step(n, carry):
        kernel_grad_tile(src, dcv, kacc, n // 8, lax.rem(n, 8))
        return carry

    lax.fori_loop(0, CUT, kgrad_step, 0)
    r0.arrive()
    for a in range(4):
        for b in range(4):
            yy, xx = a * (1 - core) + b * core, b * (1 - core) + a * core
            wa[a, :, b] = wp[core, yy, :, xx] + wcore[yy, :, xx]
    first, second = y * (1 - core) + x * core, x * (1 - core) + y * core
    to1 = [place.turn(y=off * (1 - core), x=off * core)[3] for off in range(1, 4)]
    to2 = [place.turn(y=off * core, x=off * (1 - core))[3] for off in range(1, 4)]
    to3 = [place.in_column(off) for off in range(1, 8)]
    r1 = Stage(wr1, [(wa.at[lax.rem(first + 1 + n, 4)], wr1.at[n], p) for n, p in enumerate(to1)])
    r2 = Stage(wr2, [(wb_.at[lax.rem(second + 1 + n, 4)], wr2.at[n], p) for n, p in enumerate(to2)])
    r3 = Stage(wr3.reshape(8, 8, C).at[pl.ds(0, 7)], [(wc.at[zz], wr3.at[core, z], p) for zz, p in to3])
    r1.start()
    lax.fori_loop(CUT, BLOCKS, kgrad_step, 0)

    gain_g = jnp.sum(win * nsum, axis=1, keepdims=True)
    shift_g = jnp.sum(win * inb, axis=1, keepdims=True)
    scale_g = jnp.sum(wo_t * msum, axis=1, keepdims=True)
    for n in range(K * K):
        rows[n : n + 1, :] = jnp.sum(kacc[n], axis=0, keepdims=True)
    rows[K * K : K * K + 1, :] = jnp.sum(dbacc[...], axis=0, keepdims=True)
    rows[K * K + 1 : K * K + 2, :] = jnp.sum(cotacc[...], axis=0, keepdims=True)
    rows[K * K + 2 :, :] = jnp.zeros((128 - K * K - 2, C), f32)
    grads = rows[...].T
    lane = lanes(C, 128, 1)
    cot_wide = widen(grads[:, K * K + 1 : K * K + 2], 1)
    columns = [(GAIN, gain_g), (SHIFT, shift_g), (OB, scale_wide[:, 0:C] * cot_wide), (SCALE, scale_g + ob_wide * cot_wide)]
    for k in range(4):
        terms = [jnp.where(pick[k], inb[:, 128 * t : 128 * t + 128], 0.0) for t in range(4)]
        columns.append((IB + k, jnp.sum(jnp.concatenate(terms, axis=0), axis=1, keepdims=True)))
    for at, column in columns:
        grads = jnp.where(lane == at, column, grads)
    sp.reshape(128, C)[...] = grads * factor
    q1, q2 = [], []
    for off in range(1, 8):
        g, to = place.in_plane(off)
        q1.append((sp.at[:, :, g // 2, lax.rem(g, 2)], srx.at[off - 1], to))
    for off in range(1, 16):
        yy, zz, to = place.in_wall(off)
        q2.append((sb.at[yy, zz], sry.at[off - 1], to))
    q1, q2 = Stage(srx, q1), Stage(sry, q2)
    q1.start()

    back_side0.arrive()
    back_side1.arrive()
    clear_columns(place, dcv)

    def out_step(n, carry):
        b, wb, at = column_block(n)
        acc = conv_tile(dcv, taps, b, wb, True, INNER, {p: cot[b, p, at, :] for p in range(H)})
        for p in range(H):
            fg[b, p, at, :] = acc[p]
        return carry

    def out_rest(n, carry):
        b, wb, at = column_block(n)
        acc = conv_tile(dcv, taps, b, wb, True, OUTER, {p: fg[b, p, at, :] for p in FRINGE})
        for p in FRINGE:
            fg[b, p, at, :] = acc[p]
        return carry

    lax.fori_loop(0, 5, out_step, 0)
    r1.arrive()
    for n in range(4):
        wb_[n] = wa[first, :, n] + wr1[0, :, n] + wr1[1, :, n] + wr1[2, :, n]
    r2.start()
    lax.fori_loop(5, 8, out_step, 0)
    q1.arrive()
    total = sp[:, :, x, core]
    for n in range(7):
        total = total + srx[n]
    sb[...] = total
    q2.start()
    lax.fori_loop(8, 13, out_step, 0)
    r2.arrive()
    wc[...] = wb_[second] + wr2[0] + wr2[1] + wr2[2]
    r3.start()
    wr3[core, z] = wc[z]
    lax.fori_loop(13, BLOCKS, out_step, 0)
    back_ends0.arrive()
    back_ends1.arrive()
    clear_rows(place, dcv)
    lax.fori_loop(0, BLOCKS, out_rest, 0)
    put = pltpu.make_async_copy(fg, fg_out, out_sem.at[0])
    put.start()

    for stage in stages:
        if stage not in (r3, q2):
            stage.leave()
    q2.arrive()
    total = sb[y, z]
    for n in range(15):
        total = total + sry[n]
    small_out[...] = total
    r3.arrive()
    for kind in range(2):
        total = wr3[kind, 0] + wr3[kind, 1] + wr3[kind, 2] + wr3[kind, 3]
        weight_out[kind] = jnp.where(core == 0, total[0:4], total[4:8])

    put.wait()
    r3.leave()
    q2.leave()


def deliver(
    fg_in, small_in, weight_in,
    fg_out, taps_out, cb_out, gain_out, shift_out, win_out, ib_out, wout_out, ob_out, scale_out,
    buf, row, weights, taps, cb, gain, shift, ib, ob, scale, sem,
):
    pieces = [(b, pl.ds(h, H // 2)) for b in range(B) for h in range(0, H, H // 2)]
    small = pltpu.make_async_copy(small_in, row, sem.at[8])
    weight = pltpu.make_async_copy(weight_in, weights, sem.at[9])
    gets = [pltpu.make_async_copy(fg_in.at[at], buf.at[at], sem.at[n]) for n, at in enumerate(pieces)]
    puts = [pltpu.make_async_copy(buf.at[at], fg_out.at[at], sem.at[4 + n]) for n, at in enumerate(pieces)]
    for copy in [small, weight] + gets:
        copy.start()
    small.wait()
    for i in range(K):
        for j in range(K):
            taps[i, 0, j] = row[0, TAPS + i * K + j]
    for at, ref in ((CB, cb), (GAIN, gain), (SHIFT, shift), (OB, ob), (SCALE, scale)):
        ref[0] = row[0, at]
    for k in range(4):
        ib[k] = row[0, IB + k]
    ends = [
        (taps, taps_out), (cb, cb_out), (gain, gain_out), (shift, shift_out), (ob, ob_out), (scale, scale_out),
        (ib, ib_out), (weights.at[0], win_out), (weights.at[1], wout_out),
    ]
    weight.wait()
    rest = [pltpu.make_async_copy(a, b, sem.at[10 + n]) for n, (a, b) in enumerate(ends)]
    for copy in rest:
        copy.start()
    for get, put in zip(gets, puts):
        get.wait()
        put.start()
    for copy in rest + puts:
        copy.wait()


def per_device(
    features, cotangent, conv_kernel, conv_bias, norm_gain, norm_shift,
    w_in, in_bias, w_out, out_bias, layer_scale,
):
    vmem = lambda *shape: pltpu.VMEM(shape, f32)
    smem = lambda *shape: pltpu.SMEM(shape, f32)
    half = lambda *shape: pltpu.VMEM(shape, bf16)
    dma = lambda n: pltpu.SemaphoreType.DMA((n,))
    out = lambda *shape: jax.ShapeDtypeStruct(shape, f32)
    anywhere = pl.BlockSpec(memory_space=pl.ANY)
    inside = pl.BlockSpec(memory_space=pltpu.VMEM)
    tile = (B, H, W, C)
    fg, small, weights = pl.pallas_call(
        kernel,
        out_shape=(out(*tile), out(1, C), out(2, 4, C)),
        in_specs=[anywhere] * 11,
        out_specs=(anywhere, inside, inside),
        scratch_shapes=[
            smem(K, 1, K), smem(1), smem(1), smem(1), smem(1), smem(1), smem(4), vmem(1, C),
            vmem(B, HE, WE, C), vmem(*tile), vmem(B, HE, WE, C), vmem(*tile), vmem(*tile),
            vmem(4, 4, 4, 2, 1, C), vmem(2, 4, 4, 4, 2, 4, C), vmem(K * K, 8, C),
            half(2 * C, HID), half(C, HID), half(HID, 2 * C), half(2 * C, HID), half(C, HID), vmem(1, HID),
            vmem(C, HID), vmem(C, HID), vmem(8, HID), vmem(K * K, 8, C), vmem(8, C), vmem(8, C),
            vmem(2, 4, 4, 4, 8, C), vmem(4, 4, 4, 8, C), vmem(4, 4, 4, 8, C), vmem(3, 4, 4, 8, C),
            vmem(4, 4, 8, C), vmem(3, 4, 8, C), vmem(4, 8, C), vmem(2, 4, 8, C),
            vmem(128, C), vmem(4, 4, 4, 2, 1, C), vmem(7, 4, 4, 1, C), vmem(4, 4, 1, C), vmem(15, 1, C),
            dma(11), dma(1), dma(23), dma(23),
        ],
        compiler_params=pltpu.CompilerParams(
            collective_id=0, has_side_effects=True, vmem_limit_bytes=56 * 2**20
        ),
    )(
        features, cotangent, conv_kernel.transpose(0, 2, 1), conv_bias, norm_gain, norm_shift,
        out_bias, layer_scale, in_bias, w_in.T, w_out,
    )
    fg, taps_g, cb_g, gain_g, shift_g, win_g, ib_g, wout_g, ob_g, scale_g = pl.pallas_call(
        deliver,
        out_shape=(
            out(*tile), out(K, 1, K), out(1), out(1), out(1), out(4, C), out(4), out(4, C), out(1), out(1),
        ),
        in_specs=[anywhere] * 3,
        out_specs=(anywhere,) * 10,
        scratch_shapes=[
            vmem(*tile), smem(1, C), vmem(2, 4, C), smem(K, 1, K), smem(1), smem(1), smem(1), smem(4), smem(1), smem(1), dma(19),
        ],
    )(fg, small, weights)
    return fg, taps_g.transpose(0, 2, 1), cb_g, gain_g, shift_g, win_g.T, ib_g, wout_g, ob_g, scale_g


def solution(mesh):
    both = ("row", "col")
    tile = P(None, "row", "col", None)
    taps, vector = P(None, None, both), P(both)
    return jax.shard_map(
        per_device,
        mesh=mesh,
        in_specs=(tile, tile, taps, vector, vector, vector, P(None, both), vector, P(both, None), vector, vector),
        out_specs=(tile, taps, vector, vector, vector, P(None, both), vector, P(both, None), vector, vector),
        check_vma=False,
    )
```

```python
import functools
import math

import jax
import jax.numpy as jnp
from jax import lax
from jax.experimental import pallas as pl
from jax.experimental.pallas import tpu as pltpu
from jax.sharding import PartitionSpec as P

norm_eps = 1e-06
inverse_root_two = 0.7071067811865476
inverse_root_twopi = 0.3989422804014327
MESH = pl.DeviceIdType.MESH
f32, bf16 = jnp.float32, jnp.bfloat16

K, R = 7, 3
C, HID = 128, 512
B, H, W = 2, 16, 64
LEFT = 8
WE = W + 2 * LEFT
HE = H + 2 * R
ROWS, COLS = 8, 16
QUARTER = H // 4
BLOCKS = B * W // 8
CUT = BLOCKS // 2 + 1
LATE = BLOCKS - 5
M = 2 * QUARTER * W
TAPS, CB, GAIN, SHIFT, OB, SCALE, IB = 0, 49, 50, 51, 52, 53, 54


def split(x):
    hi = x.astype(bf16)
    return hi, (x - hi.astype(f32)).astype(bf16)


def dot(a, b):
    return jnp.dot(a, b, preferred_element_type=f32)


def lanes(x, n, axis):
    return lax.broadcasted_iota(jnp.int32, (x, n), axis)


class Place:
    def __init__(self):
        self.row, self.col = lax.axis_index("row"), lax.axis_index("col")
        self.y = self.row // 2
        self.z = lax.rem(self.row, 2) * 2 + self.col // 8
        self.g = lax.rem(self.col, 8)
        self.x, self.core = self.g // 2, lax.rem(self.g, 2)

    def at(self, y, z, x, core):
        return (y * 2 + z // 2, lax.rem(z, 2) * 8 + x * 2 + core)

    def turn(self, y=0, z=0, x=0):
        y, z, x = lax.rem(self.y + y, 4), lax.rem(self.z + z, 4), lax.rem(self.x + x, 4)
        return y, z, x, self.at(y, z, x, self.core)

    def in_plane(self, off):
        other = lax.rem(self.g + off, 8)
        return other, self.at(self.y, self.z, other // 2, lax.rem(other, 2))

    def in_column(self, off):
        other = lax.rem(self.z * 2 + self.core + off, 8)
        return other // 2, self.at(self.y, other // 2, self.x, lax.rem(other, 2))

    def in_wall(self, off):
        y, z = lax.rem(self.y + off // 4, 4), lax.rem(self.z + off % 4, 4)
        return y, z, self.at(y, z, self.x, self.core)

    def sibling(self):
        return self.at(self.y, self.z, self.x, 1 - self.core)

    def neighbour(self, dr, dc):
        return (lax.rem(self.row + dr + ROWS, ROWS), lax.rem(self.col + dc + COLS, COLS))


def side_ends(place, src, row0, col0, ext):
    ends = []
    for dc in (-1, 1):
        read = col0 if dc < 0 else col0 + W - LEFT
        land = LEFT + W if dc < 0 else 0
        ends.append(
            (
                src.at[pl.ds(row0, H), pl.ds(read, LEFT), :],
                ext.at[pl.ds(R, H), pl.ds(land, LEFT), :],
                place.neighbour(0, dc),
            )
        )
    return ends


def row_ends(place, src, row0, col0, ext, near):
    odd = lax.rem(place.row, 2)
    low = odd if near else 1 - odd
    rows, landing = pl.ds(row0 + (H - R) * (1 - low), R), pl.ds((R + H) * low, R)
    ends = []
    for dc in (0, -1, 1):
        read, land, n = (col0, LEFT, W) if dc == 0 else (col0, LEFT + W, LEFT) if dc < 0 else (col0 + W - LEFT, 0, LEFT)
        ends.append(
            (
                src.at[rows, pl.ds(read, n), :],
                ext.at[landing, pl.ds(land, n), :],
                place.neighbour(1 - 2 * low, dc),
            )
        )
    return ends


def clear_columns(place, ext):
    @pl.when(place.col == 0)
    def _():
        ext[:, R : R + H, 0:LEFT] = jnp.zeros((B, H, LEFT, C), f32)

    @pl.when(place.col == COLS - 1)
    def _():
        ext[:, R : R + H, LEFT + W :] = jnp.zeros((B, H, LEFT, C), f32)


def clear_rows(place, ext):
    for edge, at in ((0, slice(0, R)), (ROWS - 1, slice(R + H, HE))):

        @pl.when(place.row == edge)
        def _():
            ext[:, at] = jnp.zeros((B, R, WE, C), f32)

        @pl.when(place.col == 0)
        def _():
            ext[:, at, 0:LEFT] = jnp.zeros((B, R, LEFT, C), f32)

        @pl.when(place.col == COLS - 1)
        def _():
            ext[:, at, LEFT + W :] = jnp.zeros((B, R, LEFT, C), f32)


def conv_tile(ext, taps, b, wb, flip, rows, acc):
    for j in range(K):
        tap = [taps[(K - 1 - i) * K + K - 1 - j] if flip else taps[i * K + j] for i in range(K)]
        for e in rows:
            x = ext[b, e, pl.ds(8 * wb + LEFT - R + j, 8), :]
            for i in range(K):
                p = e - i
                if 0 <= p < H:
                    acc[p] = acc[p] + tap[i] * x
    return acc


INNER = range(R, R + H)
OUTER = (*range(R), *range(R + H, HE))
FRINGE = (*range(R), *range(H - R, H))


def kernel_grad_tile(ext, dcv, kacc, b, wb):
    grads = [dcv[b, R + p, pl.ds(pl.multiple_of(8 * wb + LEFT, 8), 8), :] for p in range(H)]
    for j in range(K):
        acc = [kacc[i * K + j] for i in range(K)]
        for e in range(HE):
            x = ext[b, e, pl.ds(8 * wb + LEFT - R + j, 8), :]
            for i in range(K):
                p = e - i
                if 0 <= p < H:
                    acc[i] = acc[i] + grads[p] * x
        for i in range(K):
            kacc[i * K + j] = acc[i]


def widen(column, n):
    one = jnp.broadcast_to(column, (column.shape[0], 128))
    return jnp.concatenate([one] * n, axis=1)


def kernel(
    feat, cot_hbm, taps_in, cb_in, gain_in, shift_in, ob_in, scale_in, ib_in, win_in, wout_in,
    fg_out, small_out, weight_out,
    taps_s, cb_s, gain_s, shift_s, ob_s, scale_s, ib_s, srow,
    src, cot, dcv, mid, fg, sg, wg, taps,
    win2, winlo, wintop, wot2, wotlo, bias_eff,
    nacc, macc, inbacc, kacc, cotacc, dbacc,
    wp, wcore, wa, wr1, wb_, wr2, wc, wr3, rows, sp, srx, sb, sry,
    local, out_sem, sent, arrived,
):
    place = Place()
    y, z, x, core = place.y, place.z, place.x, place.core

    scalars = [(taps_in, taps_s), (cb_in, cb_s), (gain_in, gain_s), (shift_in, shift_s), (ob_in, ob_s), (scale_in, scale_s), (ib_in, ib_s)]
    params = [pltpu.make_async_copy(a, b, local.at[4 + n]) for n, (a, b) in enumerate(scalars)]
    own = [
        pltpu.make_async_copy(feat, src.at[:, pl.ds(R, H), pl.ds(LEFT, W), :], local.at[0]),
        pltpu.make_async_copy(cot_hbm, cot, local.at[1]),
        pltpu.make_async_copy(win_in, wg.at[0, y, z, x, core], local.at[2]),
        pltpu.make_async_copy(wout_in, wg.at[1, y, z, x, core], local.at[3]),
    ]
    for copy in params + own:
        copy.start()

    barrier = pltpu.get_barrier_semaphore()
    partners = [place.neighbour(dr, dc) for dr in (-1, 0, 1) for dc in (-1, 0, 1) if dr or dc]
    partners += [place.in_plane(off)[1] for off in range(1, 8)]
    partners += [place.in_column(off)[1] for off in range(1, 8)]
    partners += [place.in_wall(off)[2] for off in range(1, 16)]
    for partner in partners:
        pl.semaphore_signal(barrier, inc=1, device_id=partner, device_id_type=MESH)

    for copy in params:
        copy.wait()
    lane = lanes(1, 128, 1)
    row = jnp.zeros((1, 128), f32)
    for i in range(K):
        for j in range(K):
            row = jnp.where(lane == TAPS + i * K + j, taps_s[i, 0, j], row)
    for at, ref in ((CB, cb_s), (GAIN, gain_s), (SHIFT, shift_s), (OB, ob_s), (SCALE, scale_s)):
        row = jnp.where(lane == at, ref[0], row)
    for k in range(4):
        row = jnp.where(lane == IB + k, ib_s[k], row)
    srow[...] = row
    sg[y, z, x, core] = row
    kacc[...] = jnp.zeros_like(kacc)
    nacc[...] = jnp.zeros_like(nacc)
    macc[...] = jnp.zeros_like(macc)
    inbacc[...] = jnp.zeros_like(inbacc)
    cotacc[...] = jnp.zeros_like(cotacc)
    dbacc[...] = jnp.zeros_like(dbacc)

    pl.semaphore_wait(barrier, len(partners))

    stages = []

    class Stage:
        def __init__(self, amount, copies):
            self.n = len(stages)
            stages.append(self)
            self.amount = amount
            self.copies = [self.copy(*ends) for ends in copies]

        def copy(self, a, b, partner):
            return pltpu.make_async_remote_copy(
                src_ref=a, dst_ref=b, send_sem=sent.at[self.n], recv_sem=arrived.at[self.n],
                device_id=partner, device_id_type=MESH,
            )

        def start(self):
            for copy in self.copies:
                copy.start()

        def arrive(self):
            self.copy(self.amount, self.amount, place.sibling()).wait_recv()

        def leave(self):
            self.copy(self.amount, self.amount, place.sibling()).wait_send()

    cell = (y, z, x, core)
    plane = [place.in_plane(off)[1] for off in range(1, 8)]
    zs = [place.turn(z=off)[3] for off in range(1, 4)]
    wall = [place.in_wall(off)[2] for off in range(1, 16)]
    xs = [place.turn(x=off)[3] for off in range(1, 4)]
    ys = [place.turn(y=off)[3] for off in range(1, 4)]
    cells = wg.at[0].reshape(128, 4, C)
    s1 = Stage(srx.at[:, 0, 0], [(srow, sg.at[cell], p) for p in plane])
    w1 = Stage(cells.at[pl.ds(0, 3)], [(win_in, wg.at[(0, *cell)], p) for p in zs])
    v1 = Stage(cells.at[pl.ds(0, 3)], [(wout_in, wg.at[(1, *cell)], p) for p in zs])
    s2 = Stage(sg.reshape(128, 1, C).at[pl.ds(0, 120)], [(sg.at[y, z], sg.at[y, z], p) for p in wall])
    part = wg.at[0, y, :, x, core]
    w2 = Stage(cells.at[pl.ds(0, 12)], [(part, part, p) for p in xs])
    other = wg.at[1, y, :, x, core]
    v2 = Stage(cells.at[pl.ds(0, 12)], [(other, other, p) for p in ys])
    layer = wg.at[0, y, :, :, core]
    w3 = Stage(cells.at[pl.ds(0, 48)], [(layer, layer, p) for p in ys])
    slab = wg.at[1, :, :, x, core]
    v3 = Stage(cells.at[pl.ds(0, 48)], [(slab, slab, p) for p in xs])
    lot = wg.at[:, :, :, :, core]
    w4 = Stage(cells, [(lot, lot, place.sibling())])
    def tile_edges(ref, row0, col0, ext):
        sides, nears, fars = [], [], []
        for b in range(B):
            ends = (place, ref.at[b], row0, col0, ext.at[b])
            sides.append(Stage(src.at[b, pl.ds(0, H), pl.ds(0, 2 * LEFT), :], side_ends(*ends)))
            nears.append(Stage(src.at[b, pl.ds(0, R), :, :], row_ends(*ends, True)))
            fars.append(Stage(src.at[b, pl.ds(0, R), :, :], row_ends(*ends, False)))
        return sides, nears, fars

    def start(*stages):
        for stage in stages:
            stage.start()

    def arrive(*stages):
        for stage in stages:
            stage.arrive()

    sides, nears, fars = tile_edges(feat, 0, 0, src)

    s1.start()
    w1.start()
    v1.start()
    start(*sides)
    own[2].wait()
    own[3].wait()
    s1.arrive()
    s2.start()
    w1.arrive()
    w2.start()
    v1.arrive()
    v2.start()
    start(*nears)
    w2.arrive()
    w3.start()
    v2.arrive()
    v3.start()
    start(*fars)
    own[0].wait()
    own[1].wait()
    arrive(*sides)
    clear_columns(place, src)
    s2.arrive()

    small = sg.reshape(128, C)[...]
    small_t = small.T
    for n in range(K * K):
        taps[n] = jnp.broadcast_to(small_t[TAPS + n : TAPS + n + 1, :], (8, C))
    conv_bias = jnp.broadcast_to(small_t[CB : CB + 1, :], (8, C))

    def column_block(n):
        return n // 8, lax.rem(n, 8), pl.ds(pl.multiple_of(lax.rem(n, 8) * 8, 8), 8)

    def conv_step(n, carry):
        b, wb, at = column_block(n)
        acc = conv_tile(src, taps, b, wb, False, INNER, {p: conv_bias for p in range(H)})
        for p in range(H):
            mid[b, p, at, :] = acc[p]
        return carry

    lax.fori_loop(0, LATE, conv_step, 0)
    w3.arrive()
    v3.arrive()
    w4.start()
    lax.fori_loop(LATE, BLOCKS, conv_step, 0)

    def conv_rest(n, carry):
        b, wb, at = column_block(n)
        acc = conv_tile(src, taps, b, wb, False, OUTER, {p: mid[b, p, at, :] for p in FRINGE})
        for p in FRINGE:
            mid[b, p, at, :] = acc[p]
        return carry

    w4.arrive()
    gain_wide, shift_wide = widen(small[:, GAIN : GAIN + 1], 4), widen(small[:, SHIFT : SHIFT + 1], 4)
    scale_wide, ob_wide = widen(small[:, SCALE : SCALE + 1], 4), widen(small[:, OB : OB + 1], 1)
    win_t = wg.at[0].reshape(HID, C)[...]
    win = win_t.T
    wo_t = wg.at[1].reshape(HID, C)[...].T
    hi, lo = split(win * gain_wide)
    win2[0:C, :] = hi
    win2[C:, :] = hi
    winlo[...] = lo
    hi, lo = split(win_t * small_t[GAIN : GAIN + 1, :])
    wintop[:, 0:C] = hi
    wintop[:, C:] = lo
    hi, lo = split(wo_t * scale_wide)
    wot2[0:C, :] = hi
    wot2[C:, :] = hi
    wotlo[...] = lo
    pick = [lanes(32, 128, 1) == 4 * lanes(32, 128, 0) + k for k in range(4)]
    shifted = win * shift_wide
    for t in range(4):
        cut, band = slice(128 * t, 128 * t + 128), slice(32 * t, 32 * t + 32)
        terms = [jnp.where(pick[k], small[band, IB + k : IB + k + 1], 0.0) for k in range(4)]
        bias_eff[:, cut] = jnp.sum(shifted[:, cut], axis=0, keepdims=True) + jnp.sum(sum(terms), axis=0, keepdims=True)

    def mix(b, starts):
        spans = [pl.ds(p, QUARTER) for p in starts]
        x = jnp.concatenate([mid[b, s].reshape(M // 2, C) for s in spans], axis=0)
        ct = jnp.concatenate([cot[b, s].reshape(M // 2, C) for s in spans], axis=0)
        mean = jnp.mean(x, axis=-1, keepdims=True)
        cen = x - mean
        inv = lax.rsqrt(jnp.mean(cen * cen, axis=-1, keepdims=True) + norm_eps)
        normed = cen * inv
        n_hi, n_lo = split(normed)
        n2 = jnp.concatenate([n_hi, n_lo], axis=1)
        c_hi, c_lo = split(ct)
        c2 = jnp.concatenate([c_hi, c_lo], axis=1)
        nt2 = jnp.concatenate(split(normed.T), axis=0)
        ct2 = jnp.concatenate(split(ct.T), axis=0)
        cotacc[...] += jnp.sum(ct.reshape(M // 8, 8, C), axis=0)
        dn = jnp.zeros((M, C), f32)
        step = 256
        for h in range(0, HID, step):
            cut = slice(h, h + step)
            act = dot(n2, win2[:, cut]) + dot(n_hi, winlo[:, cut]) + bias_eff[:, cut]
            dh = dot(c2, wot2[:, cut]) + dot(c_hi, wotlo[:, cut])
            phi = 0.5 * (1.0 + lax.erf(act * inverse_root_two))
            slope = phi + act * jnp.exp(-0.5 * act * act) * inverse_root_twopi
            hid_hi, hid_lo = split(act * phi)
            da = dh * slope
            inbacc[:, cut] += jnp.sum(da.reshape(M // 8, 8, step), axis=0)
            da_hi, da_lo = split(da)
            both = dot(da_hi, wintop[cut, :])
            dn = dn + both[:, 0:C] + both[:, C:] + dot(da_lo, wintop[cut, 0:C])
            both = dot(nt2, da_hi)
            nacc[:, cut] += both[0:C] + both[C:] + dot(nt2[0:C], da_lo)
            both = dot(ct2, hid_hi)
            macc[:, cut] += both[0:C] + both[C:] + dot(ct2[0:C], hid_lo)
        dc = inv * (
            dn
            - jnp.mean(dn, axis=-1, keepdims=True)
            - normed * jnp.mean(dn * normed, axis=-1, keepdims=True)
        )
        dbacc[...] += jnp.sum(dc.reshape(M // 8, 8, C), axis=0)
        for n, p in enumerate(starts):
            part = dc[n * (M // 2) : (n + 1) * (M // 2)]
            dcv[b, pl.ds(R + p, QUARTER), LEFT : LEFT + W, :] = part.reshape(QUARTER, W, C)

    back_sides, back_nears, back_fars = tile_edges(dcv, R, LEFT, dcv)

    def mix_step(n, carry):
        outer = lax.rem((n + 1) // 2, 2)

        @pl.when(n == 1)
        def _():
            arrive(*nears, *fars)
            clear_rows(place, src)
            lax.fori_loop(0, BLOCKS, conv_rest, 0)

        @pl.when(n == 2)
        def _():
            start(back_fars[0], back_nears[0], back_sides[0])

        @pl.when(n == 3)
        def _():
            start(back_fars[1], back_nears[1])

        mix(n // 2, (QUARTER * (1 - outer), QUARTER * (2 + outer)))
        return carry

    lax.fori_loop(0, 4, mix_step, 0)
    back_sides[1].start()

    factor = 1.0 / math.sqrt(B * H * W * ROWS * COLS)
    nsum, msum = nacc[...], macc[...]
    inb = jnp.sum(inbacc[...], axis=0, keepdims=True)
    wp[0] = ((nsum * gain_wide + shift_wide * inb) * factor).T.reshape(4, 4, 4, 8, C)
    wp[1] = (msum * (scale_wide * factor)).T.reshape(4, 4, 4, 8, C)
    r0 = Stage(wcore, [(wp.at[1 - core], wcore, place.sibling())])
    r0.start()

    def kgrad_step(n, carry):
        kernel_grad_tile(src, dcv, kacc, n // 8, lax.rem(n, 8))
        return carry

    lax.fori_loop(0, CUT, kgrad_step, 0)
    r0.arrive()
    for a in range(4):
        wa[a] = wp[core, :, :, a] + wcore[:, :, a]
    to3 = [place.in_column(off) for off in range(1, 8)]
    r1 = Stage(wr1, [(wa.at[lax.rem(x + 1 + n, 4)], wr1.at[n], p) for n, p in enumerate(xs)])
    r2 = Stage(wr2, [(wb_.at[lax.rem(y + 1 + n, 4)], wr2.at[n], p) for n, p in enumerate(ys)])
    r3 = Stage(wr3.reshape(8, 8, C).at[pl.ds(0, 7)], [(wc.at[zz], wr3.at[core, z], p) for zz, p in to3])
    r1.start()
    lax.fori_loop(CUT, BLOCKS, kgrad_step, 0)

    gain_g = jnp.sum(win * nsum, axis=1, keepdims=True)
    shift_g = jnp.sum(win * inb, axis=1, keepdims=True)
    scale_g = jnp.sum(wo_t * msum, axis=1, keepdims=True)
    for n in range(K * K):
        rows[n : n + 1, :] = jnp.sum(kacc[n], axis=0, keepdims=True)
    rows[K * K : K * K + 1, :] = jnp.sum(dbacc[...], axis=0, keepdims=True)
    rows[K * K + 1 : K * K + 2, :] = jnp.sum(cotacc[...], axis=0, keepdims=True)
    rows[K * K + 2 :, :] = jnp.zeros((128 - K * K - 2, C), f32)
    grads = rows[...].T
    lane = lanes(C, 128, 1)
    cot_wide = widen(grads[:, K * K + 1 : K * K + 2], 1)
    columns = [(GAIN, gain_g), (SHIFT, shift_g), (OB, scale_wide[:, 0:C] * cot_wide), (SCALE, scale_g + ob_wide * cot_wide)]
    for k in range(4):
        terms = [jnp.where(pick[k], inb[:, 128 * t : 128 * t + 128], 0.0) for t in range(4)]
        columns.append((IB + k, jnp.sum(jnp.concatenate(terms, axis=0), axis=1, keepdims=True)))
    for at, column in columns:
        grads = jnp.where(lane == at, column, grads)
    sp.reshape(128, C)[...] = grads * factor
    q1, q2 = [], []
    for off in range(1, 8):
        g, to = place.in_plane(off)
        q1.append((sp.at[:, :, g // 2, lax.rem(g, 2)], srx.at[off - 1], to))
    for off in range(1, 16):
        yy, zz, to = place.in_wall(off)
        q2.append((sb.at[yy, zz], sry.at[off - 1], to))
    q1, q2 = Stage(srx, q1), Stage(sry, q2)
    q1.start()

    arrive(*back_sides)
    clear_columns(place, dcv)

    def out_step(n, carry):
        b, wb, at = column_block(n)
        acc = conv_tile(dcv, taps, b, wb, True, INNER, {p: cot[b, p, at, :] for p in range(H)})
        for p in range(H):
            fg[b, p, at, :] = acc[p]
        return carry

    def out_rest(n, carry):
        b, wb, at = column_block(n)
        acc = conv_tile(dcv, taps, b, wb, True, OUTER, {p: fg[b, p, at, :] for p in FRINGE})
        for p in FRINGE:
            fg[b, p, at, :] = acc[p]
        return carry

    lax.fori_loop(0, 5, out_step, 0)
    r1.arrive()
    wb_[...] = wa[x] + wr1[0] + wr1[1] + wr1[2]
    r2.start()
    lax.fori_loop(5, 8, out_step, 0)
    q1.arrive()
    total = sp[:, :, x, core]
    for n in range(7):
        total = total + srx[n]
    sb[...] = total
    q2.start()
    lax.fori_loop(8, 13, out_step, 0)
    r2.arrive()
    wc[...] = wb_[y] + wr2[0] + wr2[1] + wr2[2]
    r3.start()
    wr3[core, z] = wc[z]
    lax.fori_loop(13, BLOCKS, out_step, 0)
    arrive(*back_nears, *back_fars)
    clear_rows(place, dcv)
    lax.fori_loop(0, BLOCKS, out_rest, 0)
    put = pltpu.make_async_copy(fg, fg_out, out_sem.at[0])
    put.start()

    for stage in stages:
        if stage not in (r3, q2):
            stage.leave()
    q2.arrive()
    total = sb[y, z]
    for n in range(15):
        total = total + sry[n]
    small_out[...] = total
    r3.arrive()
    for kind in range(2):
        total = wr3[kind, 0] + wr3[kind, 1] + wr3[kind, 2] + wr3[kind, 3]
        weight_out[kind] = jnp.where(core == 0, total[0:4], total[4:8])

    put.wait()
    r3.leave()
    q2.leave()


def deliver(
    fg_in, small_in, weight_in,
    fg_out, taps_out, cb_out, gain_out, shift_out, win_out, ib_out, wout_out, ob_out, scale_out,
    buf, row, weights, taps, cb, gain, shift, ib, ob, scale, sem,
):
    pieces = [(b, pl.ds(h, H // 2)) for b in range(B) for h in range(0, H, H // 2)]
    small = pltpu.make_async_copy(small_in, row, sem.at[8])
    weight = pltpu.make_async_copy(weight_in, weights, sem.at[9])
    gets = [pltpu.make_async_copy(fg_in.at[at], buf.at[at], sem.at[n]) for n, at in enumerate(pieces)]
    puts = [pltpu.make_async_copy(buf.at[at], fg_out.at[at], sem.at[4 + n]) for n, at in enumerate(pieces)]
    for copy in [small, weight] + gets:
        copy.start()
    small.wait()
    for i in range(K):
        for j in range(K):
            taps[i, 0, j] = row[0, TAPS + i * K + j]
    for at, ref in ((CB, cb), (GAIN, gain), (SHIFT, shift), (OB, ob), (SCALE, scale)):
        ref[0] = row[0, at]
    for k in range(4):
        ib[k] = row[0, IB + k]
    ends = [
        (taps, taps_out), (cb, cb_out), (gain, gain_out), (shift, shift_out), (ob, ob_out), (scale, scale_out),
        (ib, ib_out), (weights.at[0], win_out), (weights.at[1], wout_out),
    ]
    weight.wait()
    rest = [pltpu.make_async_copy(a, b, sem.at[10 + n]) for n, (a, b) in enumerate(ends)]
    for copy in rest:
        copy.start()
    for get, put in zip(gets, puts):
        get.wait()
        put.start()
    for copy in rest + puts:
        copy.wait()


def per_device(
    features, cotangent, conv_kernel, conv_bias, norm_gain, norm_shift,
    w_in, in_bias, w_out, out_bias, layer_scale,
):
    vmem = lambda *shape: pltpu.VMEM(shape, f32)
    smem = lambda *shape: pltpu.SMEM(shape, f32)
    half = lambda *shape: pltpu.VMEM(shape, bf16)
    dma = lambda n: pltpu.SemaphoreType.DMA((n,))
    out = lambda *shape: jax.ShapeDtypeStruct(shape, f32)
    anywhere = pl.BlockSpec(memory_space=pl.ANY)
    inside = pl.BlockSpec(memory_space=pltpu.VMEM)
    tile = (B, H, W, C)
    fg, small, weights = pl.pallas_call(
        kernel,
        out_shape=(out(*tile), out(1, C), out(2, 4, C)),
        in_specs=[anywhere] * 11,
        out_specs=(anywhere, inside, inside),
        scratch_shapes=[
            smem(K, 1, K), smem(1), smem(1), smem(1), smem(1), smem(1), smem(4), vmem(1, C),
            vmem(B, HE, WE, C), vmem(*tile), vmem(B, HE, WE, C), vmem(*tile), vmem(*tile),
            vmem(4, 4, 4, 2, 1, C), vmem(2, 4, 4, 4, 2, 4, C), vmem(K * K, 8, C),
            half(2 * C, HID), half(C, HID), half(HID, 2 * C), half(2 * C, HID), half(C, HID), vmem(1, HID),
            vmem(C, HID), vmem(C, HID), vmem(8, HID), vmem(K * K, 8, C), vmem(8, C), vmem(8, C),
            vmem(2, 4, 4, 4, 8, C), vmem(4, 4, 4, 8, C), vmem(4, 4, 4, 8, C), vmem(3, 4, 4, 8, C),
            vmem(4, 4, 8, C), vmem(3, 4, 8, C), vmem(4, 8, C), vmem(2, 4, 8, C),
            vmem(128, C), vmem(4, 4, 4, 2, 1, C), vmem(7, 4, 4, 1, C), vmem(4, 4, 1, C), vmem(15, 1, C),
            dma(11), dma(1), dma(27), dma(27),
        ],
        compiler_params=pltpu.CompilerParams(
            collective_id=0, has_side_effects=True, vmem_limit_bytes=56 * 2**20
        ),
    )(
        features, cotangent, conv_kernel.transpose(0, 2, 1), conv_bias, norm_gain, norm_shift,
        out_bias, layer_scale, in_bias, w_in.T, w_out,
    )
    fg, taps_g, cb_g, gain_g, shift_g, win_g, ib_g, wout_g, ob_g, scale_g = pl.pallas_call(
        deliver,
        out_shape=(
            out(*tile), out(K, 1, K), out(1), out(1), out(1), out(4, C), out(4), out(4, C), out(1), out(1),
        ),
        in_specs=[anywhere] * 3,
        out_specs=(anywhere,) * 10,
        scratch_shapes=[
            vmem(*tile), smem(1, C), vmem(2, 4, C), smem(K, 1, K), smem(1), smem(1), smem(1), smem(4), smem(1), smem(1), dma(19),
        ],
    )(fg, small, weights)
    return fg, taps_g.transpose(0, 2, 1), cb_g, gain_g, shift_g, win_g.T, ib_g, wout_g, ob_g, scale_g


def solution(mesh):
    both = ("row", "col")
    tile = P(None, "row", "col", None)
    taps, vector = P(None, None, both), P(both)
    return jax.shard_map(
        per_device,
        mesh=mesh,
        in_specs=(tile, tile, taps, vector, vector, vector, P(None, both), vector, P(both, None), vector, vector),
        out_specs=(tile, taps, vector, vector, vector, P(None, both), vector, P(both, None), vector, vector),
        check_vma=False,
    )
```

```python
import functools
import math

import jax
import jax.numpy as jnp
from jax import lax
from jax.experimental import pallas as pl
from jax.experimental.pallas import tpu as pltpu
from jax.sharding import PartitionSpec as P

norm_eps = 1e-06
inverse_root_two = 0.7071067811865476
inverse_root_twopi = 0.3989422804014327
MESH = pl.DeviceIdType.MESH
f32, bf16 = jnp.float32, jnp.bfloat16

K, R = 7, 3
C, HID = 128, 512
B, H, W = 2, 16, 64
LEFT = 8
WE = W + 2 * LEFT
HE = H + 2 * R
ROWS, COLS = 8, 16
QUARTER = H // 4
BLOCKS = B * W // 8
CUT = BLOCKS // 2 + 1
LATE = BLOCKS - 5
M = 2 * QUARTER * W
TAPS, CB, GAIN, SHIFT, OB, SCALE, IB = 0, 49, 50, 51, 52, 53, 54


def split(x):
    hi = x.astype(bf16)
    return hi, (x - hi.astype(f32)).astype(bf16)


def dot(a, b):
    return jnp.dot(a, b, preferred_element_type=f32)


def lanes(x, n, axis):
    return lax.broadcasted_iota(jnp.int32, (x, n), axis)


class Place:
    def __init__(self):
        self.row, self.col = lax.axis_index("row"), lax.axis_index("col")
        self.y = self.row // 2
        self.z = lax.rem(self.row, 2) * 2 + self.col // 8
        self.g = lax.rem(self.col, 8)
        self.x, self.core = self.g // 2, lax.rem(self.g, 2)

    def at(self, y, z, x, core):
        return (y * 2 + z // 2, lax.rem(z, 2) * 8 + x * 2 + core)

    def turn(self, y=0, z=0, x=0):
        y, z, x = lax.rem(self.y + y, 4), lax.rem(self.z + z, 4), lax.rem(self.x + x, 4)
        return y, z, x, self.at(y, z, x, self.core)

    def in_plane(self, off):
        other = lax.rem(self.g + off, 8)
        return other, self.at(self.y, self.z, other // 2, lax.rem(other, 2))

    def in_column(self, off):
        other = lax.rem(self.z * 2 + self.core + off, 8)
        return other // 2, self.at(self.y, other // 2, self.x, lax.rem(other, 2))

    def in_wall(self, off):
        y, z = lax.rem(self.y + off // 4, 4), lax.rem(self.z + off % 4, 4)
        return y, z, self.at(y, z, self.x, self.core)

    def sibling(self):
        return self.at(self.y, self.z, self.x, 1 - self.core)

    def neighbour(self, dr, dc):
        return (lax.rem(self.row + dr + ROWS, ROWS), lax.rem(self.col + dc + COLS, COLS))


def side_ends(place, src, row0, col0, ext):
    ends = []
    for dc in (-1, 1):
        read = col0 if dc < 0 else col0 + W - LEFT
        land = LEFT + W if dc < 0 else 0
        ends.append(
            (
                src.at[pl.ds(row0, H), pl.ds(read, LEFT), :],
                ext.at[pl.ds(R, H), pl.ds(land, LEFT), :],
                place.neighbour(0, dc),
            )
        )
    return ends


def row_ends(place, src, row0, col0, ext, near):
    odd = lax.rem(place.row, 2)
    low = odd if near else 1 - odd
    rows, landing = pl.ds(row0 + (H - R) * (1 - low), R), pl.ds((R + H) * low, R)
    ends = []
    for dc in (0, -1, 1):
        read, land, n = (col0, LEFT, W) if dc == 0 else (col0, LEFT + W, LEFT) if dc < 0 else (col0 + W - LEFT, 0, LEFT)
        ends.append(
            (
                src.at[rows, pl.ds(read, n), :],
                ext.at[landing, pl.ds(land, n), :],
                place.neighbour(1 - 2 * low, dc),
            )
        )
    return ends


def clear_columns(place, ext, b):
    @pl.when(place.col == 0)
    def _():
        ext[b, R : R + H, 0:LEFT] = jnp.zeros((H, LEFT, C), f32)

    @pl.when(place.col == COLS - 1)
    def _():
        ext[b, R : R + H, LEFT + W :] = jnp.zeros((H, LEFT, C), f32)


def clear_rows(place, ext):
    for edge, at in ((0, slice(0, R)), (ROWS - 1, slice(R + H, HE))):

        @pl.when(place.row == edge)
        def _():
            ext[:, at] = jnp.zeros((B, R, WE, C), f32)

        @pl.when(place.col == 0)
        def _():
            ext[:, at, 0:LEFT] = jnp.zeros((B, R, LEFT, C), f32)

        @pl.when(place.col == COLS - 1)
        def _():
            ext[:, at, LEFT + W :] = jnp.zeros((B, R, LEFT, C), f32)


def conv_tile(ext, taps, b, wb, flip, rows, acc):
    for j in range(K):
        tap = [taps[(K - 1 - i) * K + K - 1 - j] if flip else taps[i * K + j] for i in range(K)]
        for e in rows:
            x = ext[b, e, pl.ds(8 * wb + LEFT - R + j, 8), :]
            for i in range(K):
                p = e - i
                if 0 <= p < H:
                    acc[p] = acc[p] + tap[i] * x
    return acc


INNER = range(R, R + H)
OUTER = (*range(R), *range(R + H, HE))
FRINGE = (*range(R), *range(H - R, H))


def kernel_grad_tile(ext, dcv, kacc, b, wb):
    grads = [dcv[b, R + p, pl.ds(pl.multiple_of(8 * wb + LEFT, 8), 8), :] for p in range(H)]
    for j in range(K):
        acc = [kacc[i * K + j] for i in range(K)]
        for e in range(HE):
            x = ext[b, e, pl.ds(8 * wb + LEFT - R + j, 8), :]
            for i in range(K):
                p = e - i
                if 0 <= p < H:
                    acc[i] = acc[i] + grads[p] * x
        for i in range(K):
            kacc[i * K + j] = acc[i]


def widen(column, n):
    one = jnp.broadcast_to(column, (column.shape[0], 128))
    return jnp.concatenate([one] * n, axis=1)


def kernel(
    feat, cot_hbm, taps_in, cb_in, gain_in, shift_in, ob_in, scale_in, ib_in, win_in, wout_in,
    fg_out, small_out, weight_out,
    taps_s, cb_s, gain_s, shift_s, ob_s, scale_s, ib_s, srow,
    src, cot, dcv, mid, fg, sg, wg, taps,
    win2, winlo, wintop, wot2, wotlo, bias_eff,
    nacc, macc, inbacc, kacc, cotacc, dbacc,
    wp, wcore, wa, wr1, wb_, wr2, wc, wr3, rows, sp, srx, sb, sry,
    local, out_sem, sent, arrived,
):
    place = Place()
    y, z, x, core = place.y, place.z, place.x, place.core

    scalars = [(taps_in, taps_s), (cb_in, cb_s), (gain_in, gain_s), (shift_in, shift_s), (ob_in, ob_s), (scale_in, scale_s), (ib_in, ib_s)]
    params = [pltpu.make_async_copy(a, b, local.at[4 + n]) for n, (a, b) in enumerate(scalars)]
    own = [
        pltpu.make_async_copy(feat, src.at[:, pl.ds(R, H), pl.ds(LEFT, W), :], local.at[0]),
        pltpu.make_async_copy(cot_hbm, cot, local.at[1]),
        pltpu.make_async_copy(win_in, wg.at[0, y, z, x, core], local.at[2]),
        pltpu.make_async_copy(wout_in, wg.at[1, y, z, x, core], local.at[3]),
    ]
    for copy in params + own:
        copy.start()

    barrier = pltpu.get_barrier_semaphore()
    partners = [place.neighbour(dr, dc) for dr in (-1, 0, 1) for dc in (-1, 0, 1) if dr or dc]
    partners += [place.in_plane(off)[1] for off in range(1, 8)]
    partners += [place.in_column(off)[1] for off in range(1, 8)]
    partners += [place.in_wall(off)[2] for off in range(1, 16)]
    for partner in partners:
        pl.semaphore_signal(barrier, inc=1, device_id=partner, device_id_type=MESH)

    for copy in params:
        copy.wait()
    lane = lanes(1, 128, 1)
    row = jnp.zeros((1, 128), f32)
    for i in range(K):
        for j in range(K):
            row = jnp.where(lane == TAPS + i * K + j, taps_s[i, 0, j], row)
    for at, ref in ((CB, cb_s), (GAIN, gain_s), (SHIFT, shift_s), (OB, ob_s), (SCALE, scale_s)):
        row = jnp.where(lane == at, ref[0], row)
    for k in range(4):
        row = jnp.where(lane == IB + k, ib_s[k], row)
    srow[...] = row
    sg[y, z, x, core] = row
    kacc[...] = jnp.zeros_like(kacc)
    nacc[...] = jnp.zeros_like(nacc)
    macc[...] = jnp.zeros_like(macc)
    inbacc[...] = jnp.zeros_like(inbacc)
    cotacc[...] = jnp.zeros_like(cotacc)
    dbacc[...] = jnp.zeros_like(dbacc)

    pl.semaphore_wait(barrier, len(partners))

    stages = []

    class Stage:
        def __init__(self, amount, copies):
            self.n = len(stages)
            stages.append(self)
            self.amount = amount
            self.copies = [self.copy(*ends) for ends in copies]

        def copy(self, a, b, partner):
            return pltpu.make_async_remote_copy(
                src_ref=a, dst_ref=b, send_sem=sent.at[self.n], recv_sem=arrived.at[self.n],
                device_id=partner, device_id_type=MESH,
            )

        def start(self):
            for copy in self.copies:
                copy.start()

        def arrive(self):
            self.copy(self.amount, self.amount, place.sibling()).wait_recv()

        def leave(self):
            self.copy(self.amount, self.amount, place.sibling()).wait_send()

    cell = (y, z, x, core)
    plane = [place.in_plane(off)[1] for off in range(1, 8)]
    zs = [place.turn(z=off)[3] for off in range(1, 4)]
    wall = [place.in_wall(off)[2] for off in range(1, 16)]
    xs = [place.turn(x=off)[3] for off in range(1, 4)]
    ys = [place.turn(y=off)[3] for off in range(1, 4)]
    cells = wg.at[0].reshape(128, 4, C)
    s1 = Stage(srx.at[:, 0, 0], [(srow, sg.at[cell], p) for p in plane])
    w1 = Stage(cells.at[pl.ds(0, 3)], [(win_in, wg.at[(0, *cell)], p) for p in zs])
    v1 = Stage(cells.at[pl.ds(0, 3)], [(wout_in, wg.at[(1, *cell)], p) for p in zs])
    s2 = Stage(sg.reshape(128, 1, C).at[pl.ds(0, 120)], [(sg.at[y, z], sg.at[y, z], p) for p in wall])
    part = wg.at[0, y, :, x, core]
    w2 = Stage(cells.at[pl.ds(0, 12)], [(part, part, p) for p in xs])
    other = wg.at[1, y, :, x, core]
    v2 = Stage(cells.at[pl.ds(0, 12)], [(other, other, p) for p in ys])
    layer = wg.at[0, y, :, :, core]
    w3 = Stage(cells.at[pl.ds(0, 48)], [(layer, layer, p) for p in ys])
    slab = wg.at[1, :, :, x, core]
    v3 = Stage(cells.at[pl.ds(0, 48)], [(slab, slab, p) for p in xs])
    lot = wg.at[:, :, :, :, core]
    w4 = Stage(cells, [(lot, lot, place.sibling())])
    def tile_edges(ref, row0, col0, ext):
        sides, nears, fars = [], [], []
        for b in range(B):
            ends = (place, ref.at[b], row0, col0, ext.at[b])
            sides.append(Stage(src.at[b, pl.ds(0, H), pl.ds(0, 2 * LEFT), :], side_ends(*ends)))
            nears.append(Stage(src.at[b, pl.ds(0, R), :, :], row_ends(*ends, True)))
            fars.append(Stage(src.at[b, pl.ds(0, R), :, :], row_ends(*ends, False)))
        return sides, nears, fars

    def start(*stages):
        for stage in stages:
            stage.start()

    def arrive(*stages):
        for stage in stages:
            stage.arrive()

    sides, nears, fars = tile_edges(feat, 0, 0, src)

    s1.start()
    w1.start()
    v1.start()
    start(*sides)
    own[2].wait()
    own[3].wait()
    s1.arrive()
    s2.start()
    w1.arrive()
    w2.start()
    v1.arrive()
    v2.start()
    start(*nears)
    w2.arrive()
    w3.start()
    v2.arrive()
    v3.start()
    start(*fars)
    own[0].wait()
    own[1].wait()
    arrive(*sides)
    clear_columns(place, src, 0)
    clear_columns(place, src, 1)
    s2.arrive()

    small = sg.reshape(128, C)[...]
    small_t = small.T
    for n in range(K * K):
        taps[n] = jnp.broadcast_to(small_t[TAPS + n : TAPS + n + 1, :], (8, C))
    conv_bias = jnp.broadcast_to(small_t[CB : CB + 1, :], (8, C))

    def column_block(n):
        return n // 8, lax.rem(n, 8), pl.ds(pl.multiple_of(lax.rem(n, 8) * 8, 8), 8)

    def conv_step(n, carry):
        b, wb, at = column_block(n)
        acc = conv_tile(src, taps, b, wb, False, INNER, {p: conv_bias for p in range(H)})
        for p in range(H):
            mid[b, p, at, :] = acc[p]
        return carry

    lax.fori_loop(0, LATE, conv_step, 0)
    w3.arrive()
    v3.arrive()
    w4.start()
    lax.fori_loop(LATE, BLOCKS, conv_step, 0)

    def conv_rest(n, carry):
        b, wb, at = column_block(n)
        acc = conv_tile(src, taps, b, wb, False, OUTER, {p: mid[b, p, at, :] for p in FRINGE})
        for p in FRINGE:
            mid[b, p, at, :] = acc[p]
        return carry

    w4.arrive()
    gain_wide, shift_wide = widen(small[:, GAIN : GAIN + 1], 4), widen(small[:, SHIFT : SHIFT + 1], 4)
    scale_wide, ob_wide = widen(small[:, SCALE : SCALE + 1], 4), widen(small[:, OB : OB + 1], 1)
    win_t = wg.at[0].reshape(HID, C)[...]
    win = win_t.T
    wo_t = wg.at[1].reshape(HID, C)[...].T
    hi, lo = split(win * gain_wide)
    win2[0:C, :] = hi
    win2[C:, :] = hi
    winlo[...] = lo
    hi, lo = split(win_t * small_t[GAIN : GAIN + 1, :])
    wintop[:, 0:C] = hi
    wintop[:, C:] = lo
    hi, lo = split(wo_t * scale_wide)
    wot2[0:C, :] = hi
    wot2[C:, :] = hi
    wotlo[...] = lo
    pick = [lanes(32, 128, 1) == 4 * lanes(32, 128, 0) + k for k in range(4)]
    shifted = win * shift_wide
    for t in range(4):
        cut, band = slice(128 * t, 128 * t + 128), slice(32 * t, 32 * t + 32)
        terms = [jnp.where(pick[k], small[band, IB + k : IB + k + 1], 0.0) for k in range(4)]
        bias_eff[:, cut] = jnp.sum(shifted[:, cut], axis=0, keepdims=True) + jnp.sum(sum(terms), axis=0, keepdims=True)

    def mix(b, starts):
        spans = [pl.ds(p, QUARTER) for p in starts]
        x = jnp.concatenate([mid[b, s].reshape(M // 2, C) for s in spans], axis=0)
        ct = jnp.concatenate([cot[b, s].reshape(M // 2, C) for s in spans], axis=0)
        mean = jnp.mean(x, axis=-1, keepdims=True)
        cen = x - mean
        inv = lax.rsqrt(jnp.mean(cen * cen, axis=-1, keepdims=True) + norm_eps)
        normed = cen * inv
        n_hi, n_lo = split(normed)
        n2 = jnp.concatenate([n_hi, n_lo], axis=1)
        c_hi, c_lo = split(ct)
        c2 = jnp.concatenate([c_hi, c_lo], axis=1)
        nt2 = jnp.concatenate(split(normed.T), axis=0)
        ct2 = jnp.concatenate(split(ct.T), axis=0)
        cotacc[...] += jnp.sum(ct.reshape(M // 8, 8, C), axis=0)
        dn = jnp.zeros((M, C), f32)
        step = 256
        for h in range(0, HID, step):
            cut = slice(h, h + step)
            act = dot(n2, win2[:, cut]) + dot(n_hi, winlo[:, cut]) + bias_eff[:, cut]
            dh = dot(c2, wot2[:, cut]) + dot(c_hi, wotlo[:, cut])
            phi = 0.5 * (1.0 + lax.erf(act * inverse_root_two))
            slope = phi + act * jnp.exp(-0.5 * act * act) * inverse_root_twopi
            hid_hi, hid_lo = split(act * phi)
            da = dh * slope
            inbacc[:, cut] += jnp.sum(da.reshape(M // 8, 8, step), axis=0)
            da_hi, da_lo = split(da)
            both = dot(da_hi, wintop[cut, :])
            dn = dn + both[:, 0:C] + both[:, C:] + dot(da_lo, wintop[cut, 0:C])
            both = dot(nt2, da_hi)
            nacc[:, cut] += both[0:C] + both[C:] + dot(nt2[0:C], da_lo)
            both = dot(ct2, hid_hi)
            macc[:, cut] += both[0:C] + both[C:] + dot(ct2[0:C], hid_lo)
        dc = inv * (
            dn
            - jnp.mean(dn, axis=-1, keepdims=True)
            - normed * jnp.mean(dn * normed, axis=-1, keepdims=True)
        )
        dbacc[...] += jnp.sum(dc.reshape(M // 8, 8, C), axis=0)
        for n, p in enumerate(starts):
            part = dc[n * (M // 2) : (n + 1) * (M // 2)]
            dcv[b, pl.ds(R + p, QUARTER), LEFT : LEFT + W, :] = part.reshape(QUARTER, W, C)

    back_sides, back_nears, back_fars = tile_edges(dcv, R, LEFT, dcv)

    def mix_step(n, carry):
        outer = n // 2

        @pl.when(n == 2)
        def _():
            arrive(*nears, *fars)
            clear_rows(place, src)
            lax.fori_loop(0, BLOCKS, conv_rest, 0)

        @pl.when(n == 3)
        def _():
            start(back_fars[0], back_nears[0], back_sides[0])

        mix(lax.rem(n, 2), (QUARTER * (1 - outer), QUARTER * (2 + outer)))
        return carry

    lax.fori_loop(0, 4, mix_step, 0)
    start(back_fars[1], back_nears[1])

    factor = 1.0 / math.sqrt(B * H * W * ROWS * COLS)
    nsum, msum = nacc[...], macc[...]
    inb = jnp.sum(inbacc[...], axis=0, keepdims=True)
    wp[0] = ((nsum * gain_wide + shift_wide * inb) * factor).T.reshape(4, 4, 4, 8, C)
    wp[1] = (msum * (scale_wide * factor)).T.reshape(4, 4, 4, 8, C)
    r0 = Stage(wcore, [(wp.at[1 - core], wcore, place.sibling())])
    r0.start()

    def kgrad_step(n, carry):
        kernel_grad_tile(src, dcv, kacc, n // 8, lax.rem(n, 8))
        return carry

    lax.fori_loop(0, CUT, kgrad_step, 0)
    r0.arrive()
    for a in range(4):
        wa[a] = wp[core, :, :, a] + wcore[:, :, a]
    to3 = [place.in_column(off) for off in range(1, 8)]
    r1 = Stage(wr1, [(wa.at[lax.rem(x + 1 + n, 4)], wr1.at[n], p) for n, p in enumerate(xs)])
    r2 = Stage(wr2, [(wb_.at[lax.rem(y + 1 + n, 4)], wr2.at[n], p) for n, p in enumerate(ys)])
    r3 = Stage(wr3.reshape(8, 8, C).at[pl.ds(0, 7)], [(wc.at[zz], wr3.at[core, z], p) for zz, p in to3])
    r1.start()
    back_sides[1].start()
    lax.fori_loop(CUT, BLOCKS, kgrad_step, 0)

    gain_g = jnp.sum(win * nsum, axis=1, keepdims=True)
    shift_g = jnp.sum(win * inb, axis=1, keepdims=True)
    scale_g = jnp.sum(wo_t * msum, axis=1, keepdims=True)
    for n in range(K * K):
        rows[n : n + 1, :] = jnp.sum(kacc[n], axis=0, keepdims=True)
    rows[K * K : K * K + 1, :] = jnp.sum(dbacc[...], axis=0, keepdims=True)
    rows[K * K + 1 : K * K + 2, :] = jnp.sum(cotacc[...], axis=0, keepdims=True)
    rows[K * K + 2 :, :] = jnp.zeros((128 - K * K - 2, C), f32)
    grads = rows[...].T
    lane = lanes(C, 128, 1)
    cot_wide = widen(grads[:, K * K + 1 : K * K + 2], 1)
    columns = [(GAIN, gain_g), (SHIFT, shift_g), (OB, scale_wide[:, 0:C] * cot_wide), (SCALE, scale_g + ob_wide * cot_wide)]
    for k in range(4):
        terms = [jnp.where(pick[k], inb[:, 128 * t : 128 * t + 128], 0.0) for t in range(4)]
        columns.append((IB + k, jnp.sum(jnp.concatenate(terms, axis=0), axis=1, keepdims=True)))
    for at, column in columns:
        grads = jnp.where(lane == at, column, grads)
    sp.reshape(128, C)[...] = grads * factor
    q1, q2 = [], []
    for off in range(1, 8):
        g, to = place.in_plane(off)
        q1.append((sp.at[:, :, g // 2, lax.rem(g, 2)], srx.at[off - 1], to))
    for off in range(1, 16):
        yy, zz, to = place.in_wall(off)
        q2.append((sb.at[yy, zz], sry.at[off - 1], to))
    q1, q2 = Stage(srx, q1), Stage(sry, q2)
    q1.start()

    back_sides[0].arrive()
    clear_columns(place, dcv, 0)

    def out_step(n, carry):
        b, wb, at = column_block(n)
        acc = conv_tile(dcv, taps, b, wb, True, INNER, {p: cot[b, p, at, :] for p in range(H)})
        for p in range(H):
            fg[b, p, at, :] = acc[p]
        return carry

    def out_rest(n, carry):
        b, wb, at = column_block(n)
        acc = conv_tile(dcv, taps, b, wb, True, OUTER, {p: fg[b, p, at, :] for p in FRINGE})
        for p in FRINGE:
            fg[b, p, at, :] = acc[p]
        return carry

    lax.fori_loop(0, 5, out_step, 0)
    r1.arrive()
    wb_[...] = wa[x] + wr1[0] + wr1[1] + wr1[2]
    r2.start()
    lax.fori_loop(5, 8, out_step, 0)
    q1.arrive()
    total = sp[:, :, x, core]
    for n in range(7):
        total = total + srx[n]
    sb[...] = total
    q2.start()
    back_sides[1].arrive()
    clear_columns(place, dcv, 1)
    lax.fori_loop(8, 13, out_step, 0)
    r2.arrive()
    wc[...] = wb_[y] + wr2[0] + wr2[1] + wr2[2]
    r3.start()
    wr3[core, z] = wc[z]
    lax.fori_loop(13, BLOCKS, out_step, 0)
    arrive(*back_nears, *back_fars)
    clear_rows(place, dcv)
    lax.fori_loop(0, BLOCKS, out_rest, 0)
    put = pltpu.make_async_copy(fg, fg_out, out_sem.at[0])
    put.start()

    for stage in stages:
        if stage not in (r3, q2):
            stage.leave()
    q2.arrive()
    total = sb[y, z]
    for n in range(15):
        total = total + sry[n]
    small_out[...] = total
    r3.arrive()
    for kind in range(2):
        total = wr3[kind, 0] + wr3[kind, 1] + wr3[kind, 2] + wr3[kind, 3]
        weight_out[kind] = jnp.where(core == 0, total[0:4], total[4:8])

    put.wait()
    r3.leave()
    q2.leave()


def deliver(
    fg_in, small_in, weight_in,
    fg_out, taps_out, cb_out, gain_out, shift_out, win_out, ib_out, wout_out, ob_out, scale_out,
    buf, row, weights, taps, cb, gain, shift, ib, ob, scale, sem,
):
    pieces = [(b, pl.ds(h, H // 2)) for b in range(B) for h in range(0, H, H // 2)]
    small = pltpu.make_async_copy(small_in, row, sem.at[8])
    weight = pltpu.make_async_copy(weight_in, weights, sem.at[9])
    gets = [pltpu.make_async_copy(fg_in.at[at], buf.at[at], sem.at[n]) for n, at in enumerate(pieces)]
    puts = [pltpu.make_async_copy(buf.at[at], fg_out.at[at], sem.at[4 + n]) for n, at in enumerate(pieces)]
    for copy in [small, weight] + gets:
        copy.start()
    small.wait()
    for i in range(K):
        for j in range(K):
            taps[i, 0, j] = row[0, TAPS + i * K + j]
    for at, ref in ((CB, cb), (GAIN, gain), (SHIFT, shift), (OB, ob), (SCALE, scale)):
        ref[0] = row[0, at]
    for k in range(4):
        ib[k] = row[0, IB + k]
    ends = [
        (taps, taps_out), (cb, cb_out), (gain, gain_out), (shift, shift_out), (ob, ob_out), (scale, scale_out),
        (ib, ib_out), (weights.at[0], win_out), (weights.at[1], wout_out),
    ]
    weight.wait()
    rest = [pltpu.make_async_copy(a, b, sem.at[10 + n]) for n, (a, b) in enumerate(ends)]
    for copy in rest:
        copy.start()
    for get, put in zip(gets, puts):
        get.wait()
        put.start()
    for copy in rest + puts:
        copy.wait()


def per_device(
    features, cotangent, conv_kernel, conv_bias, norm_gain, norm_shift,
    w_in, in_bias, w_out, out_bias, layer_scale,
):
    vmem = lambda *shape: pltpu.VMEM(shape, f32)
    smem = lambda *shape: pltpu.SMEM(shape, f32)
    half = lambda *shape: pltpu.VMEM(shape, bf16)
    dma = lambda n: pltpu.SemaphoreType.DMA((n,))
    out = lambda *shape: jax.ShapeDtypeStruct(shape, f32)
    anywhere = pl.BlockSpec(memory_space=pl.ANY)
    inside = pl.BlockSpec(memory_space=pltpu.VMEM)
    tile = (B, H, W, C)
    fg, small, weights = pl.pallas_call(
        kernel,
        out_shape=(out(*tile), out(1, C), out(2, 4, C)),
        in_specs=[anywhere] * 11,
        out_specs=(anywhere, inside, inside),
        scratch_shapes=[
            smem(K, 1, K), smem(1), smem(1), smem(1), smem(1), smem(1), smem(4), vmem(1, C),
            vmem(B, HE, WE, C), vmem(*tile), vmem(B, HE, WE, C), vmem(*tile), vmem(*tile),
            vmem(4, 4, 4, 2, 1, C), vmem(2, 4, 4, 4, 2, 4, C), vmem(K * K, 8, C),
            half(2 * C, HID), half(C, HID), half(HID, 2 * C), half(2 * C, HID), half(C, HID), vmem(1, HID),
            vmem(C, HID), vmem(C, HID), vmem(8, HID), vmem(K * K, 8, C), vmem(8, C), vmem(8, C),
            vmem(2, 4, 4, 4, 8, C), vmem(4, 4, 4, 8, C), vmem(4, 4, 4, 8, C), vmem(3, 4, 4, 8, C),
            vmem(4, 4, 8, C), vmem(3, 4, 8, C), vmem(4, 8, C), vmem(2, 4, 8, C),
            vmem(128, C), vmem(4, 4, 4, 2, 1, C), vmem(7, 4, 4, 1, C), vmem(4, 4, 1, C), vmem(15, 1, C),
            dma(11), dma(1), dma(27), dma(27),
        ],
        compiler_params=pltpu.CompilerParams(
            collective_id=0, has_side_effects=True, vmem_limit_bytes=56 * 2**20
        ),
    )(
        features, cotangent, conv_kernel.transpose(0, 2, 1), conv_bias, norm_gain, norm_shift,
        out_bias, layer_scale, in_bias, w_in.T, w_out,
    )
    fg, taps_g, cb_g, gain_g, shift_g, win_g, ib_g, wout_g, ob_g, scale_g = pl.pallas_call(
        deliver,
        out_shape=(
            out(*tile), out(K, 1, K), out(1), out(1), out(1), out(4, C), out(4), out(4, C), out(1), out(1),
        ),
        in_specs=[anywhere] * 3,
        out_specs=(anywhere,) * 10,
        scratch_shapes=[
            vmem(*tile), smem(1, C), vmem(2, 4, C), smem(K, 1, K), smem(1), smem(1), smem(1), smem(4), smem(1), smem(1), dma(19),
        ],
    )(fg, small, weights)
    return fg, taps_g.transpose(0, 2, 1), cb_g, gain_g, shift_g, win_g.T, ib_g, wout_g, ob_g, scale_g


def solution(mesh):
    both = ("row", "col")
    tile = P(None, "row", "col", None)
    taps, vector = P(None, None, both), P(both)
    return jax.shard_map(
        per_device,
        mesh=mesh,
        in_specs=(tile, tile, taps, vector, vector, vector, P(None, both), vector, P(both, None), vector, vector),
        out_specs=(tile, taps, vector, vector, vector, P(None, both), vector, P(both, None), vector, vector),
        check_vma=False,
    )
```

```python
import functools
import math

import jax
import jax.numpy as jnp
from jax import lax
from jax.experimental import pallas as pl
from jax.experimental.pallas import tpu as pltpu
from jax.sharding import PartitionSpec as P

norm_eps = 1e-06
inverse_root_two = 0.7071067811865476
inverse_root_twopi = 0.3989422804014327
MESH = pl.DeviceIdType.MESH
f32, bf16 = jnp.float32, jnp.bfloat16

K, R = 7, 3
C, HID = 128, 512
B, H, W = 2, 16, 64
LEFT = 8
WE = W + 2 * LEFT
HE = H + 2 * R
ROWS, COLS = 8, 16
QUARTER = H // 4
BLOCKS = B * W // 8
CUT = BLOCKS // 2 + 1
LATE = BLOCKS - 5
M = 2 * QUARTER * W
TAPS, CB, GAIN, SHIFT, OB, SCALE, IB = 0, 49, 50, 51, 52, 53, 54


def split(x):
    hi = x.astype(bf16)
    return hi, (x - hi.astype(f32)).astype(bf16)


def dot(a, b):
    return jnp.dot(a, b, preferred_element_type=f32)


def lanes(x, n, axis):
    return lax.broadcasted_iota(jnp.int32, (x, n), axis)


class Place:
    def __init__(self):
        self.row, self.col = lax.axis_index("row"), lax.axis_index("col")
        self.y = self.row // 2
        self.z = lax.rem(self.row, 2) * 2 + self.col // 8
        self.g = lax.rem(self.col, 8)
        self.x, self.core = self.g // 2, lax.rem(self.g, 2)

    def at(self, y, z, x, core):
        return (y * 2 + z // 2, lax.rem(z, 2) * 8 + x * 2 + core)

    def turn(self, y=0, z=0, x=0):
        y, z, x = lax.rem(self.y + y, 4), lax.rem(self.z + z, 4), lax.rem(self.x + x, 4)
        return y, z, x, self.at(y, z, x, self.core)

    def in_plane(self, off):
        other = lax.rem(self.g + off, 8)
        return other, self.at(self.y, self.z, other // 2, lax.rem(other, 2))

    def in_slab(self, off):
        y, z = lax.rem(self.y + off // 8, 4), lax.rem(self.z + off // 2 % 4, 4)
        return y, z, self.at(y, z, self.x, lax.rem(self.core + off, 2))

    def in_wall(self, off):
        y, z = lax.rem(self.y + off // 4, 4), lax.rem(self.z + off % 4, 4)
        return y, z, self.at(y, z, self.x, self.core)

    def sibling(self):
        return self.at(self.y, self.z, self.x, 1 - self.core)

    def neighbour(self, dr, dc):
        return (lax.rem(self.row + dr + ROWS, ROWS), lax.rem(self.col + dc + COLS, COLS))


def side_ends(place, src, row0, col0, ext):
    ends = []
    for dc in (-1, 1):
        read = col0 if dc < 0 else col0 + W - LEFT
        land = LEFT + W if dc < 0 else 0
        ends.append(
            (
                src.at[pl.ds(row0, H), pl.ds(read, LEFT), :],
                ext.at[pl.ds(R, H), pl.ds(land, LEFT), :],
                place.neighbour(0, dc),
            )
        )
    return ends


def row_ends(place, src, row0, col0, ext, near):
    odd = lax.rem(place.row, 2)
    low = odd if near else 1 - odd
    rows, landing = pl.ds(row0 + (H - R) * (1 - low), R), pl.ds((R + H) * low, R)
    ends = []
    for dc in (0, -1, 1):
        read, land, n = (col0, LEFT, W) if dc == 0 else (col0, LEFT + W, LEFT) if dc < 0 else (col0 + W - LEFT, 0, LEFT)
        ends.append(
            (
                src.at[rows, pl.ds(read, n), :],
                ext.at[landing, pl.ds(land, n), :],
                place.neighbour(1 - 2 * low, dc),
            )
        )
    return ends


def clear_columns(place, ext, b):
    @pl.when(place.col == 0)
    def _():
        ext[b, R : R + H, 0:LEFT] = jnp.zeros((H, LEFT, C), f32)

    @pl.when(place.col == COLS - 1)
    def _():
        ext[b, R : R + H, LEFT + W :] = jnp.zeros((H, LEFT, C), f32)


def clear_rows(place, ext):
    for edge, at in ((0, slice(0, R)), (ROWS - 1, slice(R + H, HE))):

        @pl.when(place.row == edge)
        def _():
            ext[:, at] = jnp.zeros((B, R, WE, C), f32)

        @pl.when(place.col == 0)
        def _():
            ext[:, at, 0:LEFT] = jnp.zeros((B, R, LEFT, C), f32)

        @pl.when(place.col == COLS - 1)
        def _():
            ext[:, at, LEFT + W :] = jnp.zeros((B, R, LEFT, C), f32)


def conv_tile(ext, taps, b, wb, flip, rows, acc):
    for j in range(K):
        tap = [taps[(K - 1 - i) * K + K - 1 - j] if flip else taps[i * K + j] for i in range(K)]
        for e in rows:
            x = ext[b, e, pl.ds(8 * wb + LEFT - R + j, 8), :]
            for i in range(K):
                p = e - i
                if 0 <= p < H:
                    acc[p] = acc[p] + tap[i] * x
    return acc


INNER = range(R, R + H)
OUTER = (*range(R), *range(R + H, HE))
FRINGE = (*range(R), *range(H - R, H))


def kernel_grad_tile(ext, dcv, kacc, b, wb):
    grads = [dcv[b, R + p, pl.ds(pl.multiple_of(8 * wb + LEFT, 8), 8), :] for p in range(H)]
    for j in range(K):
        acc = [kacc[i * K + j] for i in range(K)]
        for e in range(HE):
            x = ext[b, e, pl.ds(8 * wb + LEFT - R + j, 8), :]
            for i in range(K):
                p = e - i
                if 0 <= p < H:
                    acc[i] = acc[i] + grads[p] * x
        for i in range(K):
            kacc[i * K + j] = acc[i]


def widen(column, n):
    one = jnp.broadcast_to(column, (column.shape[0], 128))
    return jnp.concatenate([one] * n, axis=1)


def kernel(
    feat, cot_hbm, taps_in, cb_in, gain_in, shift_in, ob_in, scale_in, ib_in, win_in, wout_in,
    fg_out, small_out, weight_out,
    taps_s, cb_s, gain_s, shift_s, ob_s, scale_s, ib_s, srow,
    src, cot, dcv, mid, fg, sg, wg, taps,
    win2, winlo, wintop, wot2, wotlo, bias_eff,
    nacc, macc, inbacc, kacc, cotacc, dbacc,
    wp, wcore, wa, wr1, wb_, wr2, rows, sp, srx, sb, sry,
    local, out_sem, sent, arrived,
):
    place = Place()
    y, z, x, core = place.y, place.z, place.x, place.core

    scalars = [(taps_in, taps_s), (cb_in, cb_s), (gain_in, gain_s), (shift_in, shift_s), (ob_in, ob_s), (scale_in, scale_s), (ib_in, ib_s)]
    params = [pltpu.make_async_copy(a, b, local.at[4 + n]) for n, (a, b) in enumerate(scalars)]
    own = [
        pltpu.make_async_copy(feat, src.at[:, pl.ds(R, H), pl.ds(LEFT, W), :], local.at[0]),
        pltpu.make_async_copy(cot_hbm, cot, local.at[1]),
        pltpu.make_async_copy(win_in, wg.at[0, y, z, x, core], local.at[2]),
        pltpu.make_async_copy(wout_in, wg.at[1, y, z, x, core], local.at[3]),
    ]
    for copy in params + own:
        copy.start()

    barrier = pltpu.get_barrier_semaphore()
    partners = [place.neighbour(dr, dc) for dr in (-1, 0, 1) for dc in (-1, 0, 1) if dr or dc]
    partners += [place.in_plane(off)[1] for off in range(1, 8)]
    partners += [place.in_slab(off)[2] for off in range(1, 32)]
    for partner in partners:
        pl.semaphore_signal(barrier, inc=1, device_id=partner, device_id_type=MESH)

    for copy in params:
        copy.wait()
    lane = lanes(1, 128, 1)
    row = jnp.zeros((1, 128), f32)
    for i in range(K):
        for j in range(K):
            row = jnp.where(lane == TAPS + i * K + j, taps_s[i, 0, j], row)
    for at, ref in ((CB, cb_s), (GAIN, gain_s), (SHIFT, shift_s), (OB, ob_s), (SCALE, scale_s)):
        row = jnp.where(lane == at, ref[0], row)
    for k in range(4):
        row = jnp.where(lane == IB + k, ib_s[k], row)
    srow[...] = row
    sg[y, z, x, core] = row
    kacc[...] = jnp.zeros_like(kacc)
    nacc[...] = jnp.zeros_like(nacc)
    macc[...] = jnp.zeros_like(macc)
    inbacc[...] = jnp.zeros_like(inbacc)
    cotacc[...] = jnp.zeros_like(cotacc)
    dbacc[...] = jnp.zeros_like(dbacc)

    pl.semaphore_wait(barrier, len(partners))

    stages = []

    class Stage:
        def __init__(self, amount, copies):
            self.n = len(stages)
            stages.append(self)
            self.amount = amount
            self.copies = [self.copy(*ends) for ends in copies]

        def copy(self, a, b, partner):
            return pltpu.make_async_remote_copy(
                src_ref=a, dst_ref=b, send_sem=sent.at[self.n], recv_sem=arrived.at[self.n],
                device_id=partner, device_id_type=MESH,
            )

        def start(self):
            for copy in self.copies:
                copy.start()

        def arrive(self):
            self.copy(self.amount, self.amount, place.sibling()).wait_recv()

        def leave(self):
            self.copy(self.amount, self.amount, place.sibling()).wait_send()

    cell = (y, z, x, core)
    plane = [place.in_plane(off)[1] for off in range(1, 8)]
    zs = [place.turn(z=off)[3] for off in range(1, 4)]
    wall = [place.in_wall(off)[2] for off in range(1, 16)]
    xs = [place.turn(x=off)[3] for off in range(1, 4)]
    ys = [place.turn(y=off)[3] for off in range(1, 4)]
    cells = wg.at[0].reshape(128, 4, C)
    s1 = Stage(srx.at[:, 0, 0], [(srow, sg.at[cell], p) for p in plane])
    w1 = Stage(cells.at[pl.ds(0, 3)], [(win_in, wg.at[(0, *cell)], p) for p in zs])
    v1 = Stage(cells.at[pl.ds(0, 3)], [(wout_in, wg.at[(1, *cell)], p) for p in zs])
    s2 = Stage(sg.reshape(128, 1, C).at[pl.ds(0, 120)], [(sg.at[y, z], sg.at[y, z], p) for p in wall])
    part = wg.at[0, y, :, x, core]
    w2 = Stage(cells.at[pl.ds(0, 12)], [(part, part, p) for p in xs])
    other = wg.at[1, y, :, x, core]
    v2 = Stage(cells.at[pl.ds(0, 12)], [(other, other, p) for p in ys])
    layer = wg.at[0, y, :, :, core]
    w3 = Stage(cells.at[pl.ds(0, 48)], [(layer, layer, p) for p in ys])
    slab = wg.at[1, :, :, x, core]
    v3 = Stage(cells.at[pl.ds(0, 48)], [(slab, slab, p) for p in xs])
    lot = wg.at[:, :, :, :, core]
    w4 = Stage(cells, [(lot, lot, place.sibling())])
    def tile_edges(ref, row0, col0, ext):
        sides, nears, fars = [], [], []
        for b in range(B):
            ends = (place, ref.at[b], row0, col0, ext.at[b])
            sides.append(Stage(src.at[b, pl.ds(0, H), pl.ds(0, 2 * LEFT), :], side_ends(*ends)))
            nears.append(Stage(src.at[b, pl.ds(0, R), :, :], row_ends(*ends, True)))
            fars.append(Stage(src.at[b, pl.ds(0, R), :, :], row_ends(*ends, False)))
        return sides, nears, fars

    def start(*stages):
        for stage in stages:
            stage.start()

    def arrive(*stages):
        for stage in stages:
            stage.arrive()

    sides, nears, fars = tile_edges(feat, 0, 0, src)

    s1.start()
    w1.start()
    v1.start()
    start(*sides)
    own[2].wait()
    own[3].wait()
    s1.arrive()
    s2.start()
    w1.arrive()
    w2.start()
    v1.arrive()
    v2.start()
    start(*nears)
    w2.arrive()
    w3.start()
    v2.arrive()
    v3.start()
    start(*fars)
    own[0].wait()
    own[1].wait()
    arrive(*sides)
    clear_columns(place, src, 0)
    clear_columns(place, src, 1)
    s2.arrive()

    small = sg.reshape(128, C)[...]
    small_t = small.T
    for n in range(K * K):
        taps[n] = jnp.broadcast_to(small_t[TAPS + n : TAPS + n + 1, :], (8, C))
    conv_bias = jnp.broadcast_to(small_t[CB : CB + 1, :], (8, C))

    def column_block(n):
        return n // 8, lax.rem(n, 8), pl.ds(pl.multiple_of(lax.rem(n, 8) * 8, 8), 8)

    def conv_step(n, carry):
        b, wb, at = column_block(n)
        acc = conv_tile(src, taps, b, wb, False, INNER, {p: conv_bias for p in range(H)})
        for p in range(H):
            mid[b, p, at, :] = acc[p]
        return carry

    lax.fori_loop(0, LATE, conv_step, 0)
    w3.arrive()
    v3.arrive()
    w4.start()
    lax.fori_loop(LATE, BLOCKS, conv_step, 0)

    def conv_rest(n, carry):
        b, wb, at = column_block(n)
        acc = conv_tile(src, taps, b, wb, False, OUTER, {p: mid[b, p, at, :] for p in FRINGE})
        for p in FRINGE:
            mid[b, p, at, :] = acc[p]
        return carry

    w4.arrive()
    gain_wide, shift_wide = widen(small[:, GAIN : GAIN + 1], 4), widen(small[:, SHIFT : SHIFT + 1], 4)
    scale_wide, ob_wide = widen(small[:, SCALE : SCALE + 1], 4), widen(small[:, OB : OB + 1], 1)
    win_t = wg.at[0].reshape(HID, C)[...]
    win = win_t.T
    wo_t = wg.at[1].reshape(HID, C)[...].T
    hi, lo = split(win * gain_wide)
    win2[0:C, :] = hi
    win2[C:, :] = hi
    winlo[...] = lo
    hi, lo = split(win_t * small_t[GAIN : GAIN + 1, :])
    wintop[:, 0:C] = hi
    wintop[:, C:] = lo
    hi, lo = split(wo_t * scale_wide)
    wot2[0:C, :] = hi
    wot2[C:, :] = hi
    wotlo[...] = lo
    pick = [lanes(32, 128, 1) == 4 * lanes(32, 128, 0) + k for k in range(4)]
    shifted = win * shift_wide
    for t in range(4):
        cut, band = slice(128 * t, 128 * t + 128), slice(32 * t, 32 * t + 32)
        terms = [jnp.where(pick[k], small[band, IB + k : IB + k + 1], 0.0) for k in range(4)]
        bias_eff[:, cut] = jnp.sum(shifted[:, cut], axis=0, keepdims=True) + jnp.sum(sum(terms), axis=0, keepdims=True)

    def mix(b, starts):
        spans = [pl.ds(p, QUARTER) for p in starts]
        x = jnp.concatenate([mid[b, s].reshape(M // 2, C) for s in spans], axis=0)
        ct = jnp.concatenate([cot[b, s].reshape(M // 2, C) for s in spans], axis=0)
        mean = jnp.mean(x, axis=-1, keepdims=True)
        cen = x - mean
        inv = lax.rsqrt(jnp.mean(cen * cen, axis=-1, keepdims=True) + norm_eps)
        normed = cen * inv
        n_hi, n_lo = split(normed)
        n2 = jnp.concatenate([n_hi, n_lo], axis=1)
        c_hi, c_lo = split(ct)
        c2 = jnp.concatenate([c_hi, c_lo], axis=1)
        nt2 = jnp.concatenate(split(normed.T), axis=0)
        ct2 = jnp.concatenate(split(ct.T), axis=0)
        cotacc[...] += jnp.sum(ct.reshape(M // 8, 8, C), axis=0)
        dn = jnp.zeros((M, C), f32)
        step = 256
        for h in range(0, HID, step):
            cut = slice(h, h + step)
            act = dot(n2, win2[:, cut]) + dot(n_hi, winlo[:, cut]) + bias_eff[:, cut]
            dh = dot(c2, wot2[:, cut]) + dot(c_hi, wotlo[:, cut])
            phi = 0.5 * (1.0 + lax.erf(act * inverse_root_two))
            slope = phi + act * jnp.exp(-0.5 * act * act) * inverse_root_twopi
            hid_hi, hid_lo = split(act * phi)
            da = dh * slope
            inbacc[:, cut] += jnp.sum(da.reshape(M // 8, 8, step), axis=0)
            da_hi, da_lo = split(da)
            both = dot(da_hi, wintop[cut, :])
            dn = dn + both[:, 0:C] + both[:, C:] + dot(da_lo, wintop[cut, 0:C])
            both = dot(nt2, da_hi)
            nacc[:, cut] += both[0:C] + both[C:] + dot(nt2[0:C], da_lo)
            both = dot(ct2, hid_hi)
            macc[:, cut] += both[0:C] + both[C:] + dot(ct2[0:C], hid_lo)
        dc = inv * (
            dn
            - jnp.mean(dn, axis=-1, keepdims=True)
            - normed * jnp.mean(dn * normed, axis=-1, keepdims=True)
        )
        dbacc[...] += jnp.sum(dc.reshape(M // 8, 8, C), axis=0)
        for n, p in enumerate(starts):
            part = dc[n * (M // 2) : (n + 1) * (M // 2)]
            dcv[b, pl.ds(R + p, QUARTER), LEFT : LEFT + W, :] = part.reshape(QUARTER, W, C)

    back_sides, back_nears, back_fars = tile_edges(dcv, R, LEFT, dcv)

    def mix_step(n, carry):
        outer = n // 2

        @pl.when(n == 2)
        def _():
            arrive(*nears, *fars)
            clear_rows(place, src)
            lax.fori_loop(0, BLOCKS, conv_rest, 0)

        @pl.when(n == 3)
        def _():
            start(back_fars[0], back_nears[0], back_sides[0])

        mix(lax.rem(n, 2), (QUARTER * (1 - outer), QUARTER * (2 + outer)))
        return carry

    lax.fori_loop(0, 4, mix_step, 0)
    start(back_fars[1], back_nears[1])

    factor = 1.0 / math.sqrt(B * H * W * ROWS * COLS)
    nsum, msum = nacc[...], macc[...]
    inb = jnp.sum(inbacc[...], axis=0, keepdims=True)
    wp[0] = ((nsum * gain_wide + shift_wide * inb) * factor).T.reshape(4, 4, 4, 8, C)
    wp[1] = (msum * (scale_wide * factor)).T.reshape(4, 4, 4, 8, C)
    r0 = Stage(wcore, [(wp.at[1 - core], wcore, place.sibling())])
    r0.start()

    def kgrad_step(n, carry):
        kernel_grad_tile(src, dcv, kacc, n // 8, lax.rem(n, 8))
        return carry

    lax.fori_loop(0, CUT, kgrad_step, 0)
    r0.arrive()
    for a in range(4):
        wa[a] = wp[core, :, :, a] + wcore[:, :, a]
    slab = [place.in_slab(off) for off in range(1, 32)]
    r1 = Stage(wr1, [(wa.at[lax.rem(x + 1 + n, 4)], wr1.at[n], p) for n, p in enumerate(xs)])
    r2 = Stage(wr2.reshape(32, 8, C).at[pl.ds(0, 31)], [(wb_.at[yy, zz], wr2.at[core, y, z], p) for yy, zz, p in slab])
    r1.start()
    back_sides[1].start()
    lax.fori_loop(CUT, BLOCKS, kgrad_step, 0)

    gain_g = jnp.sum(win * nsum, axis=1, keepdims=True)
    shift_g = jnp.sum(win * inb, axis=1, keepdims=True)
    scale_g = jnp.sum(wo_t * msum, axis=1, keepdims=True)
    for n in range(K * K):
        rows[n : n + 1, :] = jnp.sum(kacc[n], axis=0, keepdims=True)
    rows[K * K : K * K + 1, :] = jnp.sum(dbacc[...], axis=0, keepdims=True)
    rows[K * K + 1 : K * K + 2, :] = jnp.sum(cotacc[...], axis=0, keepdims=True)
    rows[K * K + 2 :, :] = jnp.zeros((128 - K * K - 2, C), f32)
    grads = rows[...].T
    lane = lanes(C, 128, 1)
    cot_wide = widen(grads[:, K * K + 1 : K * K + 2], 1)
    columns = [(GAIN, gain_g), (SHIFT, shift_g), (OB, scale_wide[:, 0:C] * cot_wide), (SCALE, scale_g + ob_wide * cot_wide)]
    for k in range(4):
        terms = [jnp.where(pick[k], inb[:, 128 * t : 128 * t + 128], 0.0) for t in range(4)]
        columns.append((IB + k, jnp.sum(jnp.concatenate(terms, axis=0), axis=1, keepdims=True)))
    for at, column in columns:
        grads = jnp.where(lane == at, column, grads)
    sp.reshape(128, C)[...] = grads * factor
    q1, q2 = [], []
    for off in range(1, 8):
        g, to = place.in_plane(off)
        q1.append((sp.at[:, :, g // 2, lax.rem(g, 2)], srx.at[off - 1], to))
    for off in range(1, 16):
        yy, zz, to = place.in_wall(off)
        q2.append((sb.at[yy, zz], sry.at[off - 1], to))
    q1, q2 = Stage(srx, q1), Stage(sry, q2)
    q1.start()

    back_sides[0].arrive()
    clear_columns(place, dcv, 0)

    def out_step(n, carry):
        b, wb, at = column_block(n)
        acc = conv_tile(dcv, taps, b, wb, True, INNER, {p: cot[b, p, at, :] for p in range(H)})
        for p in range(H):
            fg[b, p, at, :] = acc[p]
        return carry

    def out_rest(n, carry):
        b, wb, at = column_block(n)
        acc = conv_tile(dcv, taps, b, wb, True, OUTER, {p: fg[b, p, at, :] for p in FRINGE})
        for p in FRINGE:
            fg[b, p, at, :] = acc[p]
        return carry

    lax.fori_loop(0, 5, out_step, 0)
    r1.arrive()
    wb_[...] = wa[x] + wr1[0] + wr1[1] + wr1[2]
    r2.start()
    wr2[core, y, z] = wb_[y, z]
    lax.fori_loop(5, 8, out_step, 0)
    q1.arrive()
    total = sp[:, :, x, core]
    for n in range(7):
        total = total + srx[n]
    sb[...] = total
    q2.start()
    back_sides[1].arrive()
    clear_columns(place, dcv, 1)
    lax.fori_loop(8, BLOCKS, out_step, 0)
    arrive(*back_nears, *back_fars)
    clear_rows(place, dcv)
    lax.fori_loop(0, BLOCKS, out_rest, 0)
    put = pltpu.make_async_copy(fg, fg_out, out_sem.at[0])
    put.start()

    for stage in stages:
        if stage not in (r2, q2):
            stage.leave()
    q2.arrive()
    total = sb[y, z]
    for n in range(15):
        total = total + sry[n]
    small_out[...] = total
    r2.arrive()
    for kind in range(2):
        total = wr2[kind, 0, 0]
        for n in range(1, 16):
            total = total + wr2[kind, n // 4, n % 4]
        weight_out[kind] = jnp.where(core == 0, total[0:4], total[4:8])

    put.wait()
    r2.leave()
    q2.leave()


def deliver(
    fg_in, small_in, weight_in,
    fg_out, taps_out, cb_out, gain_out, shift_out, win_out, ib_out, wout_out, ob_out, scale_out,
    buf, row, weights, taps, cb, gain, shift, ib, ob, scale, sem,
):
    pieces = [(b, pl.ds(h, H // 2)) for b in range(B) for h in range(0, H, H // 2)]
    small = pltpu.make_async_copy(small_in, row, sem.at[8])
    weight = pltpu.make_async_copy(weight_in, weights, sem.at[9])
    gets = [pltpu.make_async_copy(fg_in.at[at], buf.at[at], sem.at[n]) for n, at in enumerate(pieces)]
    puts = [pltpu.make_async_copy(buf.at[at], fg_out.at[at], sem.at[4 + n]) for n, at in enumerate(pieces)]
    for copy in [small, weight] + gets:
        copy.start()
    small.wait()
    for i in range(K):
        for j in range(K):
            taps[i, 0, j] = row[0, TAPS + i * K + j]
    for at, ref in ((CB, cb), (GAIN, gain), (SHIFT, shift), (OB, ob), (SCALE, scale)):
        ref[0] = row[0, at]
    for k in range(4):
        ib[k] = row[0, IB + k]
    ends = [
        (taps, taps_out), (cb, cb_out), (gain, gain_out), (shift, shift_out), (ob, ob_out), (scale, scale_out),
        (ib, ib_out), (weights.at[0], win_out), (weights.at[1], wout_out),
    ]
    weight.wait()
    rest = [pltpu.make_async_copy(a, b, sem.at[10 + n]) for n, (a, b) in enumerate(ends)]
    for copy in rest:
        copy.start()
    for get, put in zip(gets, puts):
        get.wait()
        put.start()
    for copy in rest + puts:
        copy.wait()


def per_device(
    features, cotangent, conv_kernel, conv_bias, norm_gain, norm_shift,
    w_in, in_bias, w_out, out_bias, layer_scale,
):
    vmem = lambda *shape: pltpu.VMEM(shape, f32)
    smem = lambda *shape: pltpu.SMEM(shape, f32)
    half = lambda *shape: pltpu.VMEM(shape, bf16)
    dma = lambda n: pltpu.SemaphoreType.DMA((n,))
    out = lambda *shape: jax.ShapeDtypeStruct(shape, f32)
    anywhere = pl.BlockSpec(memory_space=pl.ANY)
    inside = pl.BlockSpec(memory_space=pltpu.VMEM)
    tile = (B, H, W, C)
    fg, small, weights = pl.pallas_call(
        kernel,
        out_shape=(out(*tile), out(1, C), out(2, 4, C)),
        in_specs=[anywhere] * 11,
        out_specs=(anywhere, inside, inside),
        scratch_shapes=[
            smem(K, 1, K), smem(1), smem(1), smem(1), smem(1), smem(1), smem(4), vmem(1, C),
            vmem(B, HE, WE, C), vmem(*tile), vmem(B, HE, WE, C), vmem(*tile), vmem(*tile),
            vmem(4, 4, 4, 2, 1, C), vmem(2, 4, 4, 4, 2, 4, C), vmem(K * K, 8, C),
            half(2 * C, HID), half(C, HID), half(HID, 2 * C), half(2 * C, HID), half(C, HID), vmem(1, HID),
            vmem(C, HID), vmem(C, HID), vmem(8, HID), vmem(K * K, 8, C), vmem(8, C), vmem(8, C),
            vmem(2, 4, 4, 4, 8, C), vmem(4, 4, 4, 8, C), vmem(4, 4, 4, 8, C), vmem(3, 4, 4, 8, C),
            vmem(4, 4, 8, C), vmem(2, 4, 4, 8, C),
            vmem(128, C), vmem(4, 4, 4, 2, 1, C), vmem(7, 4, 4, 1, C), vmem(4, 4, 1, C), vmem(15, 1, C),
            dma(11), dma(1), dma(26), dma(26),
        ],
        compiler_params=pltpu.CompilerParams(
            collective_id=0, has_side_effects=True, vmem_limit_bytes=56 * 2**20
        ),
    )(
        features, cotangent, conv_kernel.transpose(0, 2, 1), conv_bias, norm_gain, norm_shift,
        out_bias, layer_scale, in_bias, w_in.T, w_out,
    )
    fg, taps_g, cb_g, gain_g, shift_g, win_g, ib_g, wout_g, ob_g, scale_g = pl.pallas_call(
        deliver,
        out_shape=(
            out(*tile), out(K, 1, K), out(1), out(1), out(1), out(4, C), out(4), out(4, C), out(1), out(1),
        ),
        in_specs=[anywhere] * 3,
        out_specs=(anywhere,) * 10,
        scratch_shapes=[
            vmem(*tile), smem(1, C), vmem(2, 4, C), smem(K, 1, K), smem(1), smem(1), smem(1), smem(4), smem(1), smem(1), dma(19),
        ],
    )(fg, small, weights)
    return fg, taps_g.transpose(0, 2, 1), cb_g, gain_g, shift_g, win_g.T, ib_g, wout_g, ob_g, scale_g


def solution(mesh):
    both = ("row", "col")
    tile = P(None, "row", "col", None)
    taps, vector = P(None, None, both), P(both)
    return jax.shard_map(
        per_device,
        mesh=mesh,
        in_specs=(tile, tile, taps, vector, vector, vector, P(None, both), vector, P(both, None), vector, vector),
        out_specs=(tile, taps, vector, vector, vector, P(None, both), vector, P(both, None), vector, vector),
        check_vma=False,
    )
```

```python
import functools
import math

import jax
import jax.numpy as jnp
from jax import lax
from jax.experimental import pallas as pl
from jax.experimental.pallas import tpu as pltpu
from jax.sharding import PartitionSpec as P

norm_eps = 1e-06
inverse_root_two = 0.7071067811865476
inverse_root_twopi = 0.3989422804014327
MESH = pl.DeviceIdType.MESH
f32, bf16 = jnp.float32, jnp.bfloat16

K, R = 7, 3
C, HID = 128, 512
B, H, W = 2, 16, 64
LEFT = 8
WE = W + 2 * LEFT
HE = H + 2 * R
ROWS, COLS = 8, 16
QUARTER = H // 4
BLOCKS = B * W // 8
CUT = BLOCKS // 2 - 2
LATE = BLOCKS - 5
M = 2 * QUARTER * W
TAPS, CB, GAIN, SHIFT, OB, SCALE, IB = 0, 49, 50, 51, 52, 53, 54


def split(x):
    hi = x.astype(bf16)
    return hi, (x - hi.astype(f32)).astype(bf16)


def dot(a, b):
    return jnp.dot(a, b, preferred_element_type=f32)


def lanes(x, n, axis):
    return lax.broadcasted_iota(jnp.int32, (x, n), axis)


class Place:
    def __init__(self):
        self.row, self.col = lax.axis_index("row"), lax.axis_index("col")
        self.y = self.row // 2
        self.z = lax.rem(self.row, 2) * 2 + self.col // 8
        self.g = lax.rem(self.col, 8)
        self.x, self.core = self.g // 2, lax.rem(self.g, 2)

    def at(self, y, z, x, core):
        return (y * 2 + z // 2, lax.rem(z, 2) * 8 + x * 2 + core)

    def turn(self, y=0, z=0, x=0):
        y, z, x = lax.rem(self.y + y, 4), lax.rem(self.z + z, 4), lax.rem(self.x + x, 4)
        return y, z, x, self.at(y, z, x, self.core)

    def in_plane(self, off):
        other = lax.rem(self.g + off, 8)
        return other, self.at(self.y, self.z, other // 2, lax.rem(other, 2))

    def in_slab(self, off):
        y, z = lax.rem(self.y + off // 8, 4), lax.rem(self.z + off // 2 % 4, 4)
        return y, z, self.at(y, z, self.x, lax.rem(self.core + off, 2))

    def in_wall(self, off):
        y, z = lax.rem(self.y + off // 4, 4), lax.rem(self.z + off % 4, 4)
        return y, z, self.at(y, z, self.x, self.core)

    def sibling(self):
        return self.at(self.y, self.z, self.x, 1 - self.core)

    def neighbour(self, dr, dc):
        return (lax.rem(self.row + dr + ROWS, ROWS), lax.rem(self.col + dc + COLS, COLS))


def side_ends(place, src, row0, col0, ext):
    ends = []
    for dc in (-1, 1):
        read = col0 if dc < 0 else col0 + W - LEFT
        land = LEFT + W if dc < 0 else 0
        ends.append(
            (
                src.at[pl.ds(row0, H), pl.ds(read, LEFT), :],
                ext.at[pl.ds(R, H), pl.ds(land, LEFT), :],
                place.neighbour(0, dc),
            )
        )
    return ends


def row_ends(place, src, row0, col0, ext, near):
    odd = lax.rem(place.row, 2)
    low = odd if near else 1 - odd
    rows, landing = pl.ds(row0 + (H - R) * (1 - low), R), pl.ds((R + H) * low, R)
    ends = []
    for dc in (0, -1, 1):
        read, land, n = (col0, LEFT, W) if dc == 0 else (col0, LEFT + W, LEFT) if dc < 0 else (col0 + W - LEFT, 0, LEFT)
        ends.append(
            (
                src.at[rows, pl.ds(read, n), :],
                ext.at[landing, pl.ds(land, n), :],
                place.neighbour(1 - 2 * low, dc),
            )
        )
    return ends


def clear_columns(place, ext, b):
    @pl.when(place.col == 0)
    def _():
        ext[b, R : R + H, 0:LEFT] = jnp.zeros((H, LEFT, C), f32)

    @pl.when(place.col == COLS - 1)
    def _():
        ext[b, R : R + H, LEFT + W :] = jnp.zeros((H, LEFT, C), f32)


def clear_rows(place, ext):
    for edge, at in ((0, slice(0, R)), (ROWS - 1, slice(R + H, HE))):

        @pl.when(place.row == edge)
        def _():
            ext[:, at] = jnp.zeros((B, R, WE, C), f32)

        @pl.when(place.col == 0)
        def _():
            ext[:, at, 0:LEFT] = jnp.zeros((B, R, LEFT, C), f32)

        @pl.when(place.col == COLS - 1)
        def _():
            ext[:, at, LEFT + W :] = jnp.zeros((B, R, LEFT, C), f32)


def conv_tile(ext, taps, b, wb, flip, rows, acc):
    for j in range(K):
        tap = [taps[(K - 1 - i) * K + K - 1 - j] if flip else taps[i * K + j] for i in range(K)]
        for e in rows:
            x = ext[b, e, pl.ds(8 * wb + LEFT - R + j, 8), :]
            for i in range(K):
                p = e - i
                if 0 <= p < H:
                    acc[p] = acc[p] + tap[i] * x
    return acc


INNER = range(R, R + H)
OUTER = (*range(R), *range(R + H, HE))
FRINGE = (*range(R), *range(H - R, H))


def kernel_grad_tile(ext, dcv, kacc, b, wb):
    grads = [dcv[b, R + p, pl.ds(pl.multiple_of(8 * wb + LEFT, 8), 8), :] for p in range(H)]
    for j in range(K):
        acc = [kacc[i * K + j] for i in range(K)]
        for e in range(HE):
            x = ext[b, e, pl.ds(8 * wb + LEFT - R + j, 8), :]
            for i in range(K):
                p = e - i
                if 0 <= p < H:
                    acc[i] = acc[i] + grads[p] * x
        for i in range(K):
            kacc[i * K + j] = acc[i]


def widen(column, n):
    one = jnp.broadcast_to(column, (column.shape[0], 128))
    return jnp.concatenate([one] * n, axis=1)


def kernel(
    feat, cot_hbm, taps_in, cb_in, gain_in, shift_in, ob_in, scale_in, ib_in, win_in, wout_in,
    fg_out, small_out, weight_out,
    taps_s, cb_s, gain_s, shift_s, ob_s, scale_s, ib_s, srow,
    src, cot, dcv, mid, fg, sg, wg, taps,
    win2, winlo, wintop, wot2, wotlo, bias_eff,
    nacc, macc, inbacc, kacc, cotacc, dbacc,
    wp, wcore, wa, wr1, wb_, wr2, rows, sp, srx, sb, sry,
    local, out_sem, sent, arrived,
):
    place = Place()
    y, z, x, core = place.y, place.z, place.x, place.core

    scalars = [(taps_in, taps_s), (cb_in, cb_s), (gain_in, gain_s), (shift_in, shift_s), (ob_in, ob_s), (scale_in, scale_s), (ib_in, ib_s)]
    params = [pltpu.make_async_copy(a, b, local.at[4 + n]) for n, (a, b) in enumerate(scalars)]
    own = [
        pltpu.make_async_copy(feat, src.at[:, pl.ds(R, H), pl.ds(LEFT, W), :], local.at[0]),
        pltpu.make_async_copy(cot_hbm, cot, local.at[1]),
        pltpu.make_async_copy(win_in, wg.at[0, y, z, x, core], local.at[2]),
        pltpu.make_async_copy(wout_in, wg.at[1, y, z, x, core], local.at[3]),
    ]
    for copy in params + own:
        copy.start()

    barrier = pltpu.get_barrier_semaphore()
    partners = [place.neighbour(dr, dc) for dr in (-1, 0, 1) for dc in (-1, 0, 1) if dr or dc]
    partners += [place.in_plane(off)[1] for off in range(1, 8)]
    partners += [place.in_slab(off)[2] for off in range(1, 32)]
    for partner in partners:
        pl.semaphore_signal(barrier, inc=1, device_id=partner, device_id_type=MESH)

    for copy in params:
        copy.wait()
    lane = lanes(1, 128, 1)
    row = jnp.zeros((1, 128), f32)
    for i in range(K):
        for j in range(K):
            row = jnp.where(lane == TAPS + i * K + j, taps_s[i, 0, j], row)
    for at, ref in ((CB, cb_s), (GAIN, gain_s), (SHIFT, shift_s), (OB, ob_s), (SCALE, scale_s)):
        row = jnp.where(lane == at, ref[0], row)
    for k in range(4):
        row = jnp.where(lane == IB + k, ib_s[k], row)
    srow[...] = row
    sg[y, z, x, core] = row
    kacc[...] = jnp.zeros_like(kacc)
    nacc[...] = jnp.zeros_like(nacc)
    macc[...] = jnp.zeros_like(macc)
    inbacc[...] = jnp.zeros_like(inbacc)
    cotacc[...] = jnp.zeros_like(cotacc)
    dbacc[...] = jnp.zeros_like(dbacc)

    pl.semaphore_wait(barrier, len(partners))

    stages = []

    class Stage:
        def __init__(self, amount, copies):
            self.n = len(stages)
            stages.append(self)
            self.amount = amount
            self.copies = [self.copy(*ends) for ends in copies]

        def copy(self, a, b, partner):
            return pltpu.make_async_remote_copy(
                src_ref=a, dst_ref=b, send_sem=sent.at[self.n], recv_sem=arrived.at[self.n],
                device_id=partner, device_id_type=MESH,
            )

        def start(self):
            for copy in self.copies:
                copy.start()

        def arrive(self):
            self.copy(self.amount, self.amount, place.sibling()).wait_recv()

        def leave(self):
            self.copy(self.amount, self.amount, place.sibling()).wait_send()

    cell = (y, z, x, core)
    plane = [place.in_plane(off)[1] for off in range(1, 8)]
    zs = [place.turn(z=off)[3] for off in range(1, 4)]
    wall = [place.in_wall(off)[2] for off in range(1, 16)]
    xs = [place.turn(x=off)[3] for off in range(1, 4)]
    ys = [place.turn(y=off)[3] for off in range(1, 4)]
    cells = wg.at[0].reshape(128, 4, C)
    s1 = Stage(srx.at[:, 0, 0], [(srow, sg.at[cell], p) for p in plane])
    w1 = Stage(cells.at[pl.ds(0, 3)], [(win_in, wg.at[(0, *cell)], p) for p in zs])
    v1 = Stage(cells.at[pl.ds(0, 3)], [(wout_in, wg.at[(1, *cell)], p) for p in zs])
    s2 = Stage(sg.reshape(128, 1, C).at[pl.ds(0, 120)], [(sg.at[y, z], sg.at[y, z], p) for p in wall])
    part = wg.at[0, y, :, x, core]
    w2 = Stage(cells.at[pl.ds(0, 12)], [(part, part, p) for p in xs])
    other = wg.at[1, y, :, x, core]
    v2 = Stage(cells.at[pl.ds(0, 12)], [(other, other, p) for p in ys])
    layer = wg.at[0, y, :, :, core]
    w3 = Stage(cells.at[pl.ds(0, 48)], [(layer, layer, p) for p in ys])
    slab = wg.at[1, :, :, x, core]
    v3 = Stage(cells.at[pl.ds(0, 48)], [(slab, slab, p) for p in xs])
    lot = wg.at[:, :, :, :, core]
    w4 = Stage(cells, [(lot, lot, place.sibling())])
    def tile_edges(ref, row0, col0, ext):
        sides, nears, fars = [], [], []
        for b in range(B):
            ends = (place, ref.at[b], row0, col0, ext.at[b])
            sides.append(Stage(src.at[b, pl.ds(0, H), pl.ds(0, 2 * LEFT), :], side_ends(*ends)))
            nears.append(Stage(src.at[b, pl.ds(0, R), :, :], row_ends(*ends, True)))
            fars.append(Stage(src.at[b, pl.ds(0, R), :, :], row_ends(*ends, False)))
        return sides, nears, fars

    def start(*stages):
        for stage in stages:
            stage.start()

    def arrive(*stages):
        for stage in stages:
            stage.arrive()

    sides, nears, fars = tile_edges(feat, 0, 0, src)

    s1.start()
    w1.start()
    v1.start()
    start(*sides)
    own[2].wait()
    own[3].wait()
    s1.arrive()
    s2.start()
    w1.arrive()
    w2.start()
    v1.arrive()
    v2.start()
    start(*nears)
    w2.arrive()
    w3.start()
    v2.arrive()
    v3.start()
    start(*fars)
    own[0].wait()
    own[1].wait()
    arrive(*sides)
    clear_columns(place, src, 0)
    clear_columns(place, src, 1)
    s2.arrive()

    small = sg.reshape(128, C)[...]
    small_t = small.T
    for n in range(K * K):
        taps[n] = jnp.broadcast_to(small_t[TAPS + n : TAPS + n + 1, :], (8, C))
    conv_bias = jnp.broadcast_to(small_t[CB : CB + 1, :], (8, C))

    def column_block(n):
        return n // 8, lax.rem(n, 8), pl.ds(pl.multiple_of(lax.rem(n, 8) * 8, 8), 8)

    def conv_step(n, carry):
        b, wb, at = column_block(n)
        acc = conv_tile(src, taps, b, wb, False, INNER, {p: conv_bias for p in range(H)})
        for p in range(H):
            mid[b, p, at, :] = acc[p]
        return carry

    lax.fori_loop(0, LATE, conv_step, 0)
    w3.arrive()
    v3.arrive()
    w4.start()
    lax.fori_loop(LATE, BLOCKS, conv_step, 0)

    def conv_rest(n, carry):
        b, wb, at = column_block(n)
        acc = conv_tile(src, taps, b, wb, False, OUTER, {p: mid[b, p, at, :] for p in FRINGE})
        for p in FRINGE:
            mid[b, p, at, :] = acc[p]
        return carry

    w4.arrive()
    gain_wide, shift_wide = widen(small[:, GAIN : GAIN + 1], 4), widen(small[:, SHIFT : SHIFT + 1], 4)
    scale_wide, ob_wide = widen(small[:, SCALE : SCALE + 1], 4), widen(small[:, OB : OB + 1], 1)
    win_t = wg.at[0].reshape(HID, C)[...]
    win = win_t.T
    wo_t = wg.at[1].reshape(HID, C)[...].T
    hi, lo = split(win * gain_wide)
    win2[0:C, :] = hi
    win2[C:, :] = hi
    winlo[...] = lo
    hi, lo = split(win_t * small_t[GAIN : GAIN + 1, :])
    wintop[:, 0:C] = hi
    wintop[:, C:] = lo
    hi, lo = split(wo_t * scale_wide)
    wot2[0:C, :] = hi
    wot2[C:, :] = hi
    wotlo[...] = lo
    pick = [lanes(32, 128, 1) == 4 * lanes(32, 128, 0) + k for k in range(4)]
    shifted = win * shift_wide
    for t in range(4):
        cut, band = slice(128 * t, 128 * t + 128), slice(32 * t, 32 * t + 32)
        terms = [jnp.where(pick[k], small[band, IB + k : IB + k + 1], 0.0) for k in range(4)]
        bias_eff[:, cut] = jnp.sum(shifted[:, cut], axis=0, keepdims=True) + jnp.sum(sum(terms), axis=0, keepdims=True)

    def mix(b, starts):
        spans = [pl.ds(p, QUARTER) for p in starts]
        x = jnp.concatenate([mid[b, s].reshape(M // 2, C) for s in spans], axis=0)
        ct = jnp.concatenate([cot[b, s].reshape(M // 2, C) for s in spans], axis=0)
        mean = jnp.mean(x, axis=-1, keepdims=True)
        cen = x - mean
        inv = lax.rsqrt(jnp.mean(cen * cen, axis=-1, keepdims=True) + norm_eps)
        normed = cen * inv
        n_hi, n_lo = split(normed)
        n2 = jnp.concatenate([n_hi, n_lo], axis=1)
        c_hi, c_lo = split(ct)
        c2 = jnp.concatenate([c_hi, c_lo], axis=1)
        nt2 = jnp.concatenate(split(normed.T), axis=0)
        ct2 = jnp.concatenate(split(ct.T), axis=0)
        cotacc[...] += jnp.sum(ct.reshape(M // 8, 8, C), axis=0)
        dn = jnp.zeros((M, C), f32)
        step = 256
        for h in range(0, HID, step):
            cut = slice(h, h + step)
            act = dot(n2, win2[:, cut]) + dot(n_hi, winlo[:, cut]) + bias_eff[:, cut]
            dh = dot(c2, wot2[:, cut]) + dot(c_hi, wotlo[:, cut])
            phi = 0.5 * (1.0 + lax.erf(act * inverse_root_two))
            slope = phi + act * jnp.exp(-0.5 * act * act) * inverse_root_twopi
            hid_hi, hid_lo = split(act * phi)
            da = dh * slope
            inbacc[:, cut] += jnp.sum(da.reshape(M // 8, 8, step), axis=0)
            da_hi, da_lo = split(da)
            both = dot(da_hi, wintop[cut, :])
            dn = dn + both[:, 0:C] + both[:, C:] + dot(da_lo, wintop[cut, 0:C])
            both = dot(nt2, da_hi)
            nacc[:, cut] += both[0:C] + both[C:] + dot(nt2[0:C], da_lo)
            both = dot(ct2, hid_hi)
            macc[:, cut] += both[0:C] + both[C:] + dot(ct2[0:C], hid_lo)
        dc = inv * (
            dn
            - jnp.mean(dn, axis=-1, keepdims=True)
            - normed * jnp.mean(dn * normed, axis=-1, keepdims=True)
        )
        dbacc[...] += jnp.sum(dc.reshape(M // 8, 8, C), axis=0)
        for n, p in enumerate(starts):
            part = dc[n * (M // 2) : (n + 1) * (M // 2)]
            dcv[b, pl.ds(R + p, QUARTER), LEFT : LEFT + W, :] = part.reshape(QUARTER, W, C)

    back_sides, back_nears, back_fars = tile_edges(dcv, R, LEFT, dcv)

    def mix_step(n, carry):
        outer = n // 2

        @pl.when(n == 2)
        def _():
            arrive(*nears, *fars)
            clear_rows(place, src)
            lax.fori_loop(0, BLOCKS, conv_rest, 0)

        @pl.when(n == 3)
        def _():
            start(back_fars[0], back_nears[0], back_sides[0])

        mix(lax.rem(n, 2), (QUARTER * (1 - outer), QUARTER * (2 + outer)))
        return carry

    lax.fori_loop(0, 4, mix_step, 0)
    start(back_fars[1], back_nears[1])

    factor = 1.0 / math.sqrt(B * H * W * ROWS * COLS)
    nsum, msum = nacc[...], macc[...]
    inb = jnp.sum(inbacc[...], axis=0, keepdims=True)
    wp[0] = ((nsum * gain_wide + shift_wide * inb) * factor).T.reshape(4, 4, 4, 8, C)
    wp[1] = (msum * (scale_wide * factor)).T.reshape(4, 4, 4, 8, C)
    r0 = Stage(wcore, [(wp.at[1 - core], wcore, place.sibling())])
    r0.start()

    def kgrad_step(n, carry):
        kernel_grad_tile(src, dcv, kacc, n // 8, lax.rem(n, 8))
        return carry

    lax.fori_loop(0, CUT, kgrad_step, 0)
    r0.arrive()
    for a in range(4):
        wa[a] = wp[core, :, :, a] + wcore[:, :, a]
    slab = [place.in_slab(off) for off in range(1, 32)]
    r1 = Stage(wr1, [(wa.at[lax.rem(x + 1 + n, 4)], wr1.at[n], p) for n, p in enumerate(xs)])
    r2 = Stage(wr2.reshape(32, 8, C).at[pl.ds(0, 31)], [(wb_.at[yy, zz], wr2.at[core, y, z], p) for yy, zz, p in slab])
    r1.start()
    back_sides[1].start()
    lax.fori_loop(CUT, BLOCKS, kgrad_step, 0)

    gain_g = jnp.sum(win * nsum, axis=1, keepdims=True)
    shift_g = jnp.sum(win * inb, axis=1, keepdims=True)
    scale_g = jnp.sum(wo_t * msum, axis=1, keepdims=True)
    for n in range(K * K):
        rows[n : n + 1, :] = jnp.sum(kacc[n], axis=0, keepdims=True)
    rows[K * K : K * K + 1, :] = jnp.sum(dbacc[...], axis=0, keepdims=True)
    rows[K * K + 1 : K * K + 2, :] = jnp.sum(cotacc[...], axis=0, keepdims=True)
    rows[K * K + 2 :, :] = jnp.zeros((128 - K * K - 2, C), f32)
    grads = rows[...].T
    lane = lanes(C, 128, 1)
    cot_wide = widen(grads[:, K * K + 1 : K * K + 2], 1)
    columns = [(GAIN, gain_g), (SHIFT, shift_g), (OB, scale_wide[:, 0:C] * cot_wide), (SCALE, scale_g + ob_wide * cot_wide)]
    for k in range(4):
        terms = [jnp.where(pick[k], inb[:, 128 * t : 128 * t + 128], 0.0) for t in range(4)]
        columns.append((IB + k, jnp.sum(jnp.concatenate(terms, axis=0), axis=1, keepdims=True)))
    for at, column in columns:
        grads = jnp.where(lane == at, column, grads)
    sp.reshape(128, C)[...] = grads * factor
    q1, q2 = [], []
    for off in range(1, 8):
        g, to = place.in_plane(off)
        q1.append((sp.at[:, :, g // 2, lax.rem(g, 2)], srx.at[off - 1], to))
    for off in range(1, 16):
        yy, zz, to = place.in_wall(off)
        q2.append((sb.at[yy, zz], sry.at[off - 1], to))
    q1, q2 = Stage(srx, q1), Stage(sry, q2)
    q1.start()

    back_sides[0].arrive()
    clear_columns(place, dcv, 0)

    def out_step(n, carry):
        b, wb, at = column_block(n)
        acc = conv_tile(dcv, taps, b, wb, True, INNER, {p: cot[b, p, at, :] for p in range(H)})
        for p in range(H):
            fg[b, p, at, :] = acc[p]
        return carry

    def out_rest(n, carry):
        b, wb, at = column_block(n)
        acc = conv_tile(dcv, taps, b, wb, True, OUTER, {p: fg[b, p, at, :] for p in FRINGE})
        for p in FRINGE:
            fg[b, p, at, :] = acc[p]
        return carry

    lax.fori_loop(0, 5, out_step, 0)
    r1.arrive()
    wb_[...] = wa[x] + wr1[0] + wr1[1] + wr1[2]
    r2.start()
    wr2[core, y, z] = wb_[y, z]
    lax.fori_loop(5, 8, out_step, 0)
    q1.arrive()
    total = sp[:, :, x, core]
    for n in range(7):
        total = total + srx[n]
    sb[...] = total
    q2.start()
    back_sides[1].arrive()
    clear_columns(place, dcv, 1)
    lax.fori_loop(8, BLOCKS, out_step, 0)
    arrive(*back_nears, *back_fars)
    clear_rows(place, dcv)
    lax.fori_loop(0, BLOCKS, out_rest, 0)
    put = pltpu.make_async_copy(fg, fg_out, out_sem.at[0])
    put.start()

    for stage in stages:
        if stage not in (r2, q2):
            stage.leave()
    q2.arrive()
    total = sb[y, z]
    for n in range(15):
        total = total + sry[n]
    small_out[...] = total
    r2.arrive()
    for kind in range(2):
        total = wr2[kind, 0, 0]
        for n in range(1, 16):
            total = total + wr2[kind, n // 4, n % 4]
        weight_out[kind] = jnp.where(core == 0, total[0:4], total[4:8])

    put.wait()
    r2.leave()
    q2.leave()


def deliver(
    fg_in, small_in, weight_in,
    fg_out, taps_out, cb_out, gain_out, shift_out, win_out, ib_out, wout_out, ob_out, scale_out,
    buf, row, weights, taps, cb, gain, shift, ib, ob, scale, sem,
):
    pieces = [(b, pl.ds(h, H // 2)) for b in range(B) for h in range(0, H, H // 2)]
    small = pltpu.make_async_copy(small_in, row, sem.at[8])
    weight = pltpu.make_async_copy(weight_in, weights, sem.at[9])
    gets = [pltpu.make_async_copy(fg_in.at[at], buf.at[at], sem.at[n]) for n, at in enumerate(pieces)]
    puts = [pltpu.make_async_copy(buf.at[at], fg_out.at[at], sem.at[4 + n]) for n, at in enumerate(pieces)]
    for copy in [small, weight] + gets:
        copy.start()
    small.wait()
    for i in range(K):
        for j in range(K):
            taps[i, 0, j] = row[0, TAPS + i * K + j]
    for at, ref in ((CB, cb), (GAIN, gain), (SHIFT, shift), (OB, ob), (SCALE, scale)):
        ref[0] = row[0, at]
    for k in range(4):
        ib[k] = row[0, IB + k]
    ends = [
        (taps, taps_out), (cb, cb_out), (gain, gain_out), (shift, shift_out), (ob, ob_out), (scale, scale_out),
        (ib, ib_out), (weights.at[0], win_out), (weights.at[1], wout_out),
    ]
    weight.wait()
    rest = [pltpu.make_async_copy(a, b, sem.at[10 + n]) for n, (a, b) in enumerate(ends)]
    for copy in rest:
        copy.start()
    for get, put in zip(gets, puts):
        get.wait()
        put.start()
    for copy in rest + puts:
        copy.wait()


def per_device(
    features, cotangent, conv_kernel, conv_bias, norm_gain, norm_shift,
    w_in, in_bias, w_out, out_bias, layer_scale,
):
    vmem = lambda *shape: pltpu.VMEM(shape, f32)
    smem = lambda *shape: pltpu.SMEM(shape, f32)
    half = lambda *shape: pltpu.VMEM(shape, bf16)
    dma = lambda n: pltpu.SemaphoreType.DMA((n,))
    out = lambda *shape: jax.ShapeDtypeStruct(shape, f32)
    anywhere = pl.BlockSpec(memory_space=pl.ANY)
    inside = pl.BlockSpec(memory_space=pltpu.VMEM)
    tile = (B, H, W, C)
    fg, small, weights = pl.pallas_call(
        kernel,
        out_shape=(out(*tile), out(1, C), out(2, 4, C)),
        in_specs=[anywhere] * 11,
        out_specs=(anywhere, inside, inside),
        scratch_shapes=[
            smem(K, 1, K), smem(1), smem(1), smem(1), smem(1), smem(1), smem(4), vmem(1, C),
            vmem(B, HE, WE, C), vmem(*tile), vmem(B, HE, WE, C), vmem(*tile), vmem(*tile),
            vmem(4, 4, 4, 2, 1, C), vmem(2, 4, 4, 4, 2, 4, C), vmem(K * K, 8, C),
            half(2 * C, HID), half(C, HID), half(HID, 2 * C), half(2 * C, HID), half(C, HID), vmem(1, HID),
            vmem(C, HID), vmem(C, HID), vmem(8, HID), vmem(K * K, 8, C), vmem(8, C), vmem(8, C),
            vmem(2, 4, 4, 4, 8, C), vmem(4, 4, 4, 8, C), vmem(4, 4, 4, 8, C), vmem(3, 4, 4, 8, C),
            vmem(4, 4, 8, C), vmem(2, 4, 4, 8, C),
            vmem(128, C), vmem(4, 4, 4, 2, 1, C), vmem(7, 4, 4, 1, C), vmem(4, 4, 1, C), vmem(15, 1, C),
            dma(11), dma(1), dma(26), dma(26),
        ],
        compiler_params=pltpu.CompilerParams(
            collective_id=0, has_side_effects=True, vmem_limit_bytes=56 * 2**20
        ),
    )(
        features, cotangent, conv_kernel.transpose(0, 2, 1), conv_bias, norm_gain, norm_shift,
        out_bias, layer_scale, in_bias, w_in.T, w_out,
    )
    fg, taps_g, cb_g, gain_g, shift_g, win_g, ib_g, wout_g, ob_g, scale_g = pl.pallas_call(
        deliver,
        out_shape=(
            out(*tile), out(K, 1, K), out(1), out(1), out(1), out(4, C), out(4), out(4, C), out(1), out(1),
        ),
        in_specs=[anywhere] * 3,
        out_specs=(anywhere,) * 10,
        scratch_shapes=[
            vmem(*tile), smem(1, C), vmem(2, 4, C), smem(K, 1, K), smem(1), smem(1), smem(1), smem(4), smem(1), smem(1), dma(19),
        ],
    )(fg, small, weights)
    return fg, taps_g.transpose(0, 2, 1), cb_g, gain_g, shift_g, win_g.T, ib_g, wout_g, ob_g, scale_g


def solution(mesh):
    both = ("row", "col")
    tile = P(None, "row", "col", None)
    taps, vector = P(None, None, both), P(both)
    return jax.shard_map(
        per_device,
        mesh=mesh,
        in_specs=(tile, tile, taps, vector, vector, vector, P(None, both), vector, P(both, None), vector, vector),
        out_specs=(tile, taps, vector, vector, vector, P(None, both), vector, P(both, None), vector, vector),
        check_vma=False,
    )
```
